32 devices in a mesh: rows: 8 (over y, x, core), seq: 4 (over z).
Axes of the slice: x: 2, y: 2, z: 4, core: 2. Of those that a mesh axis runs over, the one named last changes fastest.
Arguments:
- tokens: bfloat16 [8, 1024, 1024], P('rows', 'seq'), may hold values from -6 to 6
- doc_lengths: int32 [8, 8], P('rows'), may hold values from 1 to 512, 1024 in all within a row
- valid_counts: int32 [8], P('rows'), may hold values from 512 to 1024
- norm_in: bfloat16 [1024], replicated, may hold values from 0.099609375 to 1.8984375
- w_in: bfloat16 [1024, 3072], replicated, may hold values from -0.1875 to 0.1875
- w_conv: bfloat16 [3, 1024], replicated, may hold values from -3 to 3
- w_out: bfloat16 [1024, 1024], replicated, may hold values from -0.1875 to 0.1875
- norm_ffn: bfloat16 [1024], replicated, may hold values from 0.099609375 to 1.8984375
- w_gate: bfloat16 [1024, 4608], replicated, may hold values from -0.1875 to 0.1875
- w_up: bfloat16 [1024, 4608], replicated, may hold values from -0.1875 to 0.1875
- w_down: bfloat16 [4608, 1024], replicated, may hold values from -0.1875 to 0.1875
- cotangent: bfloat16 [8, 1024, 1024], P('rows', 'seq'), may hold values from -6 to 6
Outputs:
- layer_out: bfloat16 [8, 1024, 1024], P('rows', 'seq')
- grad_tokens: bfloat16 [8, 1024, 1024], P('rows', 'seq')
- grad_norm_in: float32 [1024], P(('rows', 'seq'))
- grad_w_in: float32 [1024, 3072], P('rows', 'seq')
- grad_w_conv: float32 [3, 1024], P(None, ('rows', 'seq'))
- grad_w_out: float32 [1024, 1024], P('rows', 'seq')
- grad_norm_ffn: float32 [1024], P(('rows', 'seq'))
- grad_w_gate: float32 [1024, 4608], P('rows', 'seq')
- grad_w_up: float32 [1024, 4608], P('rows', 'seq')
- grad_w_down: float32 [4608, 1024], P('rows', 'seq')
The draws below stay inside these ranges and needn't reach their ends.
Inputs may be any that keep to these rules, and one draw needn't show every extreme that they name: `doc_lengths`: each row's 8 document lengths sum to 1024; the longest is exactly 512. `valid_counts`: positions at or past a row's count are pads.
All inputs are finite; a program needn't handle non-finite values.
Results may differ from the reference program's by a relative error of at most 0.017.
Values may be sent and summed in bfloat16 or wider, within the bound.
A program may use at most 192 MiB of HBM per device.

```python
import math
import jax
import jax.numpy as jnp
import numpy as np
from jax import lax

D = 1024
FF = 4608
NDOC = 8
ROWS = 8
LENGTH = 1024


def with_ends(values, own_key, least, top_value):
    extent = values.shape
    spot = [jax.random.randint(jax.random.fold_in(own_key, axis), (), 0, extent[axis]) for axis in range(len(extent))]
    values = values.at[tuple(spot)].set(least)
    longest = extent.index(max(extent))
    spot[longest] = (spot[longest] + 1) % extent[longest]
    return values.at[tuple(spot)].set(top_value)


def steps_of(rng, shape, cuts, low, top_value):
    factor_of, own = 1.0, jax.random.fold_in(rng, 6)
    for axis_at, parts in cuts:
        draws = jnp.exp(jax.random.uniform(jax.random.fold_in(own, axis_at), (parts,), jnp.float32, low / len(cuts), top_value / len(cuts)))
        factor_of = factor_of * jnp.repeat(draws, shape[axis_at] // parts).reshape([-1 if axis == axis_at else 1 for axis in range(len(shape))])
    return factor_of


def length_profile(count, total, reach, skew):
    weights = [(1 << 20) // math.isqrt(standing ** skew) + 1 for standing in range(2, count + 1)]
    spare, given = total - reach - (count - 1), [1] * (count - 1)
    while spare > 0:
        movable = [i for i in range(count - 1) if given[i] < reach]
        pool, budget = sum([weights[i] for i in movable]), spare
        for i in movable:
            more = min(reach - given[i], max(1, budget * weights[i] // pool), spare)
            given[i] = given[i] + more
            spare = spare - more
    return np.array([reach] + given)


def ragged(rng, count, total, reach, skew):
    if count == 2:
        one = jax.random.randint(rng, (), max(1, total - reach), min(reach, total - 1) + 1)
        return jnp.stack([one, total - one])
    tallies = jnp.asarray(length_profile(count, total, reach, skew), jnp.int32)
    twos = (count - 1) // 2
    source_of, taker = tallies[1:1 + 2 * twos:2], tallies[2:2 + 2 * twos:2]
    margin = jnp.minimum(source_of - 1, reach - taker)
    shifted = jax.random.randint(jax.random.fold_in(rng, 1), (twos,), 0, 1 << 20) % (margin + 1)
    tallies = tallies.at[1:1 + 2 * twos:2].set(source_of - shifted).at[2:2 + 2 * twos:2].set(taker + shifted)
    return tallies[jax.random.permutation(jax.random.fold_in(rng, 2), count)]


def bell_draw(rng, dims, scale, reach, cuts=(), kind=jnp.bfloat16):
    entries = scale * jax.random.normal(rng, dims, jnp.float32)
    if cuts:
        entries = entries * steps_of(rng, dims, cuts, -0.22, 0.18)
    return jnp.clip(entries, -reach, reach).astype(kind)


def setup_inputs(seed: int = 0) -> dict:
    key_list = jax.random.split(jax.random.key(seed), 13)
    return {
        "tokens": bell_draw(key_list[0], (ROWS, LENGTH, D), 1.0, 6.0, ((0, 8), (1, 4))),
        "doc_lengths": jax.vmap(lambda own: ragged(own, NDOC, LENGTH, LENGTH // 2, 2))(jax.random.split(key_list[1], ROWS)).reshape((ROWS, NDOC)).astype(jnp.int32),
        "valid_counts": with_ends(jax.random.randint(key_list[2], (ROWS,), LENGTH // 2, LENGTH + 1), jax.random.fold_in(key_list[2], 1), LENGTH // 2, LENGTH).astype(jnp.int32),
        "norm_in": jnp.clip(1.0 + 0.18 * jax.random.normal(key_list[3], (D,), jnp.float32), 0.099609375, 1.8984375).astype(jnp.bfloat16),
        "w_in": bell_draw(key_list[4], (D, 3 * D), D ** -0.5, 0.1875),
        "w_conv": bell_draw(key_list[5], (3, D), 0.6, 3.0),
        "w_out": bell_draw(key_list[6], (D, D), D ** -0.5, 0.1875),
        "norm_ffn": jnp.clip(1.0 + 0.18 * jax.random.normal(key_list[7], (D,), jnp.float32), 0.099609375, 1.8984375).astype(jnp.bfloat16),
        "w_gate": bell_draw(key_list[8], (D, FF), D ** -0.5, 0.1875),
        "w_up": bell_draw(key_list[9], (D, FF), D ** -0.5, 0.1875),
        "w_down": bell_draw(key_list[10], (FF, D), (FF // 4) ** -0.5, 0.1875),
        "cotangent": bell_draw(key_list[11], (ROWS, LENGTH, D), 1.0, 6.0, ((0, 8), (1, 4))),
    }


@jax.custom_vjp
def low(v):
    return lax.optimization_barrier(v.astype(jnp.bfloat16)).astype(jnp.float32)

@jax.custom_vjp
def low_back(v):
    return v

def low_keep(v):
    return (low(v), None)

def low_pass(kept, grad):
    return (grad,)

def back_keep(v):
    return (v, None)

def back_low(kept, grad):
    return (low(grad),)
low.defvjp(low_keep, low_pass)
low_back.defvjp(back_keep, back_low)
EPSILON = 1e-05

def matmul(left, right):
    return jnp.dot(left, right, precision=lax.Precision.HIGHEST, preferred_element_type=jnp.float32)

def rms_scale(values):
    return lax.rsqrt(lax.optimization_barrier(jnp.mean(values * values, axis=-1, keepdims=True)) + EPSILON)

def doc_masks(lengths, positions):
    lengths = lengths.astype(jnp.int32)
    starts = (jnp.cumsum(lengths) - lengths).astype(jnp.int32)
    within = starts[None, :] <= positions[:, None]
    first = lax.optimization_barrier(jnp.max(jnp.where(within, starts[None, :], 0), axis=1)).astype(jnp.int32)
    return [(positions - offset >= first).astype(jnp.float32)[:, None] for offset in range(3)]

def layer(inputs, valid, same, norm_in, w_in, w_conv, w_out, norm_ffn, w_gate, w_up, w_down):
    width = inputs.shape[1]
    length = inputs.shape[0]
    normed = low(inputs * rms_scale(inputs) * norm_in)
    proj = low_back(matmul(normed, w_in))
    gate_b = proj[:, :width]
    gate_c = proj[:, width:2 * width]
    values = proj[:, 2 * width:]
    mixed_in = low(valid * gate_b * values)
    padded = jnp.pad(mixed_in, ((2, 0), (0, 0)))
    conv = jnp.zeros_like(mixed_in)
    for offset in range(3):
        conv = conv + w_conv[offset] * same[offset] * padded[2 - offset:2 - offset + length]
    conv = low_back(conv)
    gated = low(valid * gate_c * conv)
    mixer_out = low_back(matmul(gated, w_out))
    resid = inputs + mixer_out
    normed2 = low(resid * rms_scale(resid) * norm_ffn)
    gate_act = low_back(matmul(normed2, w_gate))
    up_act = low_back(matmul(normed2, w_up))
    hidden = low(jax.nn.silu(gate_act) * up_act)
    ffn_out = low_back(matmul(hidden, w_down))
    return resid + valid * ffn_out

def reference(tokens, doc_lengths, valid_counts, norm_in, w_in, w_conv, w_out, norm_ffn, w_gate, w_up, w_down, cotangent):
    params = tuple((p.astype(jnp.float32) for p in (norm_in, w_in, w_conv, w_out, norm_ffn, w_gate, w_up, w_down)))

    def one_row(totals, row):
        inputs, lengths, count, grad_out = row
        positions = jnp.arange(LENGTH, dtype=jnp.int32)
        valid = (positions < count).astype(jnp.float32)[:, None]
        same = doc_masks(lengths, positions)

        def forward(values, *weights):
            return layer(values, valid, same, *weights)
        result, pull = jax.vjp(forward, inputs.astype(jnp.float32), *params)
        grads = pull(grad_out.astype(jnp.float32))
        totals = tuple((total + grad for total, grad in zip(totals, grads[1:])))
        return (totals, (result.astype(jnp.bfloat16), grads[0].astype(jnp.bfloat16)))
    zeros = tuple((jnp.zeros_like(p) for p in params))
    totals, (layer_out, grad_tokens) = lax.scan(one_row, zeros, (tokens, doc_lengths, valid_counts, cotangent))
    return (layer_out, grad_tokens, totals[0], totals[1], totals[2], totals[3], totals[4], totals[5], totals[6], totals[7])
```

```python
import functools

import jax
import jax.numpy as jnp
import numpy as np
from jax import lax
from jax.experimental import pallas as pl
from jax.experimental.pallas import tpu as pltpu
from jax.sharding import PartitionSpec as P

EPSILON = 1e-05
BF = jnp.bfloat16
F32 = jnp.float32
MESH = pl.DeviceIdType.MESH


def passed_along(value, axis, steps):
    count = lax.axis_size(axis)
    first, last = (max(0, -steps), min(count, count - steps))
    return lax.ppermute(value, axis, [(source, source + steps) for source in range(first, last)])


def rms_scale(values):
    return lax.rsqrt(jnp.mean(values * values, axis=-1, keepdims=True) + EPSILON)


def doc_masks(lengths, positions):
    starts = jnp.cumsum(lengths) - lengths
    within = starts[None, :] <= positions[:, None]
    first = jnp.max(jnp.where(within, starts[None, :], 0), axis=1)
    return [(positions - offset >= first).astype(jnp.float32)[:, None] for offset in range(3)]


def weight_grad(left, right):
    return jnp.einsum("ta,tb->ab", left, right, preferred_element_type=jnp.float32)


def back_product(grad, weight):
    return jnp.einsum("tb,ab->ta", grad, weight, preferred_element_type=jnp.float32)


def scattered(value, row_dim, seq_dim):
    part = lax.psum_scatter(value.astype(BF), "rows", scatter_dimension=row_dim, tiled=True)
    part = lax.psum_scatter(part, "seq", scatter_dimension=seq_dim, tiled=True)
    return part.astype(F32)


def plain(
    tokens,
    doc_lengths,
    valid_counts,
    norm_in,
    w_in,
    w_conv,
    w_out,
    norm_ffn,
    w_gate,
    w_up,
    w_down,
    cotangent,
):
    inputs = tokens[0].astype(jnp.float32)
    span = inputs.shape[0]
    width = inputs.shape[1]
    start_pos = lax.axis_index("seq") * span
    positions = start_pos + jnp.arange(span + 2, dtype=jnp.int32)
    valid = (positions[:span] < valid_counts[0]).astype(jnp.float32)[:, None]
    same = doc_masks(doc_lengths[0], positions)
    taps = w_conv.astype(jnp.float32)
    gain_in = norm_in.astype(jnp.float32)
    gain_ffn = norm_ffn.astype(jnp.float32)
    scale1 = rms_scale(inputs)
    normed = (inputs * scale1 * gain_in).astype(jnp.bfloat16)
    proj = jnp.dot(normed, w_in, preferred_element_type=jnp.float32)
    gate_b = proj[:, :width]
    gate_c = proj[:, width : 2 * width]
    values = proj[:, 2 * width :]
    mixed_in = (valid * gate_b * values).astype(jnp.bfloat16)
    tail_rows = passed_along(mixed_in[span - 2 :], "seq", 1)
    padded = jnp.concatenate([tail_rows, mixed_in], axis=0).astype(jnp.float32)
    conv = jnp.zeros((span, width), jnp.float32)
    for offset in range(3):
        conv = conv + taps[offset] * same[offset][:span] * padded[2 - offset : 2 - offset + span]
    gated = (valid * gate_c * conv).astype(jnp.bfloat16)
    mixer_out = jnp.dot(gated, w_out, preferred_element_type=jnp.float32)
    resid = inputs + mixer_out
    scale2 = rms_scale(resid)
    normed2 = (resid * scale2 * gain_ffn).astype(jnp.bfloat16)
    gate_act = jnp.dot(normed2, w_gate, preferred_element_type=jnp.float32)
    up_act = jnp.dot(normed2, w_up, preferred_element_type=jnp.float32)
    sigmoid_gate = jax.nn.sigmoid(gate_act)
    silu_gate = gate_act * sigmoid_gate
    hidden = (silu_gate * up_act).astype(jnp.bfloat16)
    ffn_out = jnp.dot(hidden, w_down, preferred_element_type=jnp.float32)
    layer_out = (resid + valid * ffn_out).astype(jnp.bfloat16)
    grad_out = cotangent[0].astype(jnp.float32)
    d_ffn = (valid * grad_out).astype(jnp.bfloat16)
    grad_w_down = weight_grad(hidden, d_ffn)
    d_hidden = back_product(d_ffn, w_down)
    d_gate = (d_hidden * up_act * sigmoid_gate * (1.0 + gate_act * (1.0 - sigmoid_gate))).astype(
        jnp.bfloat16
    )
    d_up = (d_hidden * silu_gate).astype(jnp.bfloat16)
    grad_w_gate = weight_grad(normed2, d_gate)
    grad_w_up = weight_grad(normed2, d_up)
    d_normed2 = back_product(d_gate, w_gate) + back_product(d_up, w_up)
    grad_norm_ffn = jnp.sum(d_normed2 * resid * scale2, axis=0)
    scaled_ffn = gain_ffn * d_normed2
    d_resid = (
        grad_out
        + scale2 * scaled_ffn
        - resid * scale2**3 * jnp.mean(scaled_ffn * resid, axis=-1, keepdims=True)
    )
    d_mixer = d_resid.astype(jnp.bfloat16)
    grad_w_out = weight_grad(gated, d_mixer)
    d_gated = back_product(d_mixer, w_out)
    d_conv = (valid * gate_c * d_gated).astype(jnp.bfloat16)
    d_gate_c = valid * conv * d_gated
    head_rows = passed_along(d_conv[:2], "seq", -1)
    extended = jnp.concatenate([d_conv, head_rows], axis=0).astype(jnp.float32)
    d_mixed = jnp.zeros((span, width), jnp.float32)
    conv_rows = []
    for offset in range(3):
        d_mixed = (
            d_mixed
            + taps[offset] * same[offset][offset : offset + span] * extended[offset : offset + span]
        )
        conv_rows.append(
            jnp.sum(
                extended[:span] * same[offset][:span] * padded[2 - offset : 2 - offset + span],
                axis=0,
            )
        )
    grad_w_conv = jnp.stack(conv_rows, axis=0)
    d_proj = jnp.concatenate(
        [valid * values * d_mixed, d_gate_c, valid * gate_b * d_mixed], axis=1
    ).astype(jnp.bfloat16)
    grad_w_in = weight_grad(normed, d_proj)
    d_normed = back_product(d_proj, w_in)
    grad_norm_in = jnp.sum(d_normed * inputs * scale1, axis=0)
    scaled_in = gain_in * d_normed
    grad_tokens = (
        d_resid
        + scale1 * scaled_in
        - inputs * scale1**3 * jnp.mean(scaled_in * inputs, axis=-1, keepdims=True)
    )
    grad_tokens = grad_tokens.astype(jnp.bfloat16)
    return (
        layer_out[None],
        grad_tokens[None],
        scattered(grad_norm_in, 0, 0),
        scattered(grad_w_in, 0, 1),
        scattered(grad_w_conv, 1, 1),
        scattered(grad_w_out, 0, 1),
        scattered(grad_norm_ffn, 0, 0),
        scattered(grad_w_gate, 0, 1),
        scattered(grad_w_up, 0, 1),
        scattered(grad_w_down, 0, 1),
    )


def dot(a, b):
    return jnp.dot(a, b, preferred_element_type=F32)


def dot_nt(a, b):
    return lax.dot_general(a, b, (((1,), (1,)), ((), ())), preferred_element_type=F32)


def dot_tn(a, b):
    return lax.dot_general(a, b, (((0,), (0,)), ((), ())), preferred_element_type=F32)


def bit_of(value, weight):
    return lax.rem(lax.div(value, np.int32(weight)), np.int32(2))


def flipped(value, weight):
    return value + weight - 2 * weight * bit_of(value, weight)


def loop(count, body):
    lax.fori_loop(0, count, lambda i, carry: (body(i), carry)[1], 0)


def block(index, size):
    return pl.ds(pl.multiple_of(index * size, size), size)


N_SEM = 128
MASK_VALID, MASK_S0, MASK_S1, MASK_S2, MASK_N1, MASK_N2 = range(6)


def scratch_list(span, width, ff, rows, seq):
    quarter = ff // 4
    tall = ff // rows
    slim = width // rows
    side = width // seq
    half = slim // 2
    group = 4 * span
    return [
        ("tok", pltpu.VMEM((span, width), BF)),
        ("cot", pltpu.VMEM((span, width), BF)),
        ("wout", pltpu.VMEM((width, width), BF)),
        ("nrm", pltpu.VMEM((2 * span, width), BF)),
        ("gat", pltpu.VMEM((2 * span, width), BF)),
        ("dmx", pltpu.VMEM((2 * span, width), BF)),
        ("dpj", pltpu.VMEM((2 * span, 3 * width), BF)),
        ("gb", pltpu.VMEM((span, width), BF)),
        ("va", pltpu.VMEM((span, width), BF)),
        ("gc", pltpu.VMEM((span, width), F32)),
        ("mix", pltpu.VMEM((span + 8, width), F32)),
        ("dc", pltpu.VMEM((span + 8, width), F32)),
        ("res", pltpu.VMEM((span, width), F32)),
        ("own", pltpu.VMEM((span, width), F32)),
        ("loa", pltpu.VMEM((span, width), F32)),
        ("mask", pltpu.VMEM((span, 128), F32)),
        ("sc1", pltpu.VMEM((span, 1), F32)),
        ("sc2", pltpu.VMEM((span, 1), F32)),
        ("n2", pltpu.VMEM((group, width), BF)),
        ("df", pltpu.VMEM((group, width), BF)),
        ("hr", pltpu.VMEM((8, width), F32)),
        ("hr2", pltpu.VMEM((8, width), F32)),
        ("ps", pltpu.VMEM((2, span, width), BF)),
        ("pr", pltpu.VMEM((2, span, width), BF)),
        ("pz", pltpu.VMEM((span, width), BF)),
        ("fr", pltpu.VMEM((2, span, width), BF)),
        ("fz", pltpu.VMEM((span, width), BF)),
        ("sg", pltpu.VMEM((6, 8, width), F32)),
        ("sm", pltpu.VMEM((8, 128), F32)),
        ("gg", pltpu.VMEM((8, slim, quarter), BF)),
        ("rg1", pltpu.VMEM((4, slim, quarter), BF)),
        ("rg2", pltpu.VMEM((2, slim, quarter), BF)),
        ("rg3", pltpu.VMEM((2, slim, quarter), BF)),
        ("rg4", pltpu.VMEM((slim, quarter), BF)),
        ("gu", pltpu.VMEM((8, slim, quarter), BF)),
        ("ru1", pltpu.VMEM((4, slim, quarter), BF)),
        ("ru2", pltpu.VMEM((2, slim, quarter), BF)),
        ("ru3", pltpu.VMEM((2, slim, quarter), BF)),
        ("ru4", pltpu.VMEM((slim, quarter), BF)),
        ("gd", pltpu.VMEM((8, tall, side), BF)),
        ("ra1", pltpu.VMEM((2, tall, side), BF)),
        ("ra2", pltpu.VMEM((2, tall, side), BF)),
        ("ra3", pltpu.VMEM((tall, side), BF)),
        ("rb1", pltpu.VMEM((4, tall, side), BF)),
        ("rb2", pltpu.VMEM((2, tall, side), BF)),
        ("rb3", pltpu.VMEM((tall, side), BF)),
        ("rd4", pltpu.VMEM((tall, side), BF)),
        ("m1", pltpu.VMEM((2, 4, 2, half, width), BF)),
        ("m2", pltpu.VMEM((2, 4, half, width), BF)),
        ("m3", pltpu.VMEM((2, 2, half, width), BF)),
        ("m4", pltpu.VMEM((2, half, width), BF)),
        ("send", pltpu.SemaphoreType.DMA((N_SEM,))),
        ("recv", pltpu.SemaphoreType.DMA((N_SEM,))),
        ("local", pltpu.SemaphoreType.DMA((32,))),
    ]


OPERANDS = [
    "lengths",
    "counts",
    "tokens",
    "cotangent",
    "gain1",
    "taps",
    "gain2",
    "w_in",
    "w_out",
    "w_gate",
    "w_up",
    "w_down",
    "layer_out",
    "grad_tokens",
    "g_in",
    "g_out",
    "g_gate",
    "g_up",
    "g_down",
    "small",
]


class Refs:
    pass


class View:
    def __init__(self, ref, index):
        self.ref, self.index = ref, index

    def take(self):
        return self.ref.at[self.index]


class At:
    def __init__(self, ref):
        self.ref = ref

    def __getitem__(self, index):
        return View(self.ref, index)


def taken(ref):
    return ref.take() if isinstance(ref, View) else ref


def layer_kernel(names, *refs):
    k = Refs()
    for name, ref in zip(names, refs):
        setattr(k, name, ref)
    span, width = k.tok.shape
    quarter = k.gg.shape[2]
    tall, side = k.ra3.shape
    slim = k.gg.shape[1]
    half = slim // 2
    wide = 3 * width // 4

    r = lax.axis_index("rows")
    s = lax.axis_index("seq")
    c, x, y = bit_of(r, 1), bit_of(r, 2), bit_of(r, 4)
    z0, z1 = bit_of(s, 1), bit_of(s, 2)
    to_c = (flipped(r, 1), s)
    to_x = (flipped(r, 2), s)
    to_y = (flipped(r, 4), s)
    to_z = (r, flipped(s, 1))
    to_w = (r, flipped(s, 2))
    to_h = (r, 3 - s)
    to_t = (flipped(r, 2), flipped(s, 1))
    to_u = (flipped(flipped(r, 2), 1), flipped(s, 1))
    partners = (to_c, to_x, to_y, to_z, to_w, to_h, to_t, to_u)
    after = (r, lax.rem(s + 1, np.int32(4)))
    before = (r, lax.rem(s + 3, np.int32(4)))
    first_cols, last_cols = block(1 - z1, width // 2), block(z1, width // 2)
    active, idle = c == y, c != y
    holder, lender = c == z1, c != z1
    not_last, not_first = s < 3, s > 0
    home = [jnp.logical_and(active, jnp.logical_and(x == z0, y == i)) for i in range(2)]
    gives = [jnp.logical_and(active, jnp.logical_not(home[i])) for i in range(2)]
    targets = [(4 * y + 2 * z0 + i, 2 * z1 + x) for i in range(2)]
    away = jnp.logical_not(jnp.logical_and(active, x == z0))
    away_at = [jnp.logical_and(away, c == i) for i in range(2)]
    other_core = 1 - c

    sems = {}
    pending = []

    def sem_of(name, count=1):
        if name not in sems:
            sems[name] = sum(n for _, n in sems.values()), count
            assert sum(n for _, n in sems.values()) <= N_SEM
        return sems[name][0]

    def remote(name, src, dst, device, offset=0, count=1):
        at = sem_of(name, count) + offset
        return pltpu.make_async_remote_copy(
            src_ref=taken(src),
            dst_ref=taken(dst),
            send_sem=k.send.at[at],
            recv_sem=k.recv.at[at],
            device_id=device,
            device_id_type=MESH,
        )

    def send(name, src, dst, device, offset=0, count=1):
        remote(name, src, dst, device, offset, count).start()

    def later(cond, *args):
        pending.append((cond, args))

    def post(name, src, dst, device, cond=None, offset=0, count=1):
        def go():
            send(name, src, dst, device, offset, count)

        if cond is None:
            go()
        else:
            pl.when(cond)(go)
        later(cond, name, src, dst, device, offset, count)

    def arrived(name, dst, offset=0, count=1):
        remote(name, dst, dst, to_c, offset, count).wait_recv()

    local_count = [0]

    def fetch(src, dst):
        copy = pltpu.make_async_copy(src, dst, k.local.at[local_count[0]])
        local_count[0] += 1
        copy.start()
        return copy

    got_tok = fetch(k.tokens.at[0], k.tok)
    got_cot = fetch(k.cotangent.at[0], k.cot)
    barrier = pltpu.get_barrier_semaphore()
    for device in partners:
        pl.semaphore_signal(barrier, inc=1, device_id=device, device_id_type=MESH)
    got_wout = fetch(k.w_out, k.wout)

    position = s * span + lax.broadcasted_iota(jnp.int32, (span, 1), 0)
    starts = [np.int32(0)]
    for i in range(k.lengths.shape[1] - 1):
        starts.append(starts[-1] + k.lengths[0, i])

    def first_of(at):
        first = jnp.zeros_like(at)
        for start in starts:
            first = jnp.maximum(first, jnp.where(start <= at, start, 0))
        return first

    def flag(test):
        return jnp.where(test, 1.0, 0.0).astype(F32)

    first0, first1, first2 = (first_of(position + i) for i in range(3))
    columns = [
        flag(position < k.counts[0]),
        flag(position >= first0),
        flag(position - 1 >= first0),
        flag(position - 2 >= first0),
        flag(position >= first1),
        flag(position >= first2),
    ]
    lane = lax.broadcasted_iota(jnp.int32, (span, 128), 1)
    table = jnp.zeros((span, 128), F32)
    for i, column in enumerate(columns):
        table = jnp.where(lane == i, column, table)
    k.mask[...] = table

    def mask(i, rows=slice(None)):
        return k.mask[rows, i : i + 1]

    step = 64
    passes = span // step

    def mixer_forward(win):
        got_win = fetch(k.w_in, win)
        got_tok.wait()

        @functools.partial(loop, passes)
        def _(i):
            rows = block(i, step)
            t = k.tok[rows, :].astype(F32)
            scale = lax.rsqrt(jnp.mean(t * t, axis=-1, keepdims=True) + EPSILON)
            k.sc1[rows, :] = scale
            k.nrm[rows, :] = (t * scale * k.gain1[...].astype(F32)).astype(BF)

        got_cot.wait()

        @functools.partial(loop, passes)
        def _(i):
            rows = block(i, step)
            k.df[rows, :] = (mask(MASK_VALID, rows) * k.cot[rows, :].astype(F32)).astype(BF)

        pl.semaphore_wait(barrier, len(partners))
        own = pl.ds(0, span)
        post("df_c", At(k.df)[own], At(k.df)[pl.ds(span, span)], to_c)
        post(
            "df_z0",
            At(k.df)[own, first_cols],
            At(k.df)[pl.ds(2 * span, span), first_cols],
            to_z,
        )
        got_win.wait()

        @functools.partial(loop, width // 256)
        def _(j):
            n = k.nrm[:span, :]
            cols = block(j, 256)
            gb = dot(n, win[:, cols])
            va = dot(n, win[:, pl.ds(pl.multiple_of(2 * width + j * 256, 256), 256)])
            k.gb[:, cols] = gb.astype(BF)
            k.va[:, cols] = va.astype(BF)
            k.mix[8:, cols] = (mask(MASK_VALID) * gb * va).astype(BF).astype(F32)

        post("halo", At(k.mix)[pl.ds(span, 8)], k.hr, after, cond=not_last)

        @functools.partial(loop, width // 256)
        def _(j):
            cols = block(j, 256)
            c_cols = pl.ds(pl.multiple_of(width + j * 256, 256), 256)
            k.gc[:, cols] = dot(k.nrm[:span, :], win[:, c_cols])

    pl.run_scoped(mixer_forward, pltpu.VMEM((width, 3 * width), BF))

    @pl.when(s == 0)
    def _():
        k.mix[:8, :] = jnp.zeros((8, width), F32)

    @pl.when(s > 0)
    def _():
        arrived("halo", k.hr)
        k.mix[:8, :] = k.hr[...]

    def tap(i, cols):
        return k.taps[i : i + 1, cols].astype(F32)

    def conv_of(cols):
        return (
            tap(0, cols) * mask(MASK_S0) * k.mix[8 : 8 + span, cols]
            + tap(1, cols) * mask(MASK_S1) * k.mix[7 : 7 + span, cols]
            + tap(2, cols) * mask(MASK_S2) * k.mix[6 : 6 + span, cols]
        )

    @functools.partial(loop, width // 256)
    def _(j):
        cols = block(j, 256)
        k.gat[:span, cols] = (mask(MASK_VALID) * k.gc[:, cols] * conv_of(cols)).astype(BF)

    got_wout.wait()

    @functools.partial(loop, width // 256)
    def _(j):
        cols = block(j, 256)
        k.res[:, cols] = k.tok[:, cols].astype(F32) + dot(k.gat[:span, :], k.wout[:, cols])

    @functools.partial(loop, passes)
    def _(i):
        rows = block(i, step)
        v = k.res[rows, :]
        scale = lax.rsqrt(jnp.mean(v * v, axis=-1, keepdims=True) + EPSILON)
        k.sc2[rows, :] = scale
        k.n2[rows, :] = (v * scale * k.gain2[...].astype(F32)).astype(BF)

    part = span // 2
    for i in range(2):
        here = pl.ds(i * part, part)
        post(f"n2_z{i}", At(k.n2)[here], At(k.n2)[pl.ds(2 * span + i * part, part)], to_z)
    post("n2_c", At(k.n2)[pl.ds(0, span)], At(k.n2)[pl.ds(span, span)], to_c)
    post(
        "df_z1",
        At(k.df)[pl.ds(0, span), last_cols],
        At(k.df)[pl.ds(2 * span, span), last_cols],
        to_z,
    )
    post("nrm_c", At(k.nrm)[pl.ds(0, span)], At(k.nrm)[pl.ds(span, span)], to_c)
    post("gat_c", At(k.gat)[pl.ds(0, span)], At(k.gat)[pl.ds(span, span)], to_c)

    q = 2 * c + z0

    def gate_block(first, second, core):
        return 4 * second_of(second, y) + 2 * second_of(first, x) + core

    def second_of(rel, bit):
        return rel * bit + (1 - rel) * (1 - bit)

    def feed_forward(wg, wu, wd, hid, dg, du):
        got_wg = fetch(k.w_gate.at[:, block(q, quarter)], wg)
        got_wu = fetch(k.w_up.at[:, block(q, quarter)], wu)
        got_wd = fetch(k.w_down.at[block(q, quarter), :], wd)

        def expand(slot):
            rows = pl.ds(slot * span, span)

            def tile(cols):
                n = k.n2[rows, :]
                g = dot(n, wg[:, cols])
                u = dot(n, wu[:, cols])
                sig = jax.nn.sigmoid(g)
                silu = g * sig
                hid[rows, cols] = (silu * u).astype(BF)
                dg[rows, cols] = (u * sig * (1.0 + g * (1.0 - sig))).astype(BF)
                du[rows, cols] = silu.astype(BF)

            loop(quarter // 256, lambda j: tile(block(j, 256)))
            if quarter % 256:
                tile(pl.ds(quarter - quarter % 256, quarter % 256))

        def retreat(slot):
            rows = pl.ds(slot * span, span)

            def tile(cols):
                d = dot_nt(k.df[rows, :], wd[cols, :])
                dg[rows, cols] = (d * dg[rows, cols].astype(F32)).astype(BF)
                du[rows, cols] = (d * du[rows, cols].astype(F32)).astype(BF)

            loop(quarter // 256, lambda j: tile(block(j, 256)))
            if quarter % 256:
                tile(pl.ds(quarter - quarter % 256, quarter % 256))

        def back(slot, store):
            rows = pl.ds(slot * span, span)

            @functools.partial(loop, width // 256)
            def _(j):
                cols = block(j, 256)
                store(cols, dot_nt(dg[rows, :], wg[cols, :]) + dot_nt(du[rows, :], wu[cols, :]))

        def forth(slot, store):
            rows = pl.ds(slot * span, span)

            @functools.partial(loop, width // 256)
            def _(j):
                cols = block(j, 256)
                store(cols, dot(hid[rows, :], wd[:, cols]))

        def to_ref(ref, plus=None):
            def store(cols, value):
                if plus is not None:
                    value = value + plus[:, cols].astype(F32)
                ref[:, cols] = value.astype(ref.dtype)

            return store

        def down_grads(rel_w):
            for rel_x in range(2):
                sigma = 2 * second_of(rel_w, z1) + second_of(rel_x, x)
                value = dot_tn(hid[...], k.df[:, block(sigma, side)])
                u = 2 * rel_w + rel_x
                k.gd[u] = value[:tall].astype(BF)
                k.gd[4 + u] = value[tall:].astype(BF)
                if rel_x == 0:
                    post(f"ra1_{rel_w}", At(k.gd)[u], At(k.ra1)[rel_w], to_x)
                post(f"rb1_{u}", At(k.gd)[4 + u], At(k.rb1)[u], to_y, cond=idle)

        got_wg.wait()
        got_wu.wait()
        expand(0)
        arrived("n2_c", k.n2.at[pl.ds(span, span)])
        expand(1)
        got_wd.wait()
        retreat(0)
        arrived("df_c", k.df.at[pl.ds(span, span)])
        retreat(1)
        back(1, to_ref(k.ps.at[0]))
        post("pr0", At(k.ps)[0], At(k.pr)[0], to_c)
        z_rows = pl.ds(2 * span, span)
        t_rows = pl.ds(3 * span, span)
        arrived("df_z0", k.df.at[z_rows, first_cols])
        post("df_t0", At(k.df)[z_rows, first_cols], At(k.df)[t_rows, first_cols], to_c)
        arrived("pr0", k.pr.at[0])
        back(0, to_ref(k.own, k.pr.at[0]))
        for i in range(2):
            z_part = pl.ds(2 * span + i * part, part)
            t_part = pl.ds(3 * span + i * part, part)
            arrived(f"n2_z{i}", k.n2.at[z_part])
            post(f"n2_t{i}", At(k.n2)[z_part], At(k.n2)[t_part], to_c)
        expand(2)
        for i in range(2):
            arrived(f"n2_t{i}", k.n2.at[pl.ds(3 * span + i * part, part)])
        expand(3)
        arrived("df_t0", k.df.at[t_rows, first_cols])
        down_grads(0)
        arrived("df_z1", k.df.at[z_rows, last_cols])
        post("df_t1", At(k.df)[z_rows, last_cols], At(k.df)[t_rows, last_cols], to_c)
        retreat(2)
        arrived("df_t1", k.df.at[t_rows, last_cols])
        retreat(3)
        down_grads(1)
        back(3, to_ref(k.ps.at[1]))
        post("pr1", At(k.ps)[1], At(k.pr)[1], to_c)

        def gate_up(rel):
            @functools.partial(loop, 4)
            def _(i):
                second, core = lax.div(i, np.int32(2)), lax.rem(i, np.int32(2))
                rho = 4 * second_of(second, y) + 2 * second_of(rel, x) + core
                k.gg[4 * rel + i] = dot_tn(k.n2[:, block(rho, slim)], dg[...]).astype(BF)
                if rel == 0:
                    send("rg1", k.gg.at[i], k.rg1.at[i], to_x, i, 4)
                rho = 4 * second_of(rel, y) + 2 * second_of(second, x) + core
                k.gu[4 * rel + i] = dot_tn(k.n2[:, block(rho, slim)], du[...]).astype(BF)
                if rel == 0:
                    send("ru1", k.gu.at[i], k.ru1.at[i], to_y, i, 4)

        gate_up(0)
        for i in range(4):
            later(None, "rg1", At(k.gg)[i], At(k.rg1)[i], to_x, i, 4)
            later(None, "ru1", At(k.gu)[i], At(k.ru1)[i], to_y, i, 4)
        arrived("pr1", k.pr.at[1])
        back(2, to_ref(k.pr.at[1], k.pr.at[1]))
        post("pz", At(k.pr)[1], k.pz, to_z)
        gate_up(1)
        down_x(0)
        down_x(1)
        for i in range(2):
            cond, args = next(p for p in pending if p[1][0] == f"pr{i}")
            remote(*args).wait_send()
            pending.remove((cond, args))
        forth(1, to_ref(k.ps.at[0]))
        post("fr0", At(k.ps)[0], At(k.fr)[0], to_c)
        forth(3, to_ref(k.ps.at[1]))
        post("fr1", At(k.ps)[1], At(k.fr)[1], to_c)
        arrived("fr1", k.fr.at[1])
        forth(2, to_ref(k.fr.at[1], k.fr.at[1]))
        post("fz", At(k.fr)[1], k.fz, to_z)
        arrived("fr0", k.fr.at[0])

        def store_out(cols, value):
            value = value + k.fr[0, :, cols].astype(F32)
            k.loa[:, cols] = k.res[:, cols] + mask(MASK_VALID) * value

        forth(0, store_out)

    def add(dst, src):
        dst[...] = (dst[...].astype(F32) + src[...].astype(F32)).astype(BF)

    def down_x(rel_w):
        arrived(f"ra1_{rel_w}", k.ra1.at[rel_w])
        add(k.ra1.at[rel_w], k.gd.at[2 * rel_w + 1])
        post(f"ra2_{rel_w}", At(k.ra1)[rel_w], At(k.ra2)[rel_w], to_y, cond=idle)

    def down_y(rel_w):
        @pl.when(active)
        def _():
            arrived(f"ra2_{rel_w}", k.ra2.at[rel_w])
            add(k.ra2.at[rel_w], k.ra1.at[rel_w])

        if rel_w == 0:
            post("ra3", At(k.ra2)[0], k.ra3, to_w, cond=active)

    def up_y(u):
        @pl.when(active)
        def _():
            arrived(f"rb1_{u}", k.rb1.at[u])
            add(k.rb1.at[u], k.gd.at[4 + u])

        if u % 2 == 0:
            post(f"rb2_{u // 2}", At(k.rb1)[u], At(k.rb2)[u // 2], to_x, cond=active)

    def up_x(rel_w):
        @pl.when(active)
        def _():
            arrived(f"rb2_{rel_w}", k.rb2.at[rel_w])
            add(k.rb2.at[rel_w], k.rb1.at[2 * rel_w + 1])

        if rel_w == 0:
            post("rb3", At(k.rb2)[0], k.rb3, to_w, cond=active)

    stored = []

    def down_last(i):
        got, mine = (k.ra3, k.ra2.at[1]) if i == 0 else (k.rb3, k.rb2.at[1])

        @pl.when(active)
        def _():
            arrived("ra3" if i == 0 else "rb3", got)
            add(got, mine)

        post(f"rd4_{i}", got, k.rd4, targets[i], cond=gives[i])
        put(got, k.g_down, home[i])

    def put(src, dst, cond=None):
        at = local_count[0]
        local_count[0] += 1
        copy = pltpu.make_async_copy(src, dst, k.local.at[at])
        if cond is None:
            copy.start()
        else:
            pl.when(cond)(copy.start)
        stored.append((cond, copy))

    def down_take():
        for i in range(2):

            @pl.when(away_at[i])
            def _():
                arrived(f"rd4_{i}", k.rd4)

        put(k.rd4, k.g_down, away)

    def wide_1(tag, i):
        first, own, next_, device = (
            (k.rg1, k.gg, k.rg2, to_y) if tag == "g" else (k.ru1, k.gu, k.ru2, to_x)
        )
        arrived(f"r{tag}1", first.at[i], i, 4)
        add(first.at[i], own.at[4 + i])
        if i < 2:
            post(f"r{tag}2_{i}", At(first)[i], At(next_)[i], device)

    def wide_2(tag, i):
        first, got, next_ = (k.rg1, k.rg2, k.rg3) if tag == "g" else (k.ru1, k.ru2, k.ru3)
        arrived(f"r{tag}2_{i}", got.at[i])
        add(got.at[i], first.at[2 + i])
        post(f"r{tag}3_{i}", At(got)[i], At(next_)[i], to_w, cond=lender)

    def wide_3(tag):
        got, mine, last, out = (
            (k.rg3, k.rg2, k.rg4, k.g_gate) if tag == "g" else (k.ru3, k.ru2, k.ru4, k.g_up)
        )

        @pl.when(holder)
        def _():
            for i in range(2):
                arrived(f"r{tag}3_{i}", got.at[i])
                add(got.at[i], mine.at[i])

        post(f"r{tag}4", At(got)[other_core], last, to_c, cond=holder)
        put(got.at[c], out, holder)

    def wide_4(tag):
        last, out = (k.rg4, k.g_gate) if tag == "g" else (k.ru4, k.g_up)

        @pl.when(lender)
        def _():
            arrived(f"r{tag}4", last)

        put(last, out, lender)

    def mix_1(h, b, w):
        i = 2 * b + w
        arrived(f"m1_{h}_{i}", k.m1.at[h, i])
        add(k.m1.at[h, i], gm_ref.at[h, 1, i])
        post(f"m2_{h}_{i}", At(k.m1)[h, i, 0], At(k.m2)[h, i], to_z)

    def mix_2(h, b, w):
        i = 2 * b + w
        arrived(f"m2_{h}_{i}", k.m2.at[h, i])
        add(k.m2.at[h, i], k.m1.at[h, i, 1])
        if w == 0:
            post(f"m3_{h}_{b}", At(k.m2)[h, i], At(k.m3)[h, b], to_w)

    def mix_3(h, b):
        arrived(f"m3_{h}_{b}", k.m3.at[h, b])
        add(k.m3.at[h, b], k.m2.at[h, 2 * b + 1])
        if b == 0:
            post(f"m4_{h}", At(k.m3)[h, 0], At(k.m4)[h], to_y if h == 0 else to_x)

    def mix_4(h):
        arrived(f"m4_{h}", k.m4.at[h])
        add(k.m4.at[h], k.m3.at[h, 1])
        rows = pl.ds(h * half, half)
        put(k.m4.at[h, :, pl.ds(0, wide)], k.g_in.at[rows, :])
        put(k.m4.at[h, :, pl.ds(wide, width - wide)], k.g_out.at[rows, :])

    small_to = (to_c, to_x, to_y, to_z, to_w)

    def small_send(i):
        post(f"sg{i}", At(k.sg)[i], At(k.sg)[i + 1], small_to[i])

    def small_take(i):
        arrived(f"sg{i}", k.sg.at[i + 1])
        k.sg[i + 1] = k.sg[i + 1] + k.sg[i]

    pl.run_scoped(
        feed_forward,
        pltpu.VMEM((width, quarter), BF),
        pltpu.VMEM((width, quarter), BF),
        pltpu.VMEM((quarter, width), BF),
        pltpu.VMEM((4 * span, quarter), BF),
        pltpu.VMEM((4 * span, quarter), BF),
        pltpu.VMEM((4 * span, quarter), BF),
    )

    gm_ref = None

    def mixer_backward(win, gm):
        nonlocal gm_ref
        gm_ref = gm
        got_win = fetch(k.w_in, win)
        arrived("pz", k.pz)
        k.sg[0] = jnp.zeros((8, width), F32)

        @functools.partial(loop, passes)
        def _(i):
            rows = block(i, step)
            d = k.own[rows, :] + k.pz[rows, :].astype(F32)
            v = k.res[rows, :]
            scale = k.sc2[rows, :]
            scaled = k.gain2[...].astype(F32) * d
            k.sg[0, 1:2, :] = k.sg[0, 1:2, :] + jnp.sum(d * v * scale, axis=0, keepdims=True)
            d = (
                k.cot[rows, :].astype(F32)
                + scale * scaled
                - v * (scale * scale * scale) * jnp.mean(scaled * v, axis=-1, keepdims=True)
            )
            k.own[rows, :] = d
            k.dmx[rows, :] = d.astype(BF)

        post("dmx_c", At(k.dmx)[pl.ds(0, span)], At(k.dmx)[pl.ds(span, span)], to_c)

        @functools.partial(loop, width // 256)
        def _(j):
            cols = block(j, 256)
            d = dot_nt(k.dmx[:span, :], k.wout[cols, :])
            valid = mask(MASK_VALID)
            k.dc[:span, cols] = (valid * k.gc[:, cols] * d).astype(BF).astype(F32)
            c_cols = pl.ds(pl.multiple_of(width + j * 256, 256), 256)
            k.dpj[:span, c_cols] = (valid * conv_of(cols) * d).astype(BF)

        post("halo2", At(k.dc)[pl.ds(0, 8)], k.hr2, before, cond=not_first)

        @pl.when(s == 3)
        def _():
            k.dc[span:, :] = jnp.zeros((8, width), F32)

        @pl.when(s < 3)
        def _():
            arrived("halo2", k.hr2)
            k.dc[span:, :] = k.hr2[...]

        @functools.partial(loop, width // 256)
        def _(j):
            cols = block(j, 256)
            d0 = k.dc[:span, cols]
            d = (
                tap(0, cols) * mask(MASK_S0) * d0
                + tap(1, cols) * mask(MASK_N1) * k.dc[1 : 1 + span, cols]
                + tap(2, cols) * mask(MASK_N2) * k.dc[2 : 2 + span, cols]
            )
            valid = mask(MASK_VALID)
            k.dpj[:span, cols] = (valid * k.va[:, cols].astype(F32) * d).astype(BF)
            x_cols = pl.ds(pl.multiple_of(2 * width + j * 256, 256), 256)
            k.dpj[:span, x_cols] = (valid * k.gb[:, cols].astype(F32) * d).astype(BF)
            for i, m in ((0, MASK_S0), (1, MASK_S1), (2, MASK_S2)):
                k.sg[0, 2 + i : 3 + i, cols] = jnp.sum(
                    d0 * mask(m) * k.mix[8 - i : 8 - i + span, cols], axis=0, keepdims=True
                )

        post("dpj_c", At(k.dpj)[pl.ds(0, span)], At(k.dpj)[pl.ds(span, span)], to_c)
        for name, ref in (("nrm_c", k.nrm), ("gat_c", k.gat), ("dmx_c", k.dmx), ("dpj_c", k.dpj)):
            arrived(name, ref.at[pl.ds(span, span)])

        for rel_x in range(2):
            for rel_y in range(2):
                rho = 4 * second_of(rel_y, y) + 2 * second_of(rel_x, x) + c

                @functools.partial(loop, 4)
                def _(i):
                    w, j0 = lax.div(i, np.int32(2)), lax.rem(i, np.int32(2))
                    sigma = 2 * second_of(w, z1) + second_of(j0, z0)
                    value = dot_tn(k.nrm[:, block(rho, slim)], k.dpj[:, block(sigma, wide)])
                    lower, upper = 2 * rel_y + w, 2 * rel_x + w
                    gm[0, rel_x, lower, j0, :, :wide] = value[:half].astype(BF)
                    gm[1, rel_y, upper, j0, :, :wide] = value[half:].astype(BF)
                    value = dot_tn(k.gat[:, block(rho, slim)], k.dmx[:, block(sigma, side)])
                    gm[0, rel_x, lower, j0, :, wide:] = value[:half].astype(BF)
                    gm[1, rel_y, upper, j0, :, wide:] = value[half:].astype(BF)

                for w in range(2):
                    if rel_x == 0:
                        i = 2 * rel_y + w
                        post(f"m1_0_{i}", At(gm)[0, 0, i], At(k.m1)[0, i], to_x)
                    if rel_y == 0:
                        i = 2 * rel_x + w
                        post(f"m1_1_{i}", At(gm)[1, 0, i], At(k.m1)[1, i], to_y)

        got_win.wait()

        @functools.partial(loop, width // 256)
        def _(j):
            cols = block(j, 256)
            k.gc[:, cols] = dot_nt(k.dpj[:span, :], win[cols, :])

        @functools.partial(loop, passes)
        def _(i):
            rows = block(i, step)
            d = k.gc[rows, :]
            t = k.tok[rows, :].astype(F32)
            scale = k.sc1[rows, :]
            scaled = k.gain1[...].astype(F32) * d
            k.sg[0, 0:1, :] = k.sg[0, 0:1, :] + jnp.sum(d * t * scale, axis=0, keepdims=True)
            d = (
                k.own[rows, :]
                + scale * scaled
                - t * (scale * scale * scale) * jnp.mean(scaled * t, axis=-1, keepdims=True)
            )
            k.tok[rows, :] = d.astype(BF)

        put(k.tok, k.grad_tokens.at[0])
        small_send(0)

        for u in range(4):
            up_y(u)
        for w in range(2):
            down_y(w)
        for i in range(4):
            wide_1("g", i)
            wide_1("u", i)
            if i < 4:
                small_take(i)
                small_send(i + 1)
        small_take(4)
        k.sm[...] = k.sg[5, :, block(r, 128)]
        put(k.sm, k.small)
        arrived("fz", k.fz)

        @functools.partial(loop, passes)
        def _(i):
            rows = block(i, step)
            valid = mask(MASK_VALID, rows)
            k.cot[rows, :] = (k.loa[rows, :] + valid * k.fz[rows, :].astype(F32)).astype(BF)

        put(k.cot, k.layer_out.at[0])
        up_x(0)
        up_x(1)
        for i in range(2):
            wide_2("g", i)
            wide_2("u", i)
        down_last(0)
        down_last(1)
        order = [(0, 0), (0, 1), (1, 0), (1, 1)]
        for b, w in order:
            for h in range(2):
                mix_1(h, b, w)
        wide_3("g")
        wide_3("u")
        for b, w in order:
            for h in range(2):
                mix_2(h, b, w)
        wide_4("g")
        wide_4("u")
        down_take()
        for b in range(2):
            for h in range(2):
                mix_3(h, b)
        for h in range(2):
            mix_4(h)
        for cond, args in pending:
            leave = remote(*args).wait_send
            if cond is None:
                leave()
            else:
                pl.when(cond)(leave)
        for cond, copy in stored:
            if cond is None:
                copy.wait()
            else:
                pl.when(cond)(copy.wait)

    pl.run_scoped(
        mixer_backward,
        pltpu.VMEM((width, 3 * width), BF),
        pltpu.VMEM((2, 2, 4, 2, half, width), BF),
    )


def fused(
    tokens,
    doc_lengths,
    valid_counts,
    norm_in,
    w_in,
    w_conv,
    w_out,
    norm_ffn,
    w_gate,
    w_up,
    w_down,
    cotangent,
):
    _, span, width = tokens.shape
    ff = w_gate.shape[1]
    rows, seq = lax.axis_size("rows"), lax.axis_size("seq")
    scratch = scratch_list(span, width, ff, rows, seq)
    anywhere = pl.BlockSpec(memory_space=pl.ANY)
    scalars = pl.BlockSpec(memory_space=pltpu.SMEM)
    vectors = pl.BlockSpec(memory_space=pltpu.VMEM)
    outs = pl.pallas_call(
        functools.partial(layer_kernel, OPERANDS + [name for name, _ in scratch]),
        out_shape=[
            jax.ShapeDtypeStruct((1, span, width), BF),
            jax.ShapeDtypeStruct((1, span, width), BF),
            jax.ShapeDtypeStruct((width // rows, 3 * width // seq), BF),
            jax.ShapeDtypeStruct((width // rows, width // seq), BF),
            jax.ShapeDtypeStruct((width // rows, ff // seq), BF),
            jax.ShapeDtypeStruct((width // rows, ff // seq), BF),
            jax.ShapeDtypeStruct((ff // rows, width // seq), BF),
            jax.ShapeDtypeStruct((8, 128), F32),
        ],
        in_specs=[scalars] * 2
        + [anywhere] * 2
        + [vectors] * 3
        + [anywhere] * 5,
        out_specs=[anywhere] * 8,
        scratch_shapes=[shape for _, shape in scratch],
        compiler_params=pltpu.CompilerParams(
            collective_id=0, has_side_effects=True, vmem_limit_bytes=67043328
        ),
        name="layer",
    )(
        doc_lengths,
        valid_counts,
        tokens,
        cotangent,
        norm_in[None],
        w_conv,
        norm_ffn[None],
        w_in,
        w_out,
        w_gate,
        w_up,
        w_down,
    )
    layer_out, grad_tokens, g_in, g_out, g_gate, g_up, g_down, small = outs
    piece = width // (rows * seq)
    small = lax.dynamic_slice(small, (0, lax.axis_index("seq") * piece), (8, piece))
    return (
        layer_out,
        grad_tokens,
        small[0],
        g_in.astype(F32),
        small[2:5],
        g_out.astype(F32),
        small[1],
        g_gate.astype(F32),
        g_up.astype(F32),
        g_down.astype(F32),
    )


def solution(mesh):
    placed = (
        P("rows", "seq", None),
        P("rows", None),
        P("rows"),
        P(),
        P(),
        P(),
        P(),
        P(),
        P(),
        P(),
        P(),
        P("rows", "seq", None),
    )
    paired = mesh.shape["rows"] == 8 and mesh.shape["seq"] == 4
    return jax.shard_map(
        fused if paired else plain,
        mesh=mesh,
        in_specs=placed,
        out_specs=(
            P("rows", "seq", None),
            P("rows", "seq", None),
            P(("rows", "seq")),
            P("rows", "seq"),
            P(None, ("rows", "seq")),
            P("rows", "seq"),
            P(("rows", "seq")),
            P("rows", "seq"),
            P("rows", "seq"),
            P("rows", "seq"),
        ),
        check_vma=False,
    )
```

```python
import functools

import jax
import jax.numpy as jnp
import numpy as np
from jax import lax
from jax.experimental import pallas as pl
from jax.experimental.pallas import tpu as pltpu
from jax.sharding import PartitionSpec as P

EPSILON = 1e-05
BF = jnp.bfloat16
F32 = jnp.float32
MESH = pl.DeviceIdType.MESH


def passed_along(value, axis, steps):
    count = lax.axis_size(axis)
    first, last = (max(0, -steps), min(count, count - steps))
    return lax.ppermute(value, axis, [(source, source + steps) for source in range(first, last)])


def rms_scale(values):
    return lax.rsqrt(jnp.mean(values * values, axis=-1, keepdims=True) + EPSILON)


def doc_masks(lengths, positions):
    starts = jnp.cumsum(lengths) - lengths
    within = starts[None, :] <= positions[:, None]
    first = jnp.max(jnp.where(within, starts[None, :], 0), axis=1)
    return [(positions - offset >= first).astype(jnp.float32)[:, None] for offset in range(3)]


def weight_grad(left, right):
    return jnp.einsum("ta,tb->ab", left, right, preferred_element_type=jnp.float32)


def back_product(grad, weight):
    return jnp.einsum("tb,ab->ta", grad, weight, preferred_element_type=jnp.float32)


def scattered(value, row_dim, seq_dim):
    part = lax.psum_scatter(value.astype(BF), "rows", scatter_dimension=row_dim, tiled=True)
    part = lax.psum_scatter(part, "seq", scatter_dimension=seq_dim, tiled=True)
    return part.astype(F32)


def plain(
    tokens,
    doc_lengths,
    valid_counts,
    norm_in,
    w_in,
    w_conv,
    w_out,
    norm_ffn,
    w_gate,
    w_up,
    w_down,
    cotangent,
):
    inputs = tokens[0].astype(jnp.float32)
    span = inputs.shape[0]
    width = inputs.shape[1]
    start_pos = lax.axis_index("seq") * span
    positions = start_pos + jnp.arange(span + 2, dtype=jnp.int32)
    valid = (positions[:span] < valid_counts[0]).astype(jnp.float32)[:, None]
    same = doc_masks(doc_lengths[0], positions)
    taps = w_conv.astype(jnp.float32)
    gain_in = norm_in.astype(jnp.float32)
    gain_ffn = norm_ffn.astype(jnp.float32)
    scale1 = rms_scale(inputs)
    normed = (inputs * scale1 * gain_in).astype(jnp.bfloat16)
    proj = jnp.dot(normed, w_in, preferred_element_type=jnp.float32)
    gate_b = proj[:, :width]
    gate_c = proj[:, width : 2 * width]
    values = proj[:, 2 * width :]
    mixed_in = (valid * gate_b * values).astype(jnp.bfloat16)
    tail_rows = passed_along(mixed_in[span - 2 :], "seq", 1)
    padded = jnp.concatenate([tail_rows, mixed_in], axis=0).astype(jnp.float32)
    conv = jnp.zeros((span, width), jnp.float32)
    for offset in range(3):
        conv = conv + taps[offset] * same[offset][:span] * padded[2 - offset : 2 - offset + span]
    gated = (valid * gate_c * conv).astype(jnp.bfloat16)
    mixer_out = jnp.dot(gated, w_out, preferred_element_type=jnp.float32)
    resid = inputs + mixer_out
    scale2 = rms_scale(resid)
    normed2 = (resid * scale2 * gain_ffn).astype(jnp.bfloat16)
    gate_act = jnp.dot(normed2, w_gate, preferred_element_type=jnp.float32)
    up_act = jnp.dot(normed2, w_up, preferred_element_type=jnp.float32)
    sigmoid_gate = jax.nn.sigmoid(gate_act)
    silu_gate = gate_act * sigmoid_gate
    hidden = (silu_gate * up_act).astype(jnp.bfloat16)
    ffn_out = jnp.dot(hidden, w_down, preferred_element_type=jnp.float32)
    layer_out = (resid + valid * ffn_out).astype(jnp.bfloat16)
    grad_out = cotangent[0].astype(jnp.float32)
    d_ffn = (valid * grad_out).astype(jnp.bfloat16)
    grad_w_down = weight_grad(hidden, d_ffn)
    d_hidden = back_product(d_ffn, w_down)
    d_gate = (d_hidden * up_act * sigmoid_gate * (1.0 + gate_act * (1.0 - sigmoid_gate))).astype(
        jnp.bfloat16
    )
    d_up = (d_hidden * silu_gate).astype(jnp.bfloat16)
    grad_w_gate = weight_grad(normed2, d_gate)
    grad_w_up = weight_grad(normed2, d_up)
    d_normed2 = back_product(d_gate, w_gate) + back_product(d_up, w_up)
    grad_norm_ffn = jnp.sum(d_normed2 * resid * scale2, axis=0)
    scaled_ffn = gain_ffn * d_normed2
    d_resid = (
        grad_out
        + scale2 * scaled_ffn
        - resid * scale2**3 * jnp.mean(scaled_ffn * resid, axis=-1, keepdims=True)
    )
    d_mixer = d_resid.astype(jnp.bfloat16)
    grad_w_out = weight_grad(gated, d_mixer)
    d_gated = back_product(d_mixer, w_out)
    d_conv = (valid * gate_c * d_gated).astype(jnp.bfloat16)
    d_gate_c = valid * conv * d_gated
    head_rows = passed_along(d_conv[:2], "seq", -1)
    extended = jnp.concatenate([d_conv, head_rows], axis=0).astype(jnp.float32)
    d_mixed = jnp.zeros((span, width), jnp.float32)
    conv_rows = []
    for offset in range(3):
        d_mixed = (
            d_mixed
            + taps[offset] * same[offset][offset : offset + span] * extended[offset : offset + span]
        )
        conv_rows.append(
            jnp.sum(
                extended[:span] * same[offset][:span] * padded[2 - offset : 2 - offset + span],
                axis=0,
            )
        )
    grad_w_conv = jnp.stack(conv_rows, axis=0)
    d_proj = jnp.concatenate(
        [valid * values * d_mixed, d_gate_c, valid * gate_b * d_mixed], axis=1
    ).astype(jnp.bfloat16)
    grad_w_in = weight_grad(normed, d_proj)
    d_normed = back_product(d_proj, w_in)
    grad_norm_in = jnp.sum(d_normed * inputs * scale1, axis=0)
    scaled_in = gain_in * d_normed
    grad_tokens = (
        d_resid
        + scale1 * scaled_in
        - inputs * scale1**3 * jnp.mean(scaled_in * inputs, axis=-1, keepdims=True)
    )
    grad_tokens = grad_tokens.astype(jnp.bfloat16)
    return (
        layer_out[None],
        grad_tokens[None],
        scattered(grad_norm_in, 0, 0),
        scattered(grad_w_in, 0, 1),
        scattered(grad_w_conv, 1, 1),
        scattered(grad_w_out, 0, 1),
        scattered(grad_norm_ffn, 0, 0),
        scattered(grad_w_gate, 0, 1),
        scattered(grad_w_up, 0, 1),
        scattered(grad_w_down, 0, 1),
    )


def dot(a, b):
    return jnp.dot(a, b, preferred_element_type=F32)


def dot_nt(a, b):
    return lax.dot_general(a, b, (((1,), (1,)), ((), ())), preferred_element_type=F32)


def dot_tn(a, b):
    return lax.dot_general(a, b, (((0,), (0,)), ((), ())), preferred_element_type=F32)


def bit_of(value, weight):
    return lax.rem(lax.div(value, np.int32(weight)), np.int32(2))


def flipped(value, weights):
    for weight in (1, 2, 4):
        if weights & weight:
            value = value + weight - 2 * weight * bit_of(value, weight)
    return value


def loop(count, body, unroll=True):
    lax.fori_loop(0, count, lambda i, carry: (body(i), carry)[1], 0, unroll=unroll)


def block(index, size):
    return pl.ds(pl.multiple_of(index * size, size), size)


class Name(str):
    def __call__(self, *index):
        return (self,) + index


class Names:
    def __getattr__(self, name):
        return Name(name)


N = Names()

STAGES = {
    N.A: (N.x, N.y, N.z1),
    N.B: (N.y, N.z1, N.x),
    N.g0: (N.y, N.x, N.z1),
    N.g1: (N.x, N.y, N.z1),
    N.u0: (N.x, N.y, N.z1),
    N.u1: (N.x, N.y, N.z1),
    N.m0: (N.y, N.x, N.z0, N.z1),
    N.m1: (N.y, N.x, N.z0, N.z1),
}
ORDER = [
    N.ex(0), N.tdf(0), N.re(0), N.ex(1), N.re(1), N.bk(1), N.bk(0), N.tn(0),
    N.ex(2, 0), N.ex(3, 0), N.tn(1), N.ex(2, 1), N.ex(3, 1), N.dn(0), N.tdf(1), N.re(2),
    N.re(3), N.dn(1), N.B(0, 0), N.bk(3), N.gg(0, 0), N.uu(0, 0), N.gg(1, 0), N.A(0, 0),
    N.B(0, 1), N.uu(1, 0), N.bk(2), N.gg(0, 1), N.uu(0, 1), N.gg(1, 1), N.uu(1, 1), N.gg(0, 2),
    N.uu(0, 2), N.gg(1, 2), N.uu(1, 2), N.gg(0, 3), N.uu(0, 3), N.B(0, 2), N.gg(1, 3), N.uu(1, 3),
    N.A(0, 1), N.fo(1), N.B(1, 0), N.fo(3), N.fo(2), N.fo(0), N.B(0, 3), N.g0(0, 0),
    N.u0(0, 0), N.B(1, 1), N.g1(0, 0), N.mb(1), N.mb(2), N.g0(0, 1), N.A(1, 0), N.u1(0, 0),
    N.mb(3), N.mb(4), N.lo, N.u0(0, 1), N.mg(0, 0), N.mg(0, 1), N.u0(1, 0), N.mg(1, 0),
    N.A(1, 1), N.mg(1, 1), N.g1(0, 1), N.A(2, 0), N.dl(0), N.g1(1, 0), N.u1(0, 1), N.u0(2, 0),
    N.m0(0, 0), N.u1(1, 0), N.m1(0, 0), N.B(2, 0), N.dl(1), N.g1(2, 0), N.u1(2, 0), N.w3(N.u),
    N.m0(0, 1), N.w4(N.u), N.g0(1, 0), N.m1(0, 1), N.sg(0), N.g0(2, 0), N.w3(N.g), N.m0(0, 2),
    N.w4(N.g), N.dt, N.m1(0, 2), N.m0(0, 3), N.sg(1), N.m1(0, 3), N.m0(0, 4), N.m0(1, 0),
    N.m1(0, 4), N.m1(1, 0), N.m0(0, 5), N.m0(1, 1), N.m1(0, 5), N.m1(1, 1), N.m0(0, 6), N.m0(1, 2),
    N.m0(2, 0), N.m1(0, 6), N.m1(1, 2), N.m1(2, 0), N.m0(0, 7), N.m0(1, 3), N.m0(2, 1), N.m0(3, 0),
    N.m1(0, 7), N.m1(1, 3), N.m1(2, 1), N.m1(3, 0),
]
FEED = (N.ex, N.re, N.bk, N.dn, N.gg, N.uu, N.fo)
MIXED = [N.m0, N.m1]
DOWN = [N.A, N.B]
GATE = [N.g0, N.g1]
UP = [N.u0, N.u1]
N_SEM = 192
MASK_VALID, MASK_S0, MASK_S1, MASK_S2, MASK_N1, MASK_N2 = range(6)


def scatter_of(tag):
    return (N.x, N.y, N.z0, N.z1) if tag in MIXED else (N.x, N.z1) if tag in DOWN else (N.x, N.y)


def counts_of(tag):
    counts = [2 ** len(scatter_of(tag))]
    for dim in STAGES[tag]:
        counts.append(counts[-1] // 2 if dim in scatter_of(tag) else counts[-1])
    return counts


def unit_index(tag, rel):
    index = 0
    for dim in STAGES[tag]:
        if dim in scatter_of(tag):
            index = 2 * index + rel[dim]
    return index


def unit_bits(tag, index):
    dims = [dim for dim in STAGES[tag] if dim in scatter_of(tag)]
    return {dim: (index >> (len(dims) - 1 - i)) & 1 for i, dim in enumerate(dims)}


def unit_shape(tag, width, ff, rows, seq):
    if tag in DOWN:
        return ff // rows, width // seq
    if tag in MIXED:
        return width // rows // len(MIXED), width
    return width // rows, ff // 4


def scratch_list(span, width, ff, rows, seq):
    group = 4 * span
    shapes = dict(
        tok=pltpu.VMEM((span, width), BF),
        cot=pltpu.VMEM((span, width), BF),
        wout=pltpu.VMEM((width, width), BF),
        nrm=pltpu.VMEM((2 * span, width), BF),
        gat=pltpu.VMEM((2 * span, width), BF),
        dmx=pltpu.VMEM((2 * span, width), BF),
        dpj=pltpu.VMEM((2 * span, 3 * width), BF),
        gb=pltpu.VMEM((span, width), BF),
        va=pltpu.VMEM((span, width), BF),
        gc=pltpu.VMEM((span, width), F32),
        mix=pltpu.VMEM((span + 8, width), F32),
        dc=pltpu.VMEM((span + 8, width), F32),
        res=pltpu.VMEM((span, width), F32),
        own=pltpu.VMEM((span, width), F32),
        loa=pltpu.VMEM((span, width), F32),
        mask=pltpu.VMEM((span, 128), F32),
        sc1=pltpu.VMEM((span, 1), F32),
        sc2=pltpu.VMEM((span, 1), F32),
        n2=pltpu.VMEM((group, width), BF),
        df=pltpu.VMEM((group, width), BF),
        hr=pltpu.VMEM((8, width), F32),
        hr2=pltpu.VMEM((8, width), F32),
        ps=pltpu.VMEM((2, span, width), BF),
        pr=pltpu.VMEM((2, span, width), BF),
        pz=pltpu.VMEM((span, width), BF),
        fr=pltpu.VMEM((2, span, width), BF),
        fz=pltpu.VMEM((span, width), BF),
        sg=pltpu.VMEM((8, width), F32),
        sa=pltpu.VMEM((rows - 1, 8, width // rows), F32),
        ss=pltpu.VMEM((8, width // rows), F32),
        sb=pltpu.VMEM((seq - 1, 8, width // rows), F32),
        rd4=pltpu.VMEM(unit_shape(N.A, width, ff, rows, seq), BF),
        rg4=pltpu.VMEM(unit_shape(N.g0, width, ff, rows, seq), BF),
        ru4=pltpu.VMEM(unit_shape(N.u0, width, ff, rows, seq), BF),
        send=pltpu.SemaphoreType.DMA((N_SEM,)),
        recv=pltpu.SemaphoreType.DMA((N_SEM,)),
        local=pltpu.SemaphoreType.DMA((32,)),
    )
    for tag in STAGES:
        unit = unit_shape(tag, width, ff, rows, seq)
        counts = counts_of(tag)
        if tag not in MIXED:
            shapes[N.own, tag] = pltpu.VMEM((counts[0],) + unit, BF)
        shapes[N.got, tag] = pltpu.VMEM((sum(counts[1:]),) + unit, BF)
    return shapes


OPERANDS = [
    N.lengths,
    N.counts,
    N.tokens,
    N.cotangent,
    N.gain1,
    N.taps,
    N.gain2,
    N.w_in,
    N.w_out,
    N.w_gate,
    N.w_up,
    N.w_down,
    N.layer_out,
    N.grad_tokens,
    N.g_in,
    N.g_out,
    N.g_gate,
    N.g_up,
    N.g_down,
    N.small,
]


class Refs:
    pass


class View:
    def __init__(self, ref, index):
        self.ref, self.index = ref, index

    def take(self):
        return self.ref.at[self.index]


class At:
    def __init__(self, ref):
        self.ref = ref

    def __getitem__(self, index):
        return View(self.ref, index)


def taken(ref):
    return ref.take() if isinstance(ref, View) else ref


def layer_kernel(names, *refs):
    k = Refs()
    travelling = {}
    for name, ref in zip(names, refs):
        if isinstance(name, tuple):
            travelling[name] = ref
        else:
            setattr(k, name, ref)
    span, width = k.tok.shape
    slim, quarter = k.rg4.shape
    tall, side = k.rd4.shape
    wide = 3 * width // 4

    r = lax.axis_index("rows")
    s = lax.axis_index("seq")
    c, x, y = bit_of(r, 1), bit_of(r, 2), bit_of(r, 4)
    z0, z1 = bit_of(s, 1), bit_of(s, 2)
    row_peers = [flipped(r, i) for i in range(8)]
    seq_peers = [flipped(s, i) for i in range(4)]
    to_c = (row_peers[1], s)
    to_z = (r, seq_peers[1])
    to_dim = {
        N.x: (row_peers[2], s),
        N.y: (row_peers[4], s),
        N.z0: to_z,
        N.z1: (r, seq_peers[2]),
    }
    partners = [(row, s) for row in row_peers[1:]] + [(r, seq) for seq in seq_peers[1:]]
    partners += [(row_peers[2], seq_peers[1]), (row_peers[3], seq_peers[1])]
    after = (r, lax.rem(s + 1, np.int32(4)))
    before = (r, lax.rem(s + 3, np.int32(4)))
    first_cols, last_cols = block(1 - z1, width // 2), block(z1, width // 2)
    active, idle = c == y, c != y
    holder, lender = c == z1, c != z1
    not_last, not_first = s < 3, s > 0
    home = [jnp.logical_and(active, jnp.logical_and(x == z0, y == i)) for i in range(2)]
    gives = [jnp.logical_and(active, jnp.logical_not(home[i])) for i in range(2)]
    targets = [(4 * y + 2 * z0 + i, 2 * z1 + x) for i in range(2)]
    away = jnp.logical_not(jnp.logical_and(active, x == z0))
    away_at = [jnp.logical_and(away, c == i) for i in range(2)]
    core_is = [c == 0, c == 1]
    holds = [jnp.logical_and(holder, c == i) for i in range(2)]
    small_cols = [block(row, slim) for row in row_peers]

    sems = {}
    pending = {}

    def remote(name, src, dst, device):
        at = sems.setdefault(name, len(sems))
        assert at < N_SEM
        return pltpu.make_async_remote_copy(
            src_ref=taken(src),
            dst_ref=taken(dst),
            send_sem=k.send.at[at],
            recv_sem=k.recv.at[at],
            device_id=device,
            device_id_type=MESH,
        )

    def when(cond, go):
        if cond is None:
            go()
        else:
            pl.when(cond)(go)

    def post(name, src, dst, device, cond=None):
        when(cond, lambda: remote(name, src, dst, device).start())
        pending[name] = cond, (name, src, dst, device)

    def left(name):
        cond, args = pending.pop(name)
        when(cond, lambda: remote(*args).wait_send())

    def arrived(name, dst):
        remote(name, dst, dst, to_c).wait_recv()

    local_count = [0]

    def local_copy(src, dst):
        at = local_count[0]
        local_count[0] += 1
        return pltpu.make_async_copy(taken(src), taken(dst), k.local.at[at])

    def fetch(src, dst):
        copy = local_copy(src, dst)
        copy.start()
        return copy

    stored = []

    def put(src, dst, cond=None):
        at = local_count[0]
        local_count[0] += 1

        def copy():
            return pltpu.make_async_copy(taken(src), taken(dst), k.local.at[at])

        when(cond, lambda: copy().start())
        stored.append((cond, copy))

    def add(dst, src):
        dst[...] = (dst[...].astype(F32) + src[...].astype(F32)).astype(BF)

    def chosen(rel, bit):
        return bit if rel else 1 - bit

    class Travel:
        def __init__(self, tag, own):
            self.tag, self.own, self.order = tag, own, STAGES[tag]
            self.counts = counts_of(tag)
            self.got = travelling[N.got, tag]
            self.starts = [sum(self.counts[1 : p + 1]) for p in range(len(self.order))]
            self.alive = active if tag in DOWN else holder
            self.role_at = len(self.order)
            for p, dim in enumerate(self.order):
                if dim not in scatter_of(tag):
                    self.role_at = p

        def held(self, p, i):
            return (self.own, i) if p == 0 else (self.got, self.starts[p - 1] + i)

        def leave(self, p, i):
            if p == len(self.order):
                return
            dim = self.order[p]
            ref, at = self.held(p, i)
            cond = None
            if dim in scatter_of(self.tag):
                if i >= self.counts[p] // 2:
                    return
                if p > self.role_at:
                    cond = self.alive
            else:
                cond = idle if self.tag in DOWN else lender
            post((self.tag, p, i), At(ref)[at], At(self.got)[self.starts[p] + i], to_dim[dim], cond)

        def step(self, p, i):
            at = self.starts[p] + i
            halved = self.order[p] in scatter_of(self.tag)
            ref, mine = self.held(p, i + (self.counts[p + 1] if halved else 0))

            def go():
                arrived((self.tag, p, i), At(self.got)[at])
                add(self.got.at[at], ref.at[mine])

            when(self.alive if p >= self.role_at else None, go)
            self.leave(p + 1, i)

        def last(self):
            return At(self.got)[self.starts[-1]]

    travels = {tag: Travel(tag, travelling.get((N.own, tag))) for tag in STAGES}
    steps = {}
    for tag, travel in travels.items():
        for p in range(len(travel.order)):
            for i in range(travel.counts[p + 1]):
                steps[tag, p, i] = functools.partial(travel.step, p, i)

    got_tok = fetch(k.tokens.at[0], k.tok)
    got_cot = fetch(k.cotangent.at[0], k.cot)
    barrier = pltpu.get_barrier_semaphore()
    for device in partners:
        pl.semaphore_signal(barrier, inc=1, device_id=device, device_id_type=MESH)

    position = s * span + lax.broadcasted_iota(jnp.int32, (span, 1), 0)
    starts = [np.int32(0)]
    for i in range(k.lengths.shape[1] - 1):
        starts.append(starts[-1] + k.lengths[0, i])

    def first_of(at):
        first = jnp.zeros_like(at)
        for start in starts:
            first = jnp.maximum(first, jnp.where(start <= at, start, 0))
        return first

    def flag(test):
        return jnp.where(test, 1.0, 0.0).astype(F32)

    def write_masks():
        first0, first1, first2 = (first_of(position + i) for i in range(3))
        columns = [
            flag(position < k.counts[0]),
            flag(position >= first0),
            flag(position - 1 >= first0),
            flag(position - 2 >= first0),
            flag(position >= first1),
            flag(position >= first2),
        ]
        lane = lax.broadcasted_iota(jnp.int32, (span, 128), 1)
        table = jnp.zeros((span, 128), F32)
        for i, column in enumerate(columns):
            table = jnp.where(lane == i, column, table)
        k.mask[...] = table

    def mask(i, rows=slice(None)):
        return k.mask[rows, i : i + 1]

    def gain(ref):
        return ref[...].astype(F32)

    step = 64
    passes = span // step
    part = span // 2

    def mixer_forward(win):
        got_win = [fetch(k.w_in.at[:, block(i, width)], win.at[:, block(i, width)]) for i in (0, 2, 1)]
        got_wout = fetch(k.w_out, k.wout)
        write_masks()
        got_tok.wait()

        @functools.partial(loop, passes, unroll=False)
        def _(i):
            rows = block(i, step)
            t = k.tok[rows, :].astype(F32)
            scale = lax.rsqrt(jnp.mean(t * t, axis=-1, keepdims=True) + EPSILON)
            k.sc1[rows, :] = scale
            k.nrm[rows, :] = (t * scale * gain(k.gain1)).astype(BF)

        got_cot.wait()

        @functools.partial(loop, passes, unroll=False)
        def _(i):
            rows = block(i, step)
            k.df[rows, :] = (mask(MASK_VALID, rows) * k.cot[rows, :].astype(F32)).astype(BF)

        pl.semaphore_wait(barrier, len(partners))
        post(
            N.df_z(0),
            At(k.df)[pl.ds(0, span), first_cols],
            At(k.df)[pl.ds(2 * span, span), first_cols],
            to_z,
        )
        post(N.df_c, At(k.df)[pl.ds(0, span)], At(k.df)[pl.ds(span, span)], to_c)
        got_win[0].wait()
        got_win[1].wait()

        @functools.partial(loop, width // 256)
        def _(j):
            n = k.nrm[:span, :]
            cols = block(j, 256)
            gb = dot(n, win[:, cols])
            va = dot(n, win[:, pl.ds(pl.multiple_of(2 * width + j * 256, 256), 256)])
            k.gb[:, cols] = gb.astype(BF)
            k.va[:, cols] = va.astype(BF)
            k.mix[8:, cols] = (mask(MASK_VALID) * gb * va).astype(BF).astype(F32)

        post(N.halo, At(k.mix)[pl.ds(span, 8)], k.hr, after, not_last)
        got_win[2].wait()

        @functools.partial(loop, width // 256)
        def _(j):
            cols = block(j, 256)
            c_cols = pl.ds(pl.multiple_of(width + j * 256, 256), 256)
            k.gc[:, cols] = dot(k.nrm[:span, :], win[:, c_cols])

        got_wout.wait()

    pl.run_scoped(mixer_forward, pltpu.VMEM((width, 3 * width), BF))

    @pl.when(s == 0)
    def _():
        k.mix[:8, :] = jnp.zeros((8, width), F32)

    @pl.when(not_first)
    def _():
        arrived(N.halo, k.hr)
        k.mix[:8, :] = k.hr[...]

    def tap(i, cols):
        return k.taps[i : i + 1, cols].astype(F32)

    def conv_of(cols):
        return (
            tap(0, cols) * mask(MASK_S0) * k.mix[8 : 8 + span, cols]
            + tap(1, cols) * mask(MASK_S1) * k.mix[7 : 7 + span, cols]
            + tap(2, cols) * mask(MASK_S2) * k.mix[6 : 6 + span, cols]
        )

    @functools.partial(loop, width // 256, unroll=False)
    def _(j):
        cols = block(j, 256)
        k.gat[:span, cols] = (mask(MASK_VALID) * k.gc[:, cols] * conv_of(cols)).astype(BF)

    @functools.partial(loop, width // 256)
    def _(j):
        cols = block(j, 256)
        k.res[:, cols] = k.tok[:, cols].astype(F32) + dot(k.gat[:span, :], k.wout[:, cols])

    for i in range(2):

        @functools.partial(loop, passes // 2, unroll=False)
        def _(j):
            rows = block(i * (passes // 2) + j, step)
            v = k.res[rows, :]
            scale = lax.rsqrt(jnp.mean(v * v, axis=-1, keepdims=True) + EPSILON)
            k.sc2[rows, :] = scale
            k.n2[rows, :] = (v * scale * gain(k.gain2)).astype(BF)

        here = pl.ds(i * part, part)
        post(N.n2_z(i), At(k.n2)[here], At(k.n2)[pl.ds(2 * span + i * part, part)], to_z)
    post(N.n2_c, At(k.n2)[pl.ds(0, span)], At(k.n2)[pl.ds(span, span)], to_c)
    post(
        N.df_z(1),
        At(k.df)[pl.ds(0, span), last_cols],
        At(k.df)[pl.ds(2 * span, span), last_cols],
        to_z,
    )
    post(N.nrm_c, At(k.nrm)[pl.ds(0, span)], At(k.nrm)[pl.ds(span, span)], to_c)
    post(N.gat_c, At(k.gat)[pl.ds(0, span)], At(k.gat)[pl.ds(span, span)], to_c)

    z_rows, t_rows = pl.ds(2 * span, span), pl.ds(3 * span, span)
    z_parts = [pl.ds(2 * span + i * part, part) for i in range(2)]
    t_parts = [pl.ds(3 * span + i * part, part) for i in range(2)]
    half_cols = (first_cols, last_cols)

    def pass_df(i):
        arrived(N.df_z(i), At(k.df)[z_rows, half_cols[i]])
        post(N.df_t(i), At(k.df)[z_rows, half_cols[i]], At(k.df)[t_rows, half_cols[i]], to_c)

    def pass_n2(i):
        arrived(N.n2_z(i), At(k.n2)[z_parts[i]])
        post(N.n2_t(i), At(k.n2)[z_parts[i]], At(k.n2)[t_parts[i]], to_c)

    for i in range(2):
        steps[N.tdf(i)] = functools.partial(pass_df, i)
        steps[N.tn(i)] = functools.partial(pass_n2, i)

    def down_last(i):
        got = travels[DOWN[i]].last()
        post(N.rd4(i), got, k.rd4, targets[i], gives[i])
        put(got, k.g_down, home[i])

    def down_take():
        for i in range(2):
            when(away_at[i], lambda: arrived(N.rd4(i), k.rd4))
        put(k.rd4, k.g_down, away)

    def wide_last(tag):
        mine, out = (k.rg4, k.g_gate) if tag == N.g else (k.ru4, k.g_up)
        for core in range(2):
            got = travels[(GATE if tag == N.g else UP)[core]].last()
            post((tag, core), got, mine, to_c, holds[1 - core])
            put(got, out, holds[core])

    lends = [jnp.logical_and(lender, c == i) for i in range(2)]

    def wide_take(tag):
        mine, out = (k.rg4, k.g_gate) if tag == N.g else (k.ru4, k.g_up)
        for core in range(2):
            when(lends[core], lambda: arrived((tag, core), mine))
        put(mine, out, lender)

    for i in range(2):
        steps[N.dl(i)] = functools.partial(down_last, i)
    steps[N.dt] = down_take
    for tag in (N.g, N.u):
        steps[N.w3(tag)] = functools.partial(wide_last, tag)
        steps[N.w4(tag)] = functools.partial(wide_take, tag)

    def small_rows():
        total = k.sg[:, small_cols[0]]
        for i in range(1, 8):
            arrived(N.sa(i), At(k.sa)[i - 1])
            total = total + k.sa[i - 1]
        k.ss[...] = total
        for i in range(1, 4):
            post(N.sb(i), k.ss, At(k.sb)[i - 1], (r, seq_peers[i]))

    def small_seq():
        total = k.ss[...]
        for i in range(1, 4):
            arrived(N.sb(i), At(k.sb)[i - 1])
            left(N.sb(i))
            total = total + k.sb[i - 1]
        k.ss[...] = total
        put(k.ss, k.small)

    steps[N.sg(0)], steps[N.sg(1)] = small_rows, small_seq

    def layer_output():
        arrived(N.fz, k.fz)

        @functools.partial(loop, passes, unroll=False)
        def _(i):
            rows = block(i, step)
            valid = mask(MASK_VALID, rows)
            k.cot[rows, :] = (k.loa[rows, :] + valid * k.fz[rows, :].astype(F32)).astype(BF)

        put(k.cot, k.layer_out.at[0])

    steps[N.lo] = layer_output
    feed_end = 1 + max(i for i, name in enumerate(ORDER) if name[0] in FEED)

    def feed_forward(wg, wu, wd, hid, dg, du):
        q = 2 * c + z0
        got_wg = fetch(k.w_gate.at[:, block(q, quarter)], wg)
        got_wu = fetch(k.w_up.at[:, block(q, quarter)], wu)
        got_wd = fetch(k.w_down.at[block(q, quarter), :], wd)

        def tiles(body, unroll):
            loop(quarter // 256, lambda j: body(block(j, 256)), unroll)
            if quarter % 256:
                body(pl.ds(quarter - quarter % 256, quarter % 256))

        def expand(rows, unroll):
            def tile(cols):
                n = k.n2[rows, :]
                g = dot(n, wg[:, cols])
                u = dot(n, wu[:, cols])
                sig = jax.nn.sigmoid(g)
                silu = g * sig
                hid[rows, cols] = (silu * u).astype(BF)
                dg[rows, cols] = (u * sig * (1.0 + g * (1.0 - sig))).astype(BF)
                du[rows, cols] = silu.astype(BF)

            tiles(tile, unroll)

        def retreat(slot, unroll):
            rows = pl.ds(slot * span, span)

            def tile(cols):
                d = dot_nt(k.df[rows, :], wd[cols, :])
                dg[rows, cols] = (d * dg[rows, cols].astype(F32)).astype(BF)
                du[rows, cols] = (d * du[rows, cols].astype(F32)).astype(BF)

            tiles(tile, unroll)

        def back(slot, ref, plus, unroll):
            rows = pl.ds(slot * span, span)

            @functools.partial(loop, width // 256, unroll=unroll)
            def _(j):
                cols = block(j, 256)
                value = dot_nt(dg[rows, :], wg[cols, :]) + dot_nt(du[rows, :], wu[cols, :])
                if plus is not None:
                    value = value + plus[:, cols].astype(F32)
                ref[:, cols] = value.astype(ref.dtype)

        def forth(slot, store):
            rows = pl.ds(slot * span, span)

            @functools.partial(loop, width // 256, unroll=False)
            def _(j):
                cols = block(j, 256)
                store(cols, dot(hid[rows, :], wd[:, cols]))

        own = steps

        def ex0():
            got_wg.wait()
            got_wu.wait()
            expand(pl.ds(0, span), False)

        def ex1():
            arrived(N.n2_c, At(k.n2)[pl.ds(span, span)])
            expand(pl.ds(span, span), False)

        def re0():
            got_wd.wait()
            retreat(0, False)

        def re1():
            arrived(N.df_c, At(k.df)[pl.ds(span, span)])
            retreat(1, False)

        def bk1():
            back(1, k.ps.at[0], None, False)
            post(N.pr0, At(k.ps)[0], At(k.pr)[0], to_c)

        def bk0():
            arrived(N.pr0, At(k.pr)[0])
            back(0, k.own, k.pr.at[0], False)

        def ex2(i):
            expand(z_parts[i], True)

        def ex3(i):
            arrived(N.n2_t(i), At(k.n2)[t_parts[i]])
            expand(t_parts[i], True)

        def bk3():
            back(3, k.ps.at[1], None, True)
            post(N.pr1, At(k.ps)[1], At(k.pr)[1], to_c)

        def bk2():
            arrived(N.pr1, At(k.pr)[1])
            back(2, k.pr.at[1], k.pr.at[1], True)
            post(N.pz, At(k.pr)[1], k.pz, to_z)

        def wide_grad(tag, core, u, grad):
            travel = travels[tag]
            rel = unit_bits(tag, u)
            rho = 4 * chosen(rel[N.y], y) + 2 * chosen(rel[N.x], x) + core
            travel.own[u] = dot_tn(k.n2[:, block(rho, slim)], grad[...]).astype(BF)
            travel.leave(0, u)

        def to_ref(ref, plus=None):
            def store(cols, value):
                if plus is not None:
                    value = value + plus[:, cols].astype(F32)
                ref[:, cols] = value.astype(ref.dtype)

            return store

        def fo1():
            left(N.pr0)
            forth(1, to_ref(k.ps.at[0]))
            post(N.fr0, At(k.ps)[0], At(k.fr)[0], to_c)

        def fo3():
            left(N.pr1)
            forth(3, to_ref(k.ps.at[1]))
            post(N.fr1, At(k.ps)[1], At(k.fr)[1], to_c)

        def fo2():
            arrived(N.fr1, At(k.fr)[1])
            forth(2, to_ref(k.fr.at[1], k.fr.at[1]))
            post(N.fz, At(k.fr)[1], k.fz, to_z)

        def fo0():
            arrived(N.fr0, At(k.fr)[0])

            def store(cols, value):
                value = value + k.fr[0, :, cols].astype(F32)
                k.loa[:, cols] = k.res[:, cols] + mask(MASK_VALID) * value

            forth(0, store)

        own.update({N.ex(0): ex0, N.ex(1): ex1, N.re(0): re0, N.re(1): re1})
        own.update({N.bk(0): bk0, N.bk(1): bk1, N.bk(2): bk2, N.bk(3): bk3})
        own.update({N.fo(0): fo0, N.fo(1): fo1, N.fo(2): fo2, N.fo(3): fo3})
        own[N.re(2)] = functools.partial(retreat, 2, True)

        def re3():
            arrived_df1()
            retreat(3, True)

        seen = []

        def arrived_df1():
            if not seen:
                seen.append(1)
                arrived(N.df_t(1), At(k.df)[t_rows, half_cols[1]])

        def dn1():
            arrived_df1()
            grads_down(1)

        def dn0():
            arrived(N.df_t(0), At(k.df)[t_rows, half_cols[0]])
            grads_down(0)

        def grads_down(rel_w):
            for rel_x in range(2):
                sigma = 2 * chosen(rel_w, z1) + chosen(rel_x, x)
                value = dot_tn(hid[...], k.df[:, block(sigma, side)])
                for i, tag in enumerate(DOWN):
                    u = unit_index(tag, {N.x: rel_x, N.z1: rel_w})
                    travels[tag].own[u] = value[i * tall : (i + 1) * tall].astype(BF)
                    travels[tag].leave(0, u)

        own.update({N.re(3): re3, N.dn(0): dn0, N.dn(1): dn1})
        for i in range(2):
            own[N.ex(2, i)] = functools.partial(ex2, i)
            own[N.ex(3, i)] = functools.partial(ex3, i)
            for u in range(4):
                own[N.gg(i, u)] = functools.partial(wide_grad, GATE[i], i, u, dg)
                own[N.uu(i, u)] = functools.partial(wide_grad, UP[i], i, u, du)
        for name in ORDER[:feed_end]:
            own[name]()

    pl.run_scoped(
        feed_forward,
        pltpu.VMEM((width, quarter), BF),
        pltpu.VMEM((width, quarter), BF),
        pltpu.VMEM((quarter, width), BF),
        pltpu.VMEM((4 * span, quarter), BF),
        pltpu.VMEM((4 * span, quarter), BF),
        pltpu.VMEM((4 * span, quarter), BF),
    )

    def mixer_backward(win, gm):
        got_win = fetch(k.w_in, win)
        share = slim // len(MIXED)
        for h, tag in enumerate(MIXED):
            travels[tag].own = gm.at[h]

        def mb1():
            arrived(N.pz, k.pz)
            k.sg[...] = jnp.zeros((8, width), F32)

            @functools.partial(loop, passes, unroll=False)
            def _(i):
                rows = block(i, step)
                d = k.own[rows, :] + k.pz[rows, :].astype(F32)
                v = k.res[rows, :]
                scale = k.sc2[rows, :]
                scaled = gain(k.gain2) * d
                k.sg[1:2, :] = k.sg[1:2, :] + jnp.sum(d * v * scale, axis=0, keepdims=True)
                d = (
                    k.cot[rows, :].astype(F32)
                    + scale * scaled
                    - v * (scale * scale * scale) * jnp.mean(scaled * v, axis=-1, keepdims=True)
                )
                k.own[rows, :] = d
                k.dmx[rows, :] = d.astype(BF)

            post(N.dmx_c, At(k.dmx)[pl.ds(0, span)], At(k.dmx)[pl.ds(span, span)], to_c)

        def mb2():
            @functools.partial(loop, width // 256)
            def _(j):
                cols = block(j, 256)
                d = dot_nt(k.dmx[:span, :], k.wout[cols, :])
                valid = mask(MASK_VALID)
                k.dc[:span, cols] = (valid * k.gc[:, cols] * d).astype(BF).astype(F32)
                c_cols = pl.ds(pl.multiple_of(width + j * 256, 256), 256)
                k.dpj[:span, c_cols] = (valid * conv_of(cols) * d).astype(BF)

            post(N.halo2, At(k.dc)[pl.ds(0, 8)], k.hr2, before, not_first)

        def mb3():
            @pl.when(s == 3)
            def _():
                k.dc[span:, :] = jnp.zeros((8, width), F32)

            @pl.when(not_last)
            def _():
                arrived(N.halo2, k.hr2)
                k.dc[span:, :] = k.hr2[...]

            @functools.partial(loop, width // 256, unroll=False)
            def _(j):
                cols = block(j, 256)
                d0 = k.dc[:span, cols]
                d = (
                    tap(0, cols) * mask(MASK_S0) * d0
                    + tap(1, cols) * mask(MASK_N1) * k.dc[1 : 1 + span, cols]
                    + tap(2, cols) * mask(MASK_N2) * k.dc[2 : 2 + span, cols]
                )
                valid = mask(MASK_VALID)
                k.dpj[:span, cols] = (valid * k.va[:, cols].astype(F32) * d).astype(BF)
                x_cols = pl.ds(pl.multiple_of(2 * width + j * 256, 256), 256)
                k.dpj[:span, x_cols] = (valid * k.gb[:, cols].astype(F32) * d).astype(BF)
                for i, m in ((0, MASK_S0), (1, MASK_S1), (2, MASK_S2)):
                    k.sg[2 + i : 3 + i, cols] = jnp.sum(
                        d0 * mask(m) * k.mix[8 - i : 8 - i + span, cols], axis=0, keepdims=True
                    )

            post(N.dpj_c, At(k.dpj)[pl.ds(0, span)], At(k.dpj)[pl.ds(span, span)], to_c)

        def mb4():
            got_win.wait()

            @functools.partial(loop, width // 256)
            def _(j):
                cols = block(j, 256)
                k.gc[:, cols] = dot_nt(k.dpj[:span, :], win[cols, :])

            @functools.partial(loop, passes, unroll=False)
            def _(i):
                rows = block(i, step)
                d = k.gc[rows, :]
                t = k.tok[rows, :].astype(F32)
                scale = k.sc1[rows, :]
                scaled = gain(k.gain1) * d
                k.sg[0:1, :] = k.sg[0:1, :] + jnp.sum(d * t * scale, axis=0, keepdims=True)
                d = (
                    k.own[rows, :]
                    + scale * scaled
                    - t * (scale * scale * scale) * jnp.mean(scaled * t, axis=-1, keepdims=True)
                )
                k.tok[rows, :] = d.astype(BF)

            put(k.tok, k.grad_tokens.at[0])
            for i in range(1, 8):
                post(N.sa(i), At(k.sg)[:, small_cols[i]], At(k.sa)[i - 1], (row_peers[i], s))
            for name, ref in (
                (N.nrm_c, k.nrm),
                (N.gat_c, k.gat),
                (N.dmx_c, k.dmx),
                (N.dpj_c, k.dpj),
            ):
                arrived(name, At(ref)[pl.ds(span, span)])

        def mg(rel_x, rel_y):
            rho = 4 * chosen(rel_y, y) + 2 * chosen(rel_x, x) + c
            rows = block(rho, slim)
            leaving = []
            for a in range(2):
                for b in range(2):
                    sigma = 2 * chosen(b, z1) + chosen(a, z0)
                    first = dot_tn(k.nrm[:, rows], k.dpj[:, block(sigma, wide)])
                    second = dot_tn(k.gat[:, rows], k.dmx[:, block(sigma, side)])
                    for h, tag in enumerate(MIXED):
                        u = unit_index(tag, {N.x: rel_x, N.y: rel_y, N.z0: a, N.z1: b})
                        here = slice(h * share, (h + 1) * share)
                        gm[h, u, :, :wide] = first[here].astype(BF)
                        gm[h, u, :, wide:] = second[here].astype(BF)
                        leaving.append((u, tag, h))
            for u, tag, h in sorted(leaving):
                leave_mixed(tag, h, u)

        def leave_mixed(tag, h, u):
            travel = travels[tag]
            if u < travel.counts[0] // 2:
                dst = At(travel.got)[travel.starts[0] + u]
                post((tag, 0, u), At(gm)[h, u], dst, to_dim[travel.order[0]])

        def finish_mixed():
            for h, tag in enumerate(MIXED):
                got, at = travels[tag].got, travels[tag].starts[-1]
                rows = pl.ds(h * share, share)
                put(At(got)[at, :, pl.ds(0, wide)], At(k.g_in)[rows, :])
                put(At(got)[at, :, pl.ds(wide, width - wide)], At(k.g_out)[rows, :])

        steps.update({N.mb(1): mb1, N.mb(2): mb2, N.mb(3): mb3, N.mb(4): mb4})
        for a in range(2):
            for b in range(2):
                steps[N.mg(a, b)] = functools.partial(mg, a, b)
        for name in ORDER[feed_end:]:
            steps[name]()
        finish_mixed()
        for name in list(pending):
            left(name)
        for cond, copy in stored:
            when(cond, lambda: copy().wait())

    pl.run_scoped(
        mixer_backward,
        pltpu.VMEM((width, 3 * width), BF),
        pltpu.VMEM((len(MIXED), 16, slim // len(MIXED), width), BF),
    )


def finish_kernel(n, *refs):
    sources, small = refs[:n], refs[n]
    targets, smalls = refs[n + 1 : 2 * n + 1], refs[2 * n + 1 : 2 * n + 4]
    rest = refs[2 * n + 4 :]
    held, wide, gets, puts = rest[:n], rest[n : 2 * n], rest[2 * n], rest[2 * n + 1]
    copies = [pltpu.make_async_copy(sources[i], held[i], gets.at[i]) for i in range(n)]
    for copy in copies:
        copy.start()
    s = lax.axis_index("seq")
    piece = smalls[0].shape[-1]
    value = jnp.zeros((8, piece), F32)
    for i in range(small.shape[1] // piece):
        value = jnp.where(s == i, small[:, i * piece : (i + 1) * piece], value)
    smalls[0][...] = value[0:1]
    smalls[1][...] = value[2:5]
    smalls[2][...] = value[1:2]
    out = []
    for i in range(n):
        copies[i].wait()
        ref = held[i]
        if sources[i].dtype != targets[i].dtype:
            rows = 64

            @functools.partial(loop, ref.shape[0] // rows, unroll=False)
            def _(j):
                here = block(j, rows)
                wide[i][here, :] = ref[here, :].astype(F32)

            ref = wide[i]
        copy = pltpu.make_async_copy(ref, targets[i], puts.at[i])
        copy.start()
        out.append(copy)
    for copy in out:
        copy.wait()


def fused(
    tokens,
    doc_lengths,
    valid_counts,
    norm_in,
    w_in,
    w_conv,
    w_out,
    norm_ffn,
    w_gate,
    w_up,
    w_down,
    cotangent,
):
    _, span, width = tokens.shape
    ff = w_gate.shape[1]
    rows, seq = lax.axis_size("rows"), lax.axis_size("seq")
    scratch = scratch_list(span, width, ff, rows, seq)
    anywhere = pl.BlockSpec(memory_space=pl.ANY)
    scalars = pl.BlockSpec(memory_space=pltpu.SMEM)
    vectors = pl.BlockSpec(memory_space=pltpu.VMEM)
    grads = [
        (width // rows, 3 * width // seq),
        (width // rows, width // seq),
        (width // rows, ff // seq),
        (width // rows, ff // seq),
        (ff // rows, width // seq),
    ]
    *outs, small = pl.pallas_call(
        functools.partial(layer_kernel, OPERANDS + list(scratch)),
        out_shape=[jax.ShapeDtypeStruct((1, span, width), BF)] * 2
        + [jax.ShapeDtypeStruct(shape, BF) for shape in grads]
        + [jax.ShapeDtypeStruct((8, width // rows), F32)],
        in_specs=[scalars] * 2 + [anywhere] * 2 + [vectors] * 3 + [anywhere] * 5,
        out_specs=[anywhere] * 8,
        scratch_shapes=list(scratch.values()),
        compiler_params=pltpu.CompilerParams(
            collective_id=0, has_side_effects=True, vmem_limit_bytes=67043328
        ),
        name="layer",
    )(
        doc_lengths,
        valid_counts,
        tokens,
        cotangent,
        norm_in[None],
        w_conv,
        norm_ffn[None],
        w_in,
        w_out,
        w_gate,
        w_up,
        w_down,
    )
    piece = width // (rows * seq)
    n = len(outs)
    held = [(1, span, width)] * 2 + grads
    *final, first, taps, second = pl.pallas_call(
        functools.partial(finish_kernel, n),
        out_shape=[jax.ShapeDtypeStruct((1, span, width), BF)] * 2
        + [jax.ShapeDtypeStruct(shape, F32) for shape in grads]
        + [jax.ShapeDtypeStruct((i, piece), F32) for i in (1, 3, 1)],
        in_specs=[anywhere] * n + [vectors],
        out_specs=[anywhere] * n + [vectors] * 3,
        scratch_shapes=[pltpu.VMEM(shape, BF) for shape in held]
        + [pltpu.VMEM(shape if i > 1 else (8, 128), F32) for i, shape in enumerate(held)]
        + [pltpu.SemaphoreType.DMA((n,))] * 2,
        name="finish",
    )(*outs, small)
    layer_out, grad_tokens, g_in, g_out, g_gate, g_up, g_down = final
    return (
        layer_out,
        grad_tokens,
        first[0],
        g_in,
        taps,
        g_out,
        second[0],
        g_gate,
        g_up,
        g_down,
    )


def solution(mesh):
    placed = (
        P("rows", "seq", None),
        P("rows", None),
        P("rows"),
        P(),
        P(),
        P(),
        P(),
        P(),
        P(),
        P(),
        P(),
        P("rows", "seq", None),
    )
    paired = mesh.shape["rows"] == 8 and mesh.shape["seq"] == 4
    return jax.shard_map(
        fused if paired else plain,
        mesh=mesh,
        in_specs=placed,
        out_specs=(
            P("rows", "seq", None),
            P("rows", "seq", None),
            P(("rows", "seq")),
            P("rows", "seq"),
            P(None, ("rows", "seq")),
            P("rows", "seq"),
            P(("rows", "seq")),
            P("rows", "seq"),
            P("rows", "seq"),
            P("rows", "seq"),
        ),
        check_vma=False,
    )
```

```python
import functools

import jax
import jax.numpy as jnp
import numpy as np
from jax import lax
from jax.experimental import pallas as pl
from jax.experimental.pallas import tpu as pltpu
from jax.sharding import PartitionSpec as P

EPSILON = 1e-05
BF = jnp.bfloat16
F32 = jnp.float32
MESH = pl.DeviceIdType.MESH


def passed_along(value, axis, steps):
    count = lax.axis_size(axis)
    first, last = (max(0, -steps), min(count, count - steps))
    return lax.ppermute(value, axis, [(source, source + steps) for source in range(first, last)])


def rms_scale(values):
    return lax.rsqrt(jnp.mean(values * values, axis=-1, keepdims=True) + EPSILON)


def doc_masks(lengths, positions):
    starts = jnp.cumsum(lengths) - lengths
    within = starts[None, :] <= positions[:, None]
    first = jnp.max(jnp.where(within, starts[None, :], 0), axis=1)
    return [(positions - offset >= first).astype(jnp.float32)[:, None] for offset in range(3)]


def weight_grad(left, right):
    return jnp.einsum("ta,tb->ab", left, right, preferred_element_type=jnp.float32)


def back_product(grad, weight):
    return jnp.einsum("tb,ab->ta", grad, weight, preferred_element_type=jnp.float32)


def scattered(value, row_dim, seq_dim):
    part = lax.psum_scatter(value.astype(BF), "rows", scatter_dimension=row_dim, tiled=True)
    part = lax.psum_scatter(part, "seq", scatter_dimension=seq_dim, tiled=True)
    return part.astype(F32)


def plain(
    tokens,
    doc_lengths,
    valid_counts,
    norm_in,
    w_in,
    w_conv,
    w_out,
    norm_ffn,
    w_gate,
    w_up,
    w_down,
    cotangent,
):
    inputs = tokens[0].astype(jnp.float32)
    span = inputs.shape[0]
    width = inputs.shape[1]
    start_pos = lax.axis_index("seq") * span
    positions = start_pos + jnp.arange(span + 2, dtype=jnp.int32)
    valid = (positions[:span] < valid_counts[0]).astype(jnp.float32)[:, None]
    same = doc_masks(doc_lengths[0], positions)
    taps = w_conv.astype(jnp.float32)
    gain_in = norm_in.astype(jnp.float32)
    gain_ffn = norm_ffn.astype(jnp.float32)
    scale1 = rms_scale(inputs)
    normed = (inputs * scale1 * gain_in).astype(jnp.bfloat16)
    proj = jnp.dot(normed, w_in, preferred_element_type=jnp.float32)
    gate_b = proj[:, :width]
    gate_c = proj[:, width : 2 * width]
    values = proj[:, 2 * width :]
    mixed_in = (valid * gate_b * values).astype(jnp.bfloat16)
    tail_rows = passed_along(mixed_in[span - 2 :], "seq", 1)
    padded = jnp.concatenate([tail_rows, mixed_in], axis=0).astype(jnp.float32)
    conv = jnp.zeros((span, width), jnp.float32)
    for offset in range(3):
        conv = conv + taps[offset] * same[offset][:span] * padded[2 - offset : 2 - offset + span]
    gated = (valid * gate_c * conv).astype(jnp.bfloat16)
    mixer_out = jnp.dot(gated, w_out, preferred_element_type=jnp.float32)
    resid = inputs + mixer_out
    scale2 = rms_scale(resid)
    normed2 = (resid * scale2 * gain_ffn).astype(jnp.bfloat16)
    gate_act = jnp.dot(normed2, w_gate, preferred_element_type=jnp.float32)
    up_act = jnp.dot(normed2, w_up, preferred_element_type=jnp.float32)
    sigmoid_gate = jax.nn.sigmoid(gate_act)
    silu_gate = gate_act * sigmoid_gate
    hidden = (silu_gate * up_act).astype(jnp.bfloat16)
    ffn_out = jnp.dot(hidden, w_down, preferred_element_type=jnp.float32)
    layer_out = (resid + valid * ffn_out).astype(jnp.bfloat16)
    grad_out = cotangent[0].astype(jnp.float32)
    d_ffn = (valid * grad_out).astype(jnp.bfloat16)
    grad_w_down = weight_grad(hidden, d_ffn)
    d_hidden = back_product(d_ffn, w_down)
    d_gate = (d_hidden * up_act * sigmoid_gate * (1.0 + gate_act * (1.0 - sigmoid_gate))).astype(
        jnp.bfloat16
    )
    d_up = (d_hidden * silu_gate).astype(jnp.bfloat16)
    grad_w_gate = weight_grad(normed2, d_gate)
    grad_w_up = weight_grad(normed2, d_up)
    d_normed2 = back_product(d_gate, w_gate) + back_product(d_up, w_up)
    grad_norm_ffn = jnp.sum(d_normed2 * resid * scale2, axis=0)
    scaled_ffn = gain_ffn * d_normed2
    d_resid = (
        grad_out
        + scale2 * scaled_ffn
        - resid * scale2**3 * jnp.mean(scaled_ffn * resid, axis=-1, keepdims=True)
    )
    d_mixer = d_resid.astype(jnp.bfloat16)
    grad_w_out = weight_grad(gated, d_mixer)
    d_gated = back_product(d_mixer, w_out)
    d_conv = (valid * gate_c * d_gated).astype(jnp.bfloat16)
    d_gate_c = valid * conv * d_gated
    head_rows = passed_along(d_conv[:2], "seq", -1)
    extended = jnp.concatenate([d_conv, head_rows], axis=0).astype(jnp.float32)
    d_mixed = jnp.zeros((span, width), jnp.float32)
    conv_rows = []
    for offset in range(3):
        d_mixed = (
            d_mixed
            + taps[offset] * same[offset][offset : offset + span] * extended[offset : offset + span]
        )
        conv_rows.append(
            jnp.sum(
                extended[:span] * same[offset][:span] * padded[2 - offset : 2 - offset + span],
                axis=0,
            )
        )
    grad_w_conv = jnp.stack(conv_rows, axis=0)
    d_proj = jnp.concatenate(
        [valid * values * d_mixed, d_gate_c, valid * gate_b * d_mixed], axis=1
    ).astype(jnp.bfloat16)
    grad_w_in = weight_grad(normed, d_proj)
    d_normed = back_product(d_proj, w_in)
    grad_norm_in = jnp.sum(d_normed * inputs * scale1, axis=0)
    scaled_in = gain_in * d_normed
    grad_tokens = (
        d_resid
        + scale1 * scaled_in
        - inputs * scale1**3 * jnp.mean(scaled_in * inputs, axis=-1, keepdims=True)
    )
    grad_tokens = grad_tokens.astype(jnp.bfloat16)
    return (
        layer_out[None],
        grad_tokens[None],
        scattered(grad_norm_in, 0, 0),
        scattered(grad_w_in, 0, 1),
        scattered(grad_w_conv, 1, 1),
        scattered(grad_w_out, 0, 1),
        scattered(grad_norm_ffn, 0, 0),
        scattered(grad_w_gate, 0, 1),
        scattered(grad_w_up, 0, 1),
        scattered(grad_w_down, 0, 1),
    )


def dot(a, b):
    return jnp.dot(a, b, preferred_element_type=F32)


def dot_nt(a, b):
    return lax.dot_general(a, b, (((1,), (1,)), ((), ())), preferred_element_type=F32)


def dot_tn(a, b):
    return lax.dot_general(a, b, (((0,), (0,)), ((), ())), preferred_element_type=F32)


def bit_of(value, weight):
    return lax.rem(lax.div(value, np.int32(weight)), np.int32(2))


def flipped(value, weights):
    for weight in (1, 2, 4):
        if weights & weight:
            value = value + weight - 2 * weight * bit_of(value, weight)
    return value


def loop(count, body, unroll=True):
    lax.fori_loop(0, count, lambda i, carry: (body(i), carry)[1], 0, unroll=unroll)


def block(index, size):
    return pl.ds(pl.multiple_of(index * size, size), size)


class Name(str):
    def __call__(self, *index):
        return (self,) + index


class Names:
    def __getattr__(self, name):
        return Name(name)


N = Names()

STAGES = {
    N.A: (N.x, N.y, N.z1),
    N.B: (N.y, N.z1, N.x),
    N.g0: (N.y, N.x, N.z1),
    N.g1: (N.y, N.x, N.z1),
    N.u0: (N.x, N.z1, N.y),
    N.u1: (N.x, N.y, N.z1),
    N.m0: (N.y, N.x, N.z0, N.z1),
    N.m1: (N.x, N.z0, N.y, N.z1),
    N.m2: (N.z0, N.x, N.z1, N.y),
}
ORDER = [
    N.ex(0), N.ex(1), N.re(1), N.tn(0), N.bk(1), N.ex(2, 0), N.re(0), N.bk(0),
    N.tn(1), N.ex(2, 1), N.ex(3, 0), N.tdf(0), N.ex(3, 1), N.dn(0), N.go(N.A, 0, 0), N.go(N.B, 0, 0),
    N.tdf(1), N.dn(1), N.go(N.B, 0, 1), N.tdf(2), N.tdf(3), N.re(2), N.dn(2), N.go(N.A, 0, 1),
    N.go(N.B, 0, 2), N.re(3), N.B(0, 0), N.go(N.B, 1, 0), N.bk(3), N.gg(0, 0), N.go(N.g0, 0, 0), N.gg(1, 0),
    N.go(N.g1, 0, 0), N.uu(0, 0), N.go(N.u0, 0, 0), N.A(0, 0), N.go(N.A, 1, 0), N.uu(1, 0), N.go(N.u1, 0, 0), N.B(0, 1),
    N.go(N.B, 1, 1), N.dn(3), N.go(N.B, 0, 3), N.bk(2), N.gg(0, 1), N.go(N.g0, 0, 1), N.gg(1, 1), N.go(N.g1, 0, 1),
    N.B(0, 2), N.uu(0, 1), N.go(N.u0, 0, 1), N.gg(1, 2), N.gg(0, 3), N.uu(0, 2), N.uu(1, 1), N.go(N.u1, 0, 1),
    N.uu(1, 3), N.gg(0, 2), N.uu(0, 3), N.gg(1, 3), N.fo(1), N.uu(1, 2), N.fo(3), N.B(1, 0),
    N.go(N.B, 2, 0), N.u0(0, 0), N.go(N.u0, 1, 0), N.fo(2), N.u1(0, 0), N.go(N.u1, 1, 0), N.A(0, 1), N.go(N.A, 1, 1),
    N.fo(0), N.mb(1), N.mb(2), N.u0(0, 1), N.go(N.u0, 1, 1), N.g0(0, 0), N.go(N.g0, 1, 0), N.B(0, 3),
    N.g0(0, 1), N.B(1, 1), N.u1(0, 1), N.g1(0, 0), N.go(N.g1, 1, 0), N.A(1, 0), N.go(N.A, 2, 0), N.u0(1, 0),
    N.go(N.u0, 2, 0), N.mb(3), N.mb(4), N.lo, N.mg(0, 0), N.go(N.m0, 0, 0), N.go(N.m1, 0, 0), N.go(N.m2, 0, 0),
    N.go(N.m0, 0, 1), N.go(N.m1, 0, 1), N.go(N.m0, 0, 2), N.go(N.m2, 0, 2), N.go(N.m0, 0, 3), N.go(N.m1, 0, 4), N.go(N.m1, 0, 5), N.g1(0, 1),
    N.mg(0, 1), N.go(N.m2, 0, 1), N.go(N.m1, 0, 2), N.go(N.m1, 0, 3), N.go(N.m2, 0, 3), N.go(N.m1, 0, 6), N.go(N.m1, 0, 7), N.mg(1, 0),
    N.go(N.m0, 0, 4), N.go(N.m2, 0, 4), N.go(N.m0, 0, 5), N.go(N.m0, 0, 6), N.go(N.m2, 0, 6), N.go(N.m0, 0, 7), N.B(2, 0), N.dl(1),
    N.mg(1, 1), N.go(N.m2, 0, 5), N.go(N.m2, 0, 7), N.g0(1, 0), N.go(N.g0, 2, 0), N.sg(0), N.u1(1, 0), N.go(N.u1, 2, 0),
    N.A(1, 1), N.A(2, 0), N.m2(0, 6), N.g1(1, 0), N.go(N.g1, 2, 0), N.dl(0), N.m2(0, 0), N.go(N.m2, 1, 0),
    N.m1(0, 0), N.go(N.m1, 1, 0), N.u0(1, 1), N.m2(0, 4), N.m1(0, 1), N.go(N.m1, 1, 1), N.sg(1), N.m2(0, 2),
    N.go(N.m2, 1, 2), N.m2(0, 1), N.go(N.m2, 1, 1), N.m1(0, 7), N.m1(0, 4), N.m1(0, 5), N.m1(0, 2), N.go(N.m1, 1, 2),
    N.m2(0, 5), N.m2(0, 3), N.go(N.m2, 1, 3), N.m1(0, 6), N.m2(0, 7), N.m0(0, 0), N.go(N.m0, 1, 0), N.m1(0, 3),
    N.go(N.m1, 1, 3), N.u0(2, 0), N.m0(0, 1), N.go(N.m0, 1, 1), N.m0(0, 2), N.go(N.m0, 1, 2), N.u1(2, 0), N.m1(1, 1),
    N.go(N.m1, 2, 1), N.w3(N.u), N.m1(1, 0), N.go(N.m1, 2, 0), N.m2(1, 0), N.go(N.m2, 2, 0), N.m2(1, 1), N.go(N.m2, 2, 1),
    N.dt, N.m1(1, 2), N.m2(1, 3), N.g0(2, 0), N.w4(N.u), N.m0(0, 4), N.g1(2, 0), N.w3(N.g),
    N.m2(1, 2), N.m0(1, 0), N.go(N.m0, 2, 0), N.m1(1, 3), N.m0(0, 3), N.go(N.m0, 1, 3), N.m0(0, 6), N.m2(2, 0),
    N.go(N.m2, 3, 0), N.m2(2, 1), N.m0(0, 5), N.m0(1, 1), N.go(N.m0, 2, 1), N.m0(1, 2), N.m0(2, 0), N.go(N.m0, 3, 0),
    N.m0(0, 7), N.m0(1, 3), N.m2(3, 0), N.m1(2, 0), N.go(N.m1, 3, 0), N.m1(2, 1), N.w4(N.g), N.m0(2, 1),
    N.m0(3, 0), N.m1(3, 0),
]
FEED = (N.ex, N.re, N.bk, N.dn, N.gg, N.uu, N.fo)
EIGHTHS = {N.m0: 6, N.m1: 1, N.m2: 1}
MIXED = list(EIGHTHS)
DOWN = [N.A, N.B]
GATE = [N.g0, N.g1]
UP = [N.u0, N.u1]
N_SEM = 192
MASK_VALID, MASK_S0, MASK_S1, MASK_S2, MASK_N1, MASK_N2 = range(6)


def scatter_of(tag):
    return (N.x, N.y, N.z0, N.z1) if tag in MIXED else (N.x, N.z1) if tag in DOWN else (N.x, N.y)


def counts_of(tag):
    counts = [2 ** len(scatter_of(tag))]
    for dim in STAGES[tag]:
        counts.append(counts[-1] // 2 if dim in scatter_of(tag) else counts[-1])
    return counts


def unit_index(tag, rel):
    index = 0
    for dim in STAGES[tag]:
        if dim in scatter_of(tag):
            index = 2 * index + rel[dim]
    return index


def unit_bits(tag, index):
    dims = [dim for dim in STAGES[tag] if dim in scatter_of(tag)]
    return {dim: (index >> (len(dims) - 1 - i)) & 1 for i, dim in enumerate(dims)}


def unit_shape(tag, width, ff, rows, seq):
    if tag in DOWN:
        return ff // rows, width // seq
    if tag in MIXED:
        return width // rows * EIGHTHS[tag] // 8, width
    return width // rows, ff // 4


def scratch_list(span, width, ff, rows, seq):
    group = 4 * span
    shapes = dict(
        tok=pltpu.VMEM((span, width), BF),
        cot=pltpu.VMEM((span, width), BF),
        wout=pltpu.VMEM((width, width), BF),
        nrm=pltpu.VMEM((2 * span, width), BF),
        gat=pltpu.VMEM((2 * span, width), BF),
        dmx=pltpu.VMEM((2 * span, width), BF),
        dpj=pltpu.VMEM((2 * span, 3 * width), BF),
        gb=pltpu.VMEM((span, width), BF),
        va=pltpu.VMEM((span, width), BF),
        gc=pltpu.VMEM((span, width), F32),
        mix=pltpu.VMEM((span + 8, width), F32),
        dc=pltpu.VMEM((span + 8, width), F32),
        res=pltpu.VMEM((span, width), F32),
        own=pltpu.VMEM((span, width), F32),
        loa=pltpu.VMEM((span, width), F32),
        mask=pltpu.VMEM((span, 128), F32),
        sc1=pltpu.VMEM((span, 1), F32),
        sc2=pltpu.VMEM((span, 1), F32),
        n2=pltpu.VMEM((group, width), BF),
        df=pltpu.VMEM((group, width), BF),
        hr=pltpu.VMEM((8, width), F32),
        hr2=pltpu.VMEM((8, width), F32),
        ps=pltpu.VMEM((2, span, width), BF),
        pr=pltpu.VMEM((2, span, width), BF),
        pz=pltpu.VMEM((span, width), BF),
        fr=pltpu.VMEM((2, span, width), BF),
        fz=pltpu.VMEM((span, width), BF),
        sg=pltpu.VMEM((8, width), F32),
        sa=pltpu.VMEM((rows - 1, 8, width // rows), F32),
        ss=pltpu.VMEM((8, width // rows), F32),
        sb=pltpu.VMEM((seq - 1, 8, width // rows), F32),
        rd4=pltpu.VMEM(unit_shape(N.A, width, ff, rows, seq), BF),
        rg4=pltpu.VMEM(unit_shape(N.g0, width, ff, rows, seq), BF),
        ru4=pltpu.VMEM(unit_shape(N.u0, width, ff, rows, seq), BF),
        send=pltpu.SemaphoreType.DMA((N_SEM,)),
        recv=pltpu.SemaphoreType.DMA((N_SEM,)),
        local=pltpu.SemaphoreType.DMA((32,)),
    )
    for tag in STAGES:
        unit = unit_shape(tag, width, ff, rows, seq)
        counts = counts_of(tag)
        if tag not in MIXED:
            shapes[N.own, tag] = pltpu.VMEM((counts[0],) + unit, BF)
        shapes[N.got, tag] = pltpu.VMEM((sum(counts[1:]),) + unit, BF)
    return shapes


OPERANDS = [
    N.lengths,
    N.counts,
    N.tokens,
    N.cotangent,
    N.gain1,
    N.taps,
    N.gain2,
    N.w_in,
    N.w_out,
    N.w_gate,
    N.w_up,
    N.w_down,
    N.layer_out,
    N.grad_tokens,
    N.g_in,
    N.g_out,
    N.g_gate,
    N.g_up,
    N.g_down,
    N.small,
]


class Refs:
    pass


class View:
    def __init__(self, ref, index):
        self.ref, self.index = ref, index

    def take(self):
        return self.ref.at[self.index]


class At:
    def __init__(self, ref):
        self.ref = ref

    def __getitem__(self, index):
        return View(self.ref, index)


def taken(ref):
    return ref.take() if isinstance(ref, View) else ref


def layer_kernel(names, *refs):
    k = Refs()
    travelling = {}
    for name, ref in zip(names, refs):
        if isinstance(name, tuple):
            travelling[name] = ref
        else:
            setattr(k, name, ref)
    span, width = k.tok.shape
    slim, quarter = k.rg4.shape
    tall, side = k.rd4.shape
    wide = 3 * width // 4

    r = lax.axis_index("rows")
    s = lax.axis_index("seq")
    c, x, y = bit_of(r, 1), bit_of(r, 2), bit_of(r, 4)
    z0, z1 = bit_of(s, 1), bit_of(s, 2)
    row_peers = [flipped(r, i) for i in range(8)]
    seq_peers = [flipped(s, i) for i in range(4)]
    to_c = (row_peers[1], s)
    to_z = (r, seq_peers[1])
    to_dim = {
        N.x: (row_peers[2], s),
        N.y: (row_peers[4], s),
        N.z0: to_z,
        N.z1: (r, seq_peers[2]),
    }
    partners = [(row, s) for row in row_peers[1:]] + [(r, seq) for seq in seq_peers[1:]]
    partners += [(row_peers[2], seq_peers[1]), (row_peers[3], seq_peers[1])]
    after = (r, lax.rem(s + 1, np.int32(4)))
    before = (r, lax.rem(s + 3, np.int32(4)))
    df_cols = [block(2 * (z1 if w else 1 - z1) + (x if v else 1 - x), side) for w in (0, 1) for v in (0, 1)]
    active, idle = c == y, c != y
    holder, lender = c == z1, c != z1
    not_last, not_first = s < 3, s > 0
    home = [jnp.logical_and(active, jnp.logical_and(x == z0, y == i)) for i in range(2)]
    gives = [jnp.logical_and(active, jnp.logical_not(home[i])) for i in range(2)]
    targets = [(4 * y + 2 * z0 + i, 2 * z1 + x) for i in range(2)]
    away = jnp.logical_not(jnp.logical_and(active, x == z0))
    away_at = [jnp.logical_and(away, c == i) for i in range(2)]
    core_is = [c == 0, c == 1]
    holds = [jnp.logical_and(holder, c == i) for i in range(2)]
    small_cols = [block(row, slim) for row in row_peers]

    sems = {}
    pending = {}

    def remote(name, src, dst, device):
        at = sems.setdefault(name, len(sems))
        assert at < N_SEM
        return pltpu.make_async_remote_copy(
            src_ref=taken(src),
            dst_ref=taken(dst),
            send_sem=k.send.at[at],
            recv_sem=k.recv.at[at],
            device_id=device,
            device_id_type=MESH,
        )

    def when(cond, go):
        if cond is None:
            go()
        else:
            pl.when(cond)(go)

    def post(name, src, dst, device, cond=None):
        when(cond, lambda: remote(name, src, dst, device).start())
        pending[name] = cond, (name, src, dst, device)

    def left(name):
        cond, args = pending.pop(name)
        when(cond, lambda: remote(*args).wait_send())

    def arrived(name, dst):
        remote(name, dst, dst, to_c).wait_recv()

    local_count = [0]

    def local_copy(src, dst):
        at = local_count[0]
        local_count[0] += 1
        return pltpu.make_async_copy(taken(src), taken(dst), k.local.at[at])

    def fetch(src, dst):
        copy = local_copy(src, dst)
        copy.start()
        return copy

    stored = []

    def put(src, dst, cond=None):
        at = local_count[0]
        local_count[0] += 1

        def copy():
            return pltpu.make_async_copy(taken(src), taken(dst), k.local.at[at])

        when(cond, lambda: copy().start())
        stored.append((cond, copy))

    def add(dst, src):
        dst[...] = (dst[...].astype(F32) + src[...].astype(F32)).astype(BF)

    def chosen(rel, bit):
        return bit if rel else 1 - bit

    class Travel:
        def __init__(self, tag, own):
            self.tag, self.own, self.order = tag, own, STAGES[tag]
            self.counts = counts_of(tag)
            self.got = travelling[N.got, tag]
            self.starts = [sum(self.counts[1 : p + 1]) for p in range(len(self.order))]
            self.alive = active if tag in DOWN else holder
            self.role_at = len(self.order)
            for p, dim in enumerate(self.order):
                if dim not in scatter_of(tag):
                    self.role_at = p

        def held(self, p, i):
            return (self.own, i) if p == 0 else (self.got, self.starts[p - 1] + i)

        def leave(self, p, i):
            if p == len(self.order):
                return
            dim = self.order[p]
            ref, at = self.held(p, i)
            cond = None
            if dim in scatter_of(self.tag):
                if i >= self.counts[p] // 2:
                    return
                if p > self.role_at:
                    cond = self.alive
            else:
                cond = idle if self.tag in DOWN else lender
            post((self.tag, p, i), At(ref)[at], At(self.got)[self.starts[p] + i], to_dim[dim], cond)

        def step(self, p, i):
            at = self.starts[p] + i
            halved = self.order[p] in scatter_of(self.tag)
            ref, mine = self.held(p, i + (self.counts[p + 1] if halved else 0))

            def go():
                arrived((self.tag, p, i), At(self.got)[at])
                add(self.got.at[at], ref.at[mine])

            when(self.alive if p >= self.role_at else None, go)

        def last(self):
            return At(self.got)[self.starts[-1]]

    travels = {tag: Travel(tag, travelling.get((N.own, tag))) for tag in STAGES}
    steps = {}
    for tag, travel in travels.items():
        for p in range(len(travel.order)):
            for i in range(travel.counts[p + 1]):
                steps[tag, p, i] = functools.partial(travel.step, p, i)
        for p in range(len(travel.order)):
            for i in range(travel.counts[p]):
                steps[N.go, tag, p, i] = functools.partial(travel.leave, p, i)

    got_tok = fetch(k.tokens.at[0], k.tok)
    got_cot = fetch(k.cotangent.at[0], k.cot)
    barrier = pltpu.get_barrier_semaphore()
    for device in partners:
        pl.semaphore_signal(barrier, inc=1, device_id=device, device_id_type=MESH)

    position = s * span + lax.broadcasted_iota(jnp.int32, (span, 1), 0)
    starts = [np.int32(0)]
    for i in range(k.lengths.shape[1] - 1):
        starts.append(starts[-1] + k.lengths[0, i])

    def first_of(at):
        first = jnp.zeros_like(at)
        for start in starts:
            first = jnp.maximum(first, jnp.where(start <= at, start, 0))
        return first

    def flag(test):
        return jnp.where(test, 1.0, 0.0).astype(F32)

    def write_masks():
        first0, first1, first2 = (first_of(position + i) for i in range(3))
        columns = [
            flag(position < k.counts[0]),
            flag(position >= first0),
            flag(position - 1 >= first0),
            flag(position - 2 >= first0),
            flag(position >= first1),
            flag(position >= first2),
        ]
        lane = lax.broadcasted_iota(jnp.int32, (span, 128), 1)
        table = jnp.zeros((span, 128), F32)
        for i, column in enumerate(columns):
            table = jnp.where(lane == i, column, table)
        k.mask[...] = table

    def mask(i, rows=slice(None)):
        return k.mask[rows, i : i + 1]

    def gain(ref):
        return ref[...].astype(F32).reshape(1, width)

    step = 64
    passes = span // step
    part = span // 2

    def send_df(i):
        cols = df_cols[i]
        src, dst = At(k.df)[pl.ds(0, span), cols], At(k.df)[pl.ds(2 * span, span), cols]
        post(N.df_z(i), src, dst, to_z)

    def mixer_forward(win):
        got_win = [fetch(k.w_in.at[:, block(i, width)], win.at[:, block(i, width)]) for i in (0, 2, 1)]
        got_wout = fetch(k.w_out, k.wout)
        write_masks()
        got_tok.wait()

        @functools.partial(loop, passes, unroll=False)
        def _(i):
            rows = block(i, step)
            t = k.tok[rows, :].astype(F32)
            scale = lax.rsqrt(jnp.mean(t * t, axis=-1, keepdims=True) + EPSILON)
            k.sc1[rows, :] = scale
            k.nrm[rows, :] = (t * scale * gain(k.gain1)).astype(BF)

        got_cot.wait()

        @functools.partial(loop, passes, unroll=False)
        def _(i):
            rows = block(i, step)
            k.df[rows, :] = (mask(MASK_VALID, rows) * k.cot[rows, :].astype(F32)).astype(BF)

        pl.semaphore_wait(barrier, len(partners))
        send_df(0)
        post(N.df_c, At(k.df)[pl.ds(0, span)], At(k.df)[pl.ds(span, span)], to_c)
        got_win[0].wait()
        got_win[1].wait()

        @functools.partial(loop, width // 256)
        def _(j):
            n = k.nrm[:span, :]
            cols = block(j, 256)
            gb = dot(n, win[:, cols])
            va = dot(n, win[:, pl.ds(pl.multiple_of(2 * width + j * 256, 256), 256)])
            k.gb[:, cols] = gb.astype(BF)
            k.va[:, cols] = va.astype(BF)
            k.mix[8:, cols] = (mask(MASK_VALID) * gb * va).astype(BF).astype(F32)

        post(N.halo, At(k.mix)[pl.ds(span, 8)], k.hr, after, not_last)
        got_win[2].wait()

        @functools.partial(loop, width // 256)
        def _(j):
            cols = block(j, 256)
            c_cols = pl.ds(pl.multiple_of(width + j * 256, 256), 256)
            k.gc[:, cols] = dot(k.nrm[:span, :], win[:, c_cols])

        got_wout.wait()

    pl.run_scoped(mixer_forward, pltpu.VMEM((width, 3 * width), BF))

    @pl.when(s == 0)
    def _():
        k.mix[:8, :] = jnp.zeros((8, width), F32)

    @pl.when(not_first)
    def _():
        arrived(N.halo, k.hr)
        k.mix[:8, :] = k.hr[...]

    def tap(i, cols):
        return k.taps[i : i + 1, cols].astype(F32)

    def conv_of(cols):
        return (
            tap(0, cols) * mask(MASK_S0) * k.mix[8 : 8 + span, cols]
            + tap(1, cols) * mask(MASK_S1) * k.mix[7 : 7 + span, cols]
            + tap(2, cols) * mask(MASK_S2) * k.mix[6 : 6 + span, cols]
        )

    @functools.partial(loop, width // 256, unroll=False)
    def _(j):
        cols = block(j, 256)
        k.gat[:span, cols] = (mask(MASK_VALID) * k.gc[:, cols] * conv_of(cols)).astype(BF)

    @functools.partial(loop, width // 256)
    def _(j):
        cols = block(j, 256)
        k.res[:, cols] = k.tok[:, cols].astype(F32) + dot(k.gat[:span, :], k.wout[:, cols])

    for i in range(2):

        @functools.partial(loop, passes // 2, unroll=False)
        def _(j):
            rows = block(i * (passes // 2) + j, step)
            v = k.res[rows, :]
            scale = lax.rsqrt(jnp.mean(v * v, axis=-1, keepdims=True) + EPSILON)
            k.sc2[rows, :] = scale
            k.n2[rows, :] = (v * scale * gain(k.gain2)).astype(BF)

        here = pl.ds(i * part, part)
        post(N.n2_z(i), At(k.n2)[here], At(k.n2)[pl.ds(2 * span + i * part, part)], to_z)
    post(N.n2_c, At(k.n2)[pl.ds(0, span)], At(k.n2)[pl.ds(span, span)], to_c)
    for i in (1, 2, 3):
        send_df(i)
    post(N.nrm_c, At(k.nrm)[pl.ds(0, span)], At(k.nrm)[pl.ds(span, span)], to_c)
    post(N.gat_c, At(k.gat)[pl.ds(0, span)], At(k.gat)[pl.ds(span, span)], to_c)

    z_rows, t_rows = pl.ds(2 * span, span), pl.ds(3 * span, span)
    z_parts = [pl.ds(2 * span + i * part, part) for i in range(2)]
    t_parts = [pl.ds(3 * span + i * part, part) for i in range(2)]

    def pass_df(i):
        arrived(N.df_z(i), At(k.df)[z_rows, df_cols[i]])
        post(N.df_t(i), At(k.df)[z_rows, df_cols[i]], At(k.df)[t_rows, df_cols[i]], to_c)

    def pass_n2(i):
        arrived(N.n2_z(i), At(k.n2)[z_parts[i]])
        post(N.n2_t(i), At(k.n2)[z_parts[i]], At(k.n2)[t_parts[i]], to_c)

    for i in range(4):
        steps[N.tdf(i)] = functools.partial(pass_df, i)
    for i in range(2):
        steps[N.tn(i)] = functools.partial(pass_n2, i)

    def down_last(i):
        got = travels[DOWN[i]].last()
        post(N.rd4(i), got, k.rd4, targets[i], gives[i])
        put(got, k.g_down, home[i])

    def down_take():
        for i in range(2):
            when(away_at[i], lambda: arrived(N.rd4(i), k.rd4))
        put(k.rd4, k.g_down, away)

    def wide_last(tag):
        mine, out = (k.rg4, k.g_gate) if tag == N.g else (k.ru4, k.g_up)
        for core in range(2):
            got = travels[(GATE if tag == N.g else UP)[core]].last()
            post((tag, core), got, mine, to_c, holds[1 - core])
            put(got, out, holds[core])

    lends = [jnp.logical_and(lender, c == i) for i in range(2)]

    def wide_take(tag):
        mine, out = (k.rg4, k.g_gate) if tag == N.g else (k.ru4, k.g_up)
        for core in range(2):
            when(lends[core], lambda: arrived((tag, core), mine))
        put(mine, out, lender)

    for i in range(2):
        steps[N.dl(i)] = functools.partial(down_last, i)
    steps[N.dt] = down_take
    for tag in (N.g, N.u):
        steps[N.w3(tag)] = functools.partial(wide_last, tag)
        steps[N.w4(tag)] = functools.partial(wide_take, tag)

    def small_rows():
        total = k.sg[:, small_cols[0]]
        for i in range(1, 8):
            arrived(N.sa(i), At(k.sa)[i - 1])
            total = total + k.sa[i - 1]
        k.ss[...] = total
        for i in range(1, 4):
            post(N.sb(i), k.ss, At(k.sb)[i - 1], (r, seq_peers[i]))

    def small_seq():
        total = k.ss[...]
        for i in range(1, 4):
            arrived(N.sb(i), At(k.sb)[i - 1])
            left(N.sb(i))
            total = total + k.sb[i - 1]
        k.ss[...] = total
        put(k.ss, k.small)

    steps[N.sg(0)], steps[N.sg(1)] = small_rows, small_seq

    def layer_output():
        arrived(N.fz, k.fz)

        @functools.partial(loop, passes, unroll=False)
        def _(i):
            rows = block(i, step)
            valid = mask(MASK_VALID, rows)
            k.cot[rows, :] = (k.loa[rows, :] + valid * k.fz[rows, :].astype(F32)).astype(BF)

        put(k.cot, k.layer_out.at[0])

    steps[N.lo] = layer_output
    feed_end = 1 + max(i for i, name in enumerate(ORDER) if name[0] in FEED)

    def feed_forward(wg, wu, wd, hid, dg, du):
        q = 2 * c + z0
        got_wg = fetch(k.w_gate.at[:, block(q, quarter)], wg)
        got_wu = fetch(k.w_up.at[:, block(q, quarter)], wu)
        got_wd = fetch(k.w_down.at[block(q, quarter), :], wd)

        def tiles(body, unroll):
            loop(quarter // 256, lambda j: body(block(j, 256)), unroll)
            if quarter % 256:
                body(pl.ds(quarter - quarter % 256, quarter % 256))

        def expand(rows, unroll):
            def tile(cols):
                n = k.n2[rows, :]
                g = dot(n, wg[:, cols])
                u = dot(n, wu[:, cols])
                sig = jax.nn.sigmoid(g)
                silu = g * sig
                hid[rows, cols] = (silu * u).astype(BF)
                dg[rows, cols] = (u * sig * (1.0 + g * (1.0 - sig))).astype(BF)
                du[rows, cols] = silu.astype(BF)

            tiles(tile, unroll)

        def retreat(slot, unroll):
            rows = pl.ds(slot * span, span)

            def tile(cols):
                d = dot_nt(k.df[rows, :], wd[cols, :])
                dg[rows, cols] = (d * dg[rows, cols].astype(F32)).astype(BF)
                du[rows, cols] = (d * du[rows, cols].astype(F32)).astype(BF)

            tiles(tile, unroll)

        def back(slot, ref, plus, unroll):
            rows = pl.ds(slot * span, span)

            @functools.partial(loop, width // 256, unroll=unroll)
            def _(j):
                cols = block(j, 256)
                value = dot_nt(dg[rows, :], wg[cols, :]) + dot_nt(du[rows, :], wu[cols, :])
                if plus is not None:
                    value = value + plus[:, cols].astype(F32)
                ref[:, cols] = value.astype(ref.dtype)

        def forth(slot, store):
            rows = pl.ds(slot * span, span)

            @functools.partial(loop, width // 256, unroll=False)
            def _(j):
                cols = block(j, 256)
                store(cols, dot(hid[rows, :], wd[:, cols]))

        own = steps

        waiting = [got_wd]

        def take_wd():
            while waiting:
                waiting.pop().wait()

        def ex0():
            got_wg.wait()
            got_wu.wait()
            expand(pl.ds(0, span), False)

        def ex1():
            arrived(N.n2_c, At(k.n2)[pl.ds(span, span)])
            expand(pl.ds(span, span), False)

        def re0():
            take_wd()
            retreat(0, False)

        def re1():
            take_wd()
            arrived(N.df_c, At(k.df)[pl.ds(span, span)])
            retreat(1, False)

        def bk1():
            back(1, k.ps.at[0], None, False)
            post(N.pr0, At(k.ps)[0], At(k.pr)[0], to_c)

        def bk0():
            arrived(N.pr0, At(k.pr)[0])
            back(0, k.own, k.pr.at[0], False)

        def ex2(i):
            expand(z_parts[i], True)

        def ex3(i):
            arrived(N.n2_t(i), At(k.n2)[t_parts[i]])
            expand(t_parts[i], True)

        def bk3():
            back(3, k.ps.at[1], None, True)
            post(N.pr1, At(k.ps)[1], At(k.pr)[1], to_c)

        def bk2():
            arrived(N.pr1, At(k.pr)[1])
            back(2, k.pr.at[1], k.pr.at[1], True)
            post(N.pz, At(k.pr)[1], k.pz, to_z)

        def wide_grad(tag, core, u, grad):
            travel = travels[tag]
            rel = unit_bits(tag, u)
            rho = 4 * chosen(rel[N.y], y) + 2 * chosen(rel[N.x], x) + core
            travel.own[u] = dot_tn(k.n2[:, block(rho, slim)], grad[...]).astype(BF)

        def to_ref(ref, plus=None):
            def store(cols, value):
                if plus is not None:
                    value = value + plus[:, cols].astype(F32)
                ref[:, cols] = value.astype(ref.dtype)

            return store

        def fo1():
            left(N.pr0)
            forth(1, to_ref(k.ps.at[0]))
            post(N.fr0, At(k.ps)[0], At(k.fr)[0], to_c)

        def fo3():
            left(N.pr1)
            forth(3, to_ref(k.ps.at[1]))
            post(N.fr1, At(k.ps)[1], At(k.fr)[1], to_c)

        def fo2():
            arrived(N.fr1, At(k.fr)[1])
            forth(2, to_ref(k.fr.at[1], k.fr.at[1]))
            post(N.fz, At(k.fr)[1], k.fz, to_z)

        def fo0():
            arrived(N.fr0, At(k.fr)[0])

            def store(cols, value):
                value = value + k.fr[0, :, cols].astype(F32)
                k.loa[:, cols] = k.res[:, cols] + mask(MASK_VALID) * value

            forth(0, store)

        own.update({N.ex(0): ex0, N.ex(1): ex1, N.re(0): re0, N.re(1): re1})
        own.update({N.bk(0): bk0, N.bk(1): bk1, N.bk(2): bk2, N.bk(3): bk3})
        own.update({N.fo(0): fo0, N.fo(1): fo1, N.fo(2): fo2, N.fo(3): fo3})
        own[N.re(2)] = functools.partial(retreat, 2, True)

        taken_df = set()

        def take_df(i):
            if i not in taken_df:
                taken_df.add(i)
                arrived(N.df_t(i), At(k.df)[t_rows, df_cols[i]])

        def re3():
            for i in range(4):
                take_df(i)
            retreat(3, True)

        def dn(i):
            take_df(i)
            rel = {N.x: i % 2, N.z1: i // 2}
            value = dot_tn(hid[...], k.df[:, df_cols[i]])
            for j, tag in enumerate(DOWN):
                travels[tag].own[unit_index(tag, rel)] = value[j * tall : (j + 1) * tall].astype(BF)

        own[N.re(3)] = re3
        for i in range(4):
            own[N.dn(i)] = functools.partial(dn, i)
        for i in range(2):
            own[N.ex(2, i)] = functools.partial(ex2, i)
            own[N.ex(3, i)] = functools.partial(ex3, i)
            for u in range(4):
                own[N.gg(i, u)] = functools.partial(wide_grad, GATE[i], i, u, dg)
                own[N.uu(i, u)] = functools.partial(wide_grad, UP[i], i, u, du)
        for name in ORDER[:feed_end]:
            own[name]()

    pl.run_scoped(
        feed_forward,
        pltpu.VMEM((width, quarter), BF),
        pltpu.VMEM((width, quarter), BF),
        pltpu.VMEM((quarter, width), BF),
        pltpu.VMEM((4 * span, quarter), BF),
        pltpu.VMEM((4 * span, quarter), BF),
        pltpu.VMEM((4 * span, quarter), BF),
    )

    shares, start = {}, 0
    for tag in MIXED:
        size = unit_shape(tag, slim * 8, 0, 8, 4)[0]
        shares[tag] = slice(start, start + size)
        start += size

    def mixer_backward(win, *own_mixed):
        got_win = fetch(k.w_in, win)
        for tag, own in zip(MIXED, own_mixed):
            travels[tag].own = own

        def mb1():
            arrived(N.pz, k.pz)
            k.sg[...] = jnp.zeros((8, width), F32)

            @functools.partial(loop, passes, unroll=False)
            def _(i):
                rows = block(i, step)
                d = k.own[rows, :] + k.pz[rows, :].astype(F32)
                v = k.res[rows, :]
                scale = k.sc2[rows, :]
                scaled = gain(k.gain2) * d
                k.sg[1:2, :] = k.sg[1:2, :] + jnp.sum(d * v * scale, axis=0, keepdims=True)
                d = (
                    k.cot[rows, :].astype(F32)
                    + scale * scaled
                    - v * (scale * scale * scale) * jnp.mean(scaled * v, axis=-1, keepdims=True)
                )
                k.own[rows, :] = d
                k.dmx[rows, :] = d.astype(BF)

            post(N.dmx_c, At(k.dmx)[pl.ds(0, span)], At(k.dmx)[pl.ds(span, span)], to_c)

        def mb2():
            @functools.partial(loop, width // 256)
            def _(j):
                cols = block(j, 256)
                d = dot_nt(k.dmx[:span, :], k.wout[cols, :])
                valid = mask(MASK_VALID)
                k.dc[:span, cols] = (valid * k.gc[:, cols] * d).astype(BF).astype(F32)
                c_cols = pl.ds(pl.multiple_of(width + j * 256, 256), 256)
                k.dpj[:span, c_cols] = (valid * conv_of(cols) * d).astype(BF)

            post(N.halo2, At(k.dc)[pl.ds(0, 8)], k.hr2, before, not_first)

        def mb3():
            @pl.when(s == 3)
            def _():
                k.dc[span:, :] = jnp.zeros((8, width), F32)

            @pl.when(not_last)
            def _():
                arrived(N.halo2, k.hr2)
                k.dc[span:, :] = k.hr2[...]

            @functools.partial(loop, width // 256, unroll=False)
            def _(j):
                cols = block(j, 256)
                d0 = k.dc[:span, cols]
                d = (
                    tap(0, cols) * mask(MASK_S0) * d0
                    + tap(1, cols) * mask(MASK_N1) * k.dc[1 : 1 + span, cols]
                    + tap(2, cols) * mask(MASK_N2) * k.dc[2 : 2 + span, cols]
                )
                valid = mask(MASK_VALID)
                k.dpj[:span, cols] = (valid * k.va[:, cols].astype(F32) * d).astype(BF)
                x_cols = pl.ds(pl.multiple_of(2 * width + j * 256, 256), 256)
                k.dpj[:span, x_cols] = (valid * k.gb[:, cols].astype(F32) * d).astype(BF)
                for i, m in ((0, MASK_S0), (1, MASK_S1), (2, MASK_S2)):
                    k.sg[2 + i : 3 + i, cols] = jnp.sum(
                        d0 * mask(m) * k.mix[8 - i : 8 - i + span, cols], axis=0, keepdims=True
                    )

            post(N.dpj_c, At(k.dpj)[pl.ds(0, span)], At(k.dpj)[pl.ds(span, span)], to_c)

        def mb4():
            got_win.wait()

            @functools.partial(loop, width // 256)
            def _(j):
                cols = block(j, 256)
                k.gc[:, cols] = dot_nt(k.dpj[:span, :], win[cols, :])

            @functools.partial(loop, passes, unroll=False)
            def _(i):
                rows = block(i, step)
                d = k.gc[rows, :]
                t = k.tok[rows, :].astype(F32)
                scale = k.sc1[rows, :]
                scaled = gain(k.gain1) * d
                k.sg[0:1, :] = k.sg[0:1, :] + jnp.sum(d * t * scale, axis=0, keepdims=True)
                d = (
                    k.own[rows, :]
                    + scale * scaled
                    - t * (scale * scale * scale) * jnp.mean(scaled * t, axis=-1, keepdims=True)
                )
                k.tok[rows, :] = d.astype(BF)

            put(k.tok, k.grad_tokens.at[0])
            for i in range(1, 8):
                post(N.sa(i), At(k.sg)[:, small_cols[i]], At(k.sa)[i - 1], (row_peers[i], s))
            for name, ref in (
                (N.nrm_c, k.nrm),
                (N.gat_c, k.gat),
                (N.dmx_c, k.dmx),
                (N.dpj_c, k.dpj),
            ):
                arrived(name, At(ref)[pl.ds(span, span)])

        def mg(rel_x, rel_y):
            rho = 4 * chosen(rel_y, y) + 2 * chosen(rel_x, x) + c
            rows = block(rho, slim)
            for a in range(2):
                for b in range(2):
                    sigma = 2 * chosen(b, z1) + chosen(a, z0)
                    first = dot_tn(k.nrm[:, rows], k.dpj[:, block(sigma, wide)])
                    second = dot_tn(k.gat[:, rows], k.dmx[:, block(sigma, side)])
                    for tag in MIXED:
                        u = unit_index(tag, {N.x: rel_x, N.y: rel_y, N.z0: a, N.z1: b})
                        own = travels[tag].own
                        own[u, :, :wide] = first[shares[tag]].astype(BF)
                        own[u, :, wide:] = second[shares[tag]].astype(BF)

        def finish_mixed():
            for tag in MIXED:
                got, at = travels[tag].got, travels[tag].starts[-1]
                rows = pl.ds(shares[tag].start, shares[tag].stop - shares[tag].start)
                put(At(got)[at, :, pl.ds(0, wide)], At(k.g_in)[rows, :])
                put(At(got)[at, :, pl.ds(wide, width - wide)], At(k.g_out)[rows, :])

        steps.update({N.mb(1): mb1, N.mb(2): mb2, N.mb(3): mb3, N.mb(4): mb4})
        for a in range(2):
            for b in range(2):
                steps[N.mg(a, b)] = functools.partial(mg, a, b)
        for name in ORDER[feed_end:]:
            steps[name]()
        finish_mixed()
        for name in list(pending):
            left(name)
        for cond, copy in stored:
            when(cond, lambda: copy().wait())

    pl.run_scoped(
        mixer_backward,
        pltpu.VMEM((width, 3 * width), BF),
        *[pltpu.VMEM((16, shares[tag].stop - shares[tag].start, width), BF) for tag in MIXED],
    )


def finish_kernel(n, *refs):
    sources, small = refs[:n], refs[n]
    targets, smalls = refs[n + 1 : 2 * n + 1], refs[2 * n + 1 : 2 * n + 4]
    rest = refs[2 * n + 4 :]
    held, wide, gets, puts = rest[:n], rest[n : 2 * n], rest[2 * n], rest[2 * n + 1]
    copies = [pltpu.make_async_copy(sources[i], held[i], gets.at[i]) for i in range(n)]
    for copy in copies:
        copy.start()
    s = lax.axis_index("seq")
    piece = smalls[0].shape[-1]
    value = jnp.zeros((8, piece), F32)
    for i in range(small.shape[1] // piece):
        value = jnp.where(s == i, small[:, i * piece : (i + 1) * piece], value)
    smalls[0][...] = value[0:1]
    smalls[1][...] = value[2:5]
    smalls[2][...] = value[1:2]
    out = []
    for i in range(n):
        copies[i].wait()
        ref = held[i]
        if sources[i].dtype != targets[i].dtype:
            rows = 64

            @functools.partial(loop, ref.shape[0] // rows, unroll=False)
            def _(j):
                here = block(j, rows)
                wide[i][here, :] = ref[here, :].astype(F32)

            ref = wide[i]
        copy = pltpu.make_async_copy(ref, targets[i], puts.at[i])
        copy.start()
        out.append(copy)
    for copy in out:
        copy.wait()


def fused(
    tokens,
    doc_lengths,
    valid_counts,
    norm_in,
    w_in,
    w_conv,
    w_out,
    norm_ffn,
    w_gate,
    w_up,
    w_down,
    cotangent,
):
    _, span, width = tokens.shape
    ff = w_gate.shape[1]
    rows, seq = lax.axis_size("rows"), lax.axis_size("seq")
    scratch = scratch_list(span, width, ff, rows, seq)
    anywhere = pl.BlockSpec(memory_space=pl.ANY)
    scalars = pl.BlockSpec(memory_space=pltpu.SMEM)
    vectors = pl.BlockSpec(memory_space=pltpu.VMEM)
    grads = [
        (width // rows, 3 * width // seq),
        (width // rows, width // seq),
        (width // rows, ff // seq),
        (width // rows, ff // seq),
        (ff // rows, width // seq),
    ]
    *outs, small = pl.pallas_call(
        functools.partial(layer_kernel, OPERANDS + list(scratch)),
        out_shape=[jax.ShapeDtypeStruct((1, span, width), BF)] * 2
        + [jax.ShapeDtypeStruct(shape, BF) for shape in grads]
        + [jax.ShapeDtypeStruct((8, width // rows), F32)],
        in_specs=[scalars] * 2 + [anywhere] * 2 + [vectors] * 3 + [anywhere] * 5,
        out_specs=[anywhere] * 8,
        scratch_shapes=list(scratch.values()),
        compiler_params=pltpu.CompilerParams(
            collective_id=0, has_side_effects=True, vmem_limit_bytes=67043328
        ),
        name="layer",
    )(
        doc_lengths,
        valid_counts,
        tokens,
        cotangent,
        norm_in,
        w_conv,
        norm_ffn,
        w_in,
        w_out,
        w_gate,
        w_up,
        w_down,
    )
    piece = width // (rows * seq)
    n = len(outs)
    held = [(1, span, width)] * 2 + grads
    *final, first, taps, second = pl.pallas_call(
        functools.partial(finish_kernel, n),
        out_shape=[jax.ShapeDtypeStruct((1, span, width), BF)] * 2
        + [jax.ShapeDtypeStruct(shape, F32) for shape in grads]
        + [jax.ShapeDtypeStruct((i, piece), F32) for i in (1, 3, 1)],
        in_specs=[anywhere] * n + [vectors],
        out_specs=[anywhere] * n + [vectors] * 3,
        scratch_shapes=[pltpu.VMEM(shape, BF) for shape in held]
        + [pltpu.VMEM(shape if i > 1 else (8, 128), F32) for i, shape in enumerate(held)]
        + [pltpu.SemaphoreType.DMA((n,))] * 2,
        name="finish",
    )(*outs, small)
    layer_out, grad_tokens, g_in, g_out, g_gate, g_up, g_down = final
    return (
        layer_out,
        grad_tokens,
        first[0],
        g_in,
        taps,
        g_out,
        second[0],
        g_gate,
        g_up,
        g_down,
    )


def solution(mesh):
    placed = (
        P("rows", "seq", None),
        P("rows", None),
        P("rows"),
        P(),
        P(),
        P(),
        P(),
        P(),
        P(),
        P(),
        P(),
        P("rows", "seq", None),
    )
    paired = mesh.shape["rows"] == 8 and mesh.shape["seq"] == 4
    return jax.shard_map(
        fused if paired else plain,
        mesh=mesh,
        in_specs=placed,
        out_specs=(
            P("rows", "seq", None),
            P("rows", "seq", None),
            P(("rows", "seq")),
            P("rows", "seq"),
            P(None, ("rows", "seq")),
            P("rows", "seq"),
            P(("rows", "seq")),
            P("rows", "seq"),
            P("rows", "seq"),
            P("rows", "seq"),
        ),
        check_vma=False,
    )
```

```python
import functools

import jax
import jax.numpy as jnp
import numpy as np
from jax import lax
from jax.experimental import pallas as pl
from jax.experimental.pallas import tpu as pltpu
from jax.sharding import PartitionSpec as P

EPSILON = 1e-05
BF = jnp.bfloat16
F32 = jnp.float32
MESH = pl.DeviceIdType.MESH


def passed_along(value, axis, steps):
    count = lax.axis_size(axis)
    first, last = (max(0, -steps), min(count, count - steps))
    return lax.ppermute(value, axis, [(source, source + steps) for source in range(first, last)])


def rms_scale(values):
    return lax.rsqrt(jnp.mean(values * values, axis=-1, keepdims=True) + EPSILON)


def doc_masks(lengths, positions):
    starts = jnp.cumsum(lengths) - lengths
    within = starts[None, :] <= positions[:, None]
    first = jnp.max(jnp.where(within, starts[None, :], 0), axis=1)
    return [(positions - offset >= first).astype(jnp.float32)[:, None] for offset in range(3)]


def weight_grad(left, right):
    return jnp.einsum("ta,tb->ab", left, right, preferred_element_type=jnp.float32)


def back_product(grad, weight):
    return jnp.einsum("tb,ab->ta", grad, weight, preferred_element_type=jnp.float32)


def scattered(value, row_dim, seq_dim):
    part = lax.psum_scatter(value.astype(BF), "rows", scatter_dimension=row_dim, tiled=True)
    part = lax.psum_scatter(part, "seq", scatter_dimension=seq_dim, tiled=True)
    return part.astype(F32)


def plain(
    tokens,
    doc_lengths,
    valid_counts,
    norm_in,
    w_in,
    w_conv,
    w_out,
    norm_ffn,
    w_gate,
    w_up,
    w_down,
    cotangent,
):
    inputs = tokens[0].astype(jnp.float32)
    span = inputs.shape[0]
    width = inputs.shape[1]
    start_pos = lax.axis_index("seq") * span
    positions = start_pos + jnp.arange(span + 2, dtype=jnp.int32)
    valid = (positions[:span] < valid_counts[0]).astype(jnp.float32)[:, None]
    same = doc_masks(doc_lengths[0], positions)
    taps = w_conv.astype(jnp.float32)
    gain_in = norm_in.astype(jnp.float32)
    gain_ffn = norm_ffn.astype(jnp.float32)
    scale1 = rms_scale(inputs)
    normed = (inputs * scale1 * gain_in).astype(jnp.bfloat16)
    proj = jnp.dot(normed, w_in, preferred_element_type=jnp.float32)
    gate_b = proj[:, :width]
    gate_c = proj[:, width : 2 * width]
    values = proj[:, 2 * width :]
    mixed_in = (valid * gate_b * values).astype(jnp.bfloat16)
    tail_rows = passed_along(mixed_in[span - 2 :], "seq", 1)
    padded = jnp.concatenate([tail_rows, mixed_in], axis=0).astype(jnp.float32)
    conv = jnp.zeros((span, width), jnp.float32)
    for offset in range(3):
        conv = conv + taps[offset] * same[offset][:span] * padded[2 - offset : 2 - offset + span]
    gated = (valid * gate_c * conv).astype(jnp.bfloat16)
    mixer_out = jnp.dot(gated, w_out, preferred_element_type=jnp.float32)
    resid = inputs + mixer_out
    scale2 = rms_scale(resid)
    normed2 = (resid * scale2 * gain_ffn).astype(jnp.bfloat16)
    gate_act = jnp.dot(normed2, w_gate, preferred_element_type=jnp.float32)
    up_act = jnp.dot(normed2, w_up, preferred_element_type=jnp.float32)
    sigmoid_gate = jax.nn.sigmoid(gate_act)
    silu_gate = gate_act * sigmoid_gate
    hidden = (silu_gate * up_act).astype(jnp.bfloat16)
    ffn_out = jnp.dot(hidden, w_down, preferred_element_type=jnp.float32)
    layer_out = (resid + valid * ffn_out).astype(jnp.bfloat16)
    grad_out = cotangent[0].astype(jnp.float32)
    d_ffn = (valid * grad_out).astype(jnp.bfloat16)
    grad_w_down = weight_grad(hidden, d_ffn)
    d_hidden = back_product(d_ffn, w_down)
    d_gate = (d_hidden * up_act * sigmoid_gate * (1.0 + gate_act * (1.0 - sigmoid_gate))).astype(
        jnp.bfloat16
    )
    d_up = (d_hidden * silu_gate).astype(jnp.bfloat16)
    grad_w_gate = weight_grad(normed2, d_gate)
    grad_w_up = weight_grad(normed2, d_up)
    d_normed2 = back_product(d_gate, w_gate) + back_product(d_up, w_up)
    grad_norm_ffn = jnp.sum(d_normed2 * resid * scale2, axis=0)
    scaled_ffn = gain_ffn * d_normed2
    d_resid = (
        grad_out
        + scale2 * scaled_ffn
        - resid * scale2**3 * jnp.mean(scaled_ffn * resid, axis=-1, keepdims=True)
    )
    d_mixer = d_resid.astype(jnp.bfloat16)
    grad_w_out = weight_grad(gated, d_mixer)
    d_gated = back_product(d_mixer, w_out)
    d_conv = (valid * gate_c * d_gated).astype(jnp.bfloat16)
    d_gate_c = valid * conv * d_gated
    head_rows = passed_along(d_conv[:2], "seq", -1)
    extended = jnp.concatenate([d_conv, head_rows], axis=0).astype(jnp.float32)
    d_mixed = jnp.zeros((span, width), jnp.float32)
    conv_rows = []
    for offset in range(3):
        d_mixed = (
            d_mixed
            + taps[offset] * same[offset][offset : offset + span] * extended[offset : offset + span]
        )
        conv_rows.append(
            jnp.sum(
                extended[:span] * same[offset][:span] * padded[2 - offset : 2 - offset + span],
                axis=0,
            )
        )
    grad_w_conv = jnp.stack(conv_rows, axis=0)
    d_proj = jnp.concatenate(
        [valid * values * d_mixed, d_gate_c, valid * gate_b * d_mixed], axis=1
    ).astype(jnp.bfloat16)
    grad_w_in = weight_grad(normed, d_proj)
    d_normed = back_product(d_proj, w_in)
    grad_norm_in = jnp.sum(d_normed * inputs * scale1, axis=0)
    scaled_in = gain_in * d_normed
    grad_tokens = (
        d_resid
        + scale1 * scaled_in
        - inputs * scale1**3 * jnp.mean(scaled_in * inputs, axis=-1, keepdims=True)
    )
    grad_tokens = grad_tokens.astype(jnp.bfloat16)
    return (
        layer_out[None],
        grad_tokens[None],
        scattered(grad_norm_in, 0, 0),
        scattered(grad_w_in, 0, 1),
        scattered(grad_w_conv, 1, 1),
        scattered(grad_w_out, 0, 1),
        scattered(grad_norm_ffn, 0, 0),
        scattered(grad_w_gate, 0, 1),
        scattered(grad_w_up, 0, 1),
        scattered(grad_w_down, 0, 1),
    )


def dot(a, b):
    return jnp.dot(a, b, preferred_element_type=F32)


def dot_nt(a, b):
    return lax.dot_general(a, b, (((1,), (1,)), ((), ())), preferred_element_type=F32)


def dot_tn(a, b):
    return lax.dot_general(a, b, (((0,), (0,)), ((), ())), preferred_element_type=F32)


def bit_of(value, weight):
    return lax.rem(lax.div(value, np.int32(weight)), np.int32(2))


def flipped(value, weights):
    for weight in (1, 2, 4):
        if weights & weight:
            value = value + weight - 2 * weight * bit_of(value, weight)
    return value


def loop(count, body, unroll=True):
    lax.fori_loop(0, count, lambda i, carry: (body(i), carry)[1], 0, unroll=unroll)


def block(index, size):
    return pl.ds(pl.multiple_of(index * size, size), size)


class Name(str):
    def __call__(self, *index):
        return (self,) + index


class Names:
    def __getattr__(self, name):
        return Name(name)


N = Names()

STAGES = {
    N.A: (N.x, N.y, N.z1),
    N.B: (N.y, N.z1, N.x),
    N.g0: (N.y, N.x, N.z1),
    N.g1: (N.y, N.x, N.z1),
    N.u0: (N.x, N.z1, N.y),
    N.u1: (N.x, N.y, N.z1),
    N.m0: (N.y, N.x, N.z0, N.z1),
    N.m1: (N.x, N.z0, N.y, N.z1),
    N.m2: (N.z0, N.x, N.z1, N.y),
}
ORDER = [
    N.ex(0), N.ex(1), N.re(1), N.tn(0), N.bk(1), N.ex(2, 0), N.re(0), N.bk(0),
    N.tn(1), N.tdf(0), N.ex(2, 1), N.ex(3, 0), N.ex(3, 1), N.dn(0), N.go(N.A, 0, 0), N.go(N.B, 0, 0),
    N.tdf(1), N.dn(1), N.go(N.B, 0, 1), N.tdf(2), N.tdf(3), N.re(2), N.dn(2), N.go(N.A, 0, 1),
    N.go(N.B, 0, 2), N.B(0, 0), N.go(N.B, 1, 0), N.re(3), N.bk(3), N.gg(0, 3), N.gg(0, 0), N.go(N.g0, 0, 0),
    N.gg(1, 0), N.go(N.g1, 0, 0), N.uu(0, 0), N.go(N.u0, 0, 0), N.B(0, 1), N.go(N.B, 1, 1), N.A(0, 0), N.go(N.A, 1, 0),
    N.bk(2), N.uu(1, 0), N.go(N.u1, 0, 0), N.dn(3), N.go(N.B, 0, 3), N.gg(0, 1), N.go(N.g0, 0, 1), N.uu(0, 3),
    N.gg(1, 1), N.go(N.g1, 0, 1), N.uu(0, 2), N.gg(1, 2), N.uu(1, 3), N.fo(1), N.uu(0, 1), N.go(N.u0, 0, 1),
    N.uu(1, 1), N.go(N.u1, 0, 1), N.uu(1, 2), N.B(0, 2), N.gg(1, 3), N.fo(3), N.u0(0, 0), N.go(N.u0, 1, 0),
    N.fo(2), N.u1(0, 0), N.go(N.u1, 1, 0), N.A(0, 1), N.go(N.A, 1, 1), N.B(1, 0), N.go(N.B, 2, 0), N.fo(0),
    N.gg(0, 2), N.g0(0, 0), N.go(N.g0, 1, 0), N.mb(1), N.mb(2), N.u0(0, 1), N.go(N.u0, 1, 1), N.u1(0, 1),
    N.B(0, 3), N.g1(0, 0), N.go(N.g1, 1, 0), N.g0(0, 1), N.u0(1, 0), N.go(N.u0, 2, 0), N.B(1, 1), N.mb(3),
    N.A(1, 0), N.go(N.A, 2, 0), N.mb(4), N.lo, N.mg(0, 0), N.go(N.m0, 0, 0), N.go(N.m1, 0, 0), N.go(N.m2, 0, 0),
    N.go(N.m0, 0, 1), N.go(N.m1, 0, 1), N.go(N.m0, 0, 2), N.go(N.m2, 0, 2), N.go(N.m0, 0, 3), N.go(N.m1, 0, 4), N.go(N.m1, 0, 5), N.g1(0, 1),
    N.mg(0, 1), N.go(N.m2, 0, 1), N.go(N.m1, 0, 2), N.go(N.m1, 0, 3), N.go(N.m2, 0, 3), N.go(N.m1, 0, 6), N.go(N.m1, 0, 7), N.mg(1, 0),
    N.go(N.m0, 0, 4), N.go(N.m2, 0, 4), N.go(N.m0, 0, 5), N.go(N.m0, 0, 6), N.go(N.m2, 0, 6), N.go(N.m0, 0, 7), N.B(2, 0), N.mg(1, 1),
    N.go(N.m2, 0, 5), N.go(N.m2, 0, 7), N.g0(1, 0), N.go(N.g0, 2, 0), N.sg(0), N.dl(1), N.u1(1, 0), N.go(N.u1, 2, 0),
    N.m2(0, 6), N.A(1, 1), N.A(2, 0), N.dl(0), N.u0(1, 1), N.g1(1, 0), N.go(N.g1, 2, 0), N.m2(0, 0),
    N.go(N.m2, 1, 0), N.m1(0, 0), N.go(N.m1, 1, 0), N.m2(0, 3), N.go(N.m2, 1, 3), N.m2(0, 1), N.go(N.m2, 1, 1), N.m1(0, 1),
    N.go(N.m1, 1, 1), N.m2(0, 4), N.m2(0, 2), N.go(N.m2, 1, 2), N.m2(0, 5), N.m1(0, 4), N.m1(0, 7), N.m1(0, 5),
    N.m0(0, 0), N.go(N.m0, 1, 0), N.u0(2, 0), N.m1(0, 2), N.go(N.m1, 1, 2), N.m0(0, 1), N.go(N.m0, 1, 1), N.sg(1),
    N.u1(2, 0), N.m1(0, 3), N.go(N.m1, 1, 3), N.m0(0, 2), N.go(N.m0, 1, 2), N.m1(1, 0), N.go(N.m1, 2, 0), N.m1(1, 1),
    N.go(N.m1, 2, 1), N.m2(0, 7), N.w3(N.u), N.m2(1, 0), N.go(N.m2, 2, 0), N.w4(N.u), N.m0(0, 3), N.go(N.m0, 1, 3),
    N.m1(0, 6), N.m2(1, 1), N.go(N.m2, 2, 1), N.m1(1, 2), N.m2(1, 3), N.m0(0, 4), N.dt, N.g1(2, 0),
    N.m0(1, 0), N.go(N.m0, 2, 0), N.m1(1, 3), N.m2(1, 2), N.g0(2, 0), N.m2(2, 0), N.go(N.m2, 3, 0), N.m0(0, 5),
    N.m2(2, 1), N.m0(0, 6), N.m0(1, 1), N.go(N.m0, 2, 1), N.m0(1, 2), N.m0(2, 0), N.go(N.m0, 3, 0), N.m1(2, 0),
    N.go(N.m1, 3, 0), N.m0(0, 7), N.w3(N.g), N.m2(3, 0), N.m0(1, 3), N.m1(2, 1), N.w4(N.g), N.m0(2, 1),
    N.m0(3, 0), N.m1(3, 0),
]
FEED = (N.ex, N.re, N.bk, N.dn, N.gg, N.uu, N.fo)
EIGHTHS = {N.m0: 6, N.m1: 1, N.m2: 1}
MIXED = list(EIGHTHS)
DOWN = [N.A, N.B]
GATE = [N.g0, N.g1]
UP = [N.u0, N.u1]
N_SEM = 192
MASK_VALID, MASK_S0, MASK_S1, MASK_S2, MASK_N1, MASK_N2 = range(6)


def scatter_of(tag):
    return (N.x, N.y, N.z0, N.z1) if tag in MIXED else (N.x, N.z1) if tag in DOWN else (N.x, N.y)


def counts_of(tag):
    counts = [2 ** len(scatter_of(tag))]
    for dim in STAGES[tag]:
        counts.append(counts[-1] // 2 if dim in scatter_of(tag) else counts[-1])
    return counts


def unit_index(tag, rel):
    index = 0
    for dim in STAGES[tag]:
        if dim in scatter_of(tag):
            index = 2 * index + rel[dim]
    return index


def unit_bits(tag, index):
    dims = [dim for dim in STAGES[tag] if dim in scatter_of(tag)]
    return {dim: (index >> (len(dims) - 1 - i)) & 1 for i, dim in enumerate(dims)}


def unit_shape(tag, width, ff, rows, seq):
    if tag in DOWN:
        return ff // rows, width // seq
    if tag in MIXED:
        return width // rows * EIGHTHS[tag] // 8, width
    return width // rows, ff // 4


def scratch_list(span, width, ff, rows, seq):
    group = 4 * span
    shapes = dict(
        tok=pltpu.VMEM((span, width), BF),
        cot=pltpu.VMEM((span, width), BF),
        wout=pltpu.VMEM((width, width), BF),
        nrm=pltpu.VMEM((2 * span, width), BF),
        gat=pltpu.VMEM((2 * span, width), BF),
        dmx=pltpu.VMEM((2 * span, width), BF),
        dpj=pltpu.VMEM((2 * span, 3 * width), BF),
        gb=pltpu.VMEM((span, width), BF),
        va=pltpu.VMEM((span, width), BF),
        gc=pltpu.VMEM((span, width), F32),
        mix=pltpu.VMEM((span + 8, width), F32),
        dc=pltpu.VMEM((span + 8, width), F32),
        res=pltpu.VMEM((span, width), F32),
        own=pltpu.VMEM((span, width), F32),
        loa=pltpu.VMEM((span, width), F32),
        mask=pltpu.VMEM((span, 128), F32),
        sc1=pltpu.VMEM((span, 1), F32),
        sc2=pltpu.VMEM((span, 1), F32),
        n2=pltpu.VMEM((group, width), BF),
        df=pltpu.VMEM((group, width), BF),
        hr=pltpu.VMEM((8, width), F32),
        hr2=pltpu.VMEM((8, width), F32),
        ps=pltpu.VMEM((2, span, width), BF),
        pr=pltpu.VMEM((2, span, width), BF),
        pz=pltpu.VMEM((span, width), BF),
        fr=pltpu.VMEM((2, span, width), BF),
        fz=pltpu.VMEM((span, width), BF),
        sg=pltpu.VMEM((8, width), F32),
        sa=pltpu.VMEM((rows - 1, 8, width // rows), F32),
        ss=pltpu.VMEM((8, width // rows), F32),
        sb=pltpu.VMEM((seq - 1, 8, width // rows), F32),
        rd4=pltpu.VMEM(unit_shape(N.A, width, ff, rows, seq), BF),
        rg4=pltpu.VMEM(unit_shape(N.g0, width, ff, rows, seq), BF),
        ru4=pltpu.VMEM(unit_shape(N.u0, width, ff, rows, seq), BF),
        send=pltpu.SemaphoreType.DMA((N_SEM,)),
        recv=pltpu.SemaphoreType.DMA((N_SEM,)),
        local=pltpu.SemaphoreType.DMA((32,)),
    )
    for tag in STAGES:
        unit = unit_shape(tag, width, ff, rows, seq)
        counts = counts_of(tag)
        if tag not in MIXED:
            shapes[N.own, tag] = pltpu.VMEM((counts[0],) + unit, BF)
        shapes[N.got, tag] = pltpu.VMEM((sum(counts[1:]),) + unit, BF)
    return shapes


OPERANDS = [
    N.lengths,
    N.counts,
    N.tokens,
    N.cotangent,
    N.gain1,
    N.taps,
    N.gain2,
    N.w_in,
    N.w_out,
    N.w_gate,
    N.w_up,
    N.w_down,
    N.layer_out,
    N.grad_tokens,
    N.g_in,
    N.g_out,
    N.g_gate,
    N.g_up,
    N.g_down,
    N.small,
]


class Refs:
    pass


class View:
    def __init__(self, ref, index):
        self.ref, self.index = ref, index

    def take(self):
        return self.ref.at[self.index]


class At:
    def __init__(self, ref):
        self.ref = ref

    def __getitem__(self, index):
        return View(self.ref, index)


def taken(ref):
    return ref.take() if isinstance(ref, View) else ref


def layer_kernel(names, *refs):
    k = Refs()
    travelling = {}
    for name, ref in zip(names, refs):
        if isinstance(name, tuple):
            travelling[name] = ref
        else:
            setattr(k, name, ref)
    span, width = k.tok.shape
    slim, quarter = k.rg4.shape
    tall, side = k.rd4.shape
    wide = 3 * width // 4

    r = lax.axis_index("rows")
    s = lax.axis_index("seq")
    c, x, y = bit_of(r, 1), bit_of(r, 2), bit_of(r, 4)
    z0, z1 = bit_of(s, 1), bit_of(s, 2)
    row_peers = [flipped(r, i) for i in range(8)]
    seq_peers = [flipped(s, i) for i in range(4)]
    to_c = (row_peers[1], s)
    to_z = (r, seq_peers[1])
    to_dim = {
        N.x: (row_peers[2], s),
        N.y: (row_peers[4], s),
        N.z0: to_z,
        N.z1: (r, seq_peers[2]),
    }
    partners = [(row, s) for row in row_peers[1:]] + [(r, seq) for seq in seq_peers[1:]]
    partners += [(row_peers[2], seq_peers[1]), (row_peers[3], seq_peers[1])]
    after = (r, lax.rem(s + 1, np.int32(4)))
    before = (r, lax.rem(s + 3, np.int32(4)))
    df_cols = [block(2 * (z1 if w else 1 - z1) + (x if v else 1 - x), side) for w in (0, 1) for v in (0, 1)]
    active, idle = c == y, c != y
    holder, lender = c == z1, c != z1
    not_last, not_first = s < 3, s > 0
    home = [jnp.logical_and(active, jnp.logical_and(x == z0, y == i)) for i in range(2)]
    gives = [jnp.logical_and(active, jnp.logical_not(home[i])) for i in range(2)]
    targets = [(4 * y + 2 * z0 + i, 2 * z1 + x) for i in range(2)]
    away = jnp.logical_not(jnp.logical_and(active, x == z0))
    away_at = [jnp.logical_and(away, c == i) for i in range(2)]
    core_is = [c == 0, c == 1]
    holds = [jnp.logical_and(holder, c == i) for i in range(2)]
    small_cols = [block(row, slim) for row in row_peers]

    sems = {}
    pending = {}

    def remote(name, src, dst, device):
        at = sems.setdefault(name, len(sems))
        assert at < N_SEM
        return pltpu.make_async_remote_copy(
            src_ref=taken(src),
            dst_ref=taken(dst),
            send_sem=k.send.at[at],
            recv_sem=k.recv.at[at],
            device_id=device,
            device_id_type=MESH,
        )

    def when(cond, go):
        if cond is None:
            go()
        else:
            pl.when(cond)(go)

    def post(name, src, dst, device, cond=None):
        when(cond, lambda: remote(name, src, dst, device).start())
        pending[name] = cond, (name, src, dst, device)

    def left(name):
        cond, args = pending.pop(name)
        when(cond, lambda: remote(*args).wait_send())

    def arrived(name, dst):
        remote(name, dst, dst, to_c).wait_recv()

    local_count = [0]

    def local_copy(src, dst):
        at = local_count[0]
        local_count[0] += 1
        return pltpu.make_async_copy(taken(src), taken(dst), k.local.at[at])

    def fetch(src, dst):
        copy = local_copy(src, dst)
        copy.start()
        return copy

    stored = []

    def put(src, dst, cond=None):
        at = local_count[0]
        local_count[0] += 1

        def copy():
            return pltpu.make_async_copy(taken(src), taken(dst), k.local.at[at])

        when(cond, lambda: copy().start())
        stored.append((cond, copy))

    def add(dst, src):
        dst[...] = (dst[...].astype(F32) + src[...].astype(F32)).astype(BF)

    def chosen(rel, bit):
        return bit if rel else 1 - bit

    class Travel:
        def __init__(self, tag, own):
            self.tag, self.own, self.order = tag, own, STAGES[tag]
            self.counts = counts_of(tag)
            self.got = travelling[N.got, tag]
            self.starts = [sum(self.counts[1 : p + 1]) for p in range(len(self.order))]
            self.alive = active if tag in DOWN else holder
            self.role_at = len(self.order)
            for p, dim in enumerate(self.order):
                if dim not in scatter_of(tag):
                    self.role_at = p

        def held(self, p, i):
            return (self.own, i) if p == 0 else (self.got, self.starts[p - 1] + i)

        def leave(self, p, i):
            if p == len(self.order):
                return
            dim = self.order[p]
            ref, at = self.held(p, i)
            cond = None
            if dim in scatter_of(self.tag):
                if i >= self.counts[p] // 2:
                    return
                if p > self.role_at:
                    cond = self.alive
            else:
                cond = idle if self.tag in DOWN else lender
            post((self.tag, p, i), At(ref)[at], At(self.got)[self.starts[p] + i], to_dim[dim], cond)

        def step(self, p, i):
            at = self.starts[p] + i
            halved = self.order[p] in scatter_of(self.tag)
            ref, mine = self.held(p, i + (self.counts[p + 1] if halved else 0))

            def go():
                arrived((self.tag, p, i), At(self.got)[at])
                add(self.got.at[at], ref.at[mine])

            when(self.alive if p >= self.role_at else None, go)

        def last(self):
            return At(self.got)[self.starts[-1]]

    travels = {tag: Travel(tag, travelling.get((N.own, tag))) for tag in STAGES}
    steps = {}
    for tag, travel in travels.items():
        for p in range(len(travel.order)):
            for i in range(travel.counts[p + 1]):
                steps[tag, p, i] = functools.partial(travel.step, p, i)
        for p in range(len(travel.order)):
            for i in range(travel.counts[p]):
                steps[N.go, tag, p, i] = functools.partial(travel.leave, p, i)

    got_tok = fetch(k.tokens.at[0], k.tok)
    got_cot = fetch(k.cotangent.at[0], k.cot)
    barrier = pltpu.get_barrier_semaphore()
    for device in partners:
        pl.semaphore_signal(barrier, inc=1, device_id=device, device_id_type=MESH)

    position = s * span + lax.broadcasted_iota(jnp.int32, (span, 1), 0)
    starts = [np.int32(0)]
    for i in range(k.lengths.shape[1] - 1):
        starts.append(starts[-1] + k.lengths[0, i])

    def first_of(at):
        first = jnp.zeros_like(at)
        for start in starts:
            first = jnp.maximum(first, jnp.where(start <= at, start, 0))
        return first

    def flag(test):
        return jnp.where(test, 1.0, 0.0).astype(F32)

    def write_masks():
        first0, first1, first2 = (first_of(position + i) for i in range(3))
        columns = [
            flag(position < k.counts[0]),
            flag(position >= first0),
            flag(position - 1 >= first0),
            flag(position - 2 >= first0),
            flag(position >= first1),
            flag(position >= first2),
        ]
        lane = lax.broadcasted_iota(jnp.int32, (span, 128), 1)
        table = jnp.zeros((span, 128), F32)
        for i, column in enumerate(columns):
            table = jnp.where(lane == i, column, table)
        k.mask[...] = table

    def mask(i, rows=slice(None)):
        return k.mask[rows, i : i + 1]

    def gain(ref):
        return ref[...].astype(F32).reshape(1, width)

    step = 64
    passes = span // step
    part = span // 2

    def send_df(i):
        cols = df_cols[i]
        src, dst = At(k.df)[pl.ds(0, span), cols], At(k.df)[pl.ds(2 * span, span), cols]
        post(N.df_z(i), src, dst, to_z)

    def mixer_forward(win):
        got_win = [fetch(k.w_in.at[:, block(i, width)], win.at[:, block(i, width)]) for i in (0, 2, 1)]
        got_wout = fetch(k.w_out, k.wout)
        write_masks()
        got_tok.wait()

        @functools.partial(loop, passes, unroll=False)
        def _(i):
            rows = block(i, step)
            t = k.tok[rows, :].astype(F32)
            scale = lax.rsqrt(jnp.mean(t * t, axis=-1, keepdims=True) + EPSILON)
            k.sc1[rows, :] = scale
            k.nrm[rows, :] = (t * scale * gain(k.gain1)).astype(BF)

        got_cot.wait()

        @functools.partial(loop, passes, unroll=False)
        def _(i):
            rows = block(i, step)
            k.df[rows, :] = (mask(MASK_VALID, rows) * k.cot[rows, :].astype(F32)).astype(BF)

        pl.semaphore_wait(barrier, len(partners))
        send_df(0)
        post(N.df_c, At(k.df)[pl.ds(0, span)], At(k.df)[pl.ds(span, span)], to_c)
        got_win[0].wait()
        got_win[1].wait()

        @functools.partial(loop, width // 256)
        def _(j):
            n = k.nrm[:span, :]
            cols = block(j, 256)
            gb = dot(n, win[:, cols])
            va = dot(n, win[:, pl.ds(pl.multiple_of(2 * width + j * 256, 256), 256)])
            k.gb[:, cols] = gb.astype(BF)
            k.va[:, cols] = va.astype(BF)
            k.mix[8:, cols] = (mask(MASK_VALID) * gb * va).astype(BF).astype(F32)

        post(N.halo, At(k.mix)[pl.ds(span, 8)], k.hr, after, not_last)
        got_win[2].wait()

        @functools.partial(loop, width // 256)
        def _(j):
            cols = block(j, 256)
            c_cols = pl.ds(pl.multiple_of(width + j * 256, 256), 256)
            k.gc[:, cols] = dot(k.nrm[:span, :], win[:, c_cols])

        got_wout.wait()

    pl.run_scoped(mixer_forward, pltpu.VMEM((width, 3 * width), BF))

    @pl.when(s == 0)
    def _():
        k.mix[:8, :] = jnp.zeros((8, width), F32)

    @pl.when(not_first)
    def _():
        arrived(N.halo, k.hr)
        k.mix[:8, :] = k.hr[...]

    def tap(i, cols):
        return k.taps[i : i + 1, cols].astype(F32)

    def conv_of(cols):
        return (
            tap(0, cols) * mask(MASK_S0) * k.mix[8 : 8 + span, cols]
            + tap(1, cols) * mask(MASK_S1) * k.mix[7 : 7 + span, cols]
            + tap(2, cols) * mask(MASK_S2) * k.mix[6 : 6 + span, cols]
        )

    @functools.partial(loop, width // 256)
    def _(j):
        cols = block(j, 256)
        k.gat[:span, cols] = (mask(MASK_VALID) * k.gc[:, cols] * conv_of(cols)).astype(BF)

    @functools.partial(loop, width // 256)
    def _(j):
        cols = block(j, 256)
        k.res[:, cols] = k.tok[:, cols].astype(F32) + dot(k.gat[:span, :], k.wout[:, cols])

    for i in range(2):

        @functools.partial(loop, passes // 2)
        def _(j):
            rows = block(i * (passes // 2) + j, step)
            v = k.res[rows, :]
            scale = lax.rsqrt(jnp.mean(v * v, axis=-1, keepdims=True) + EPSILON)
            k.sc2[rows, :] = scale
            k.n2[rows, :] = (v * scale * gain(k.gain2)).astype(BF)

        here = pl.ds(i * part, part)
        post(N.n2_z(i), At(k.n2)[here], At(k.n2)[pl.ds(2 * span + i * part, part)], to_z)
    post(N.n2_c, At(k.n2)[pl.ds(0, span)], At(k.n2)[pl.ds(span, span)], to_c)
    for i in (1, 2, 3):
        send_df(i)
    post(N.nrm_c, At(k.nrm)[pl.ds(0, span)], At(k.nrm)[pl.ds(span, span)], to_c)
    post(N.gat_c, At(k.gat)[pl.ds(0, span)], At(k.gat)[pl.ds(span, span)], to_c)

    z_rows, t_rows = pl.ds(2 * span, span), pl.ds(3 * span, span)
    z_parts = [pl.ds(2 * span + i * part, part) for i in range(2)]
    t_parts = [pl.ds(3 * span + i * part, part) for i in range(2)]

    def pass_df(i):
        arrived(N.df_z(i), At(k.df)[z_rows, df_cols[i]])
        post(N.df_t(i), At(k.df)[z_rows, df_cols[i]], At(k.df)[t_rows, df_cols[i]], to_c)

    def pass_n2(i):
        arrived(N.n2_z(i), At(k.n2)[z_parts[i]])
        post(N.n2_t(i), At(k.n2)[z_parts[i]], At(k.n2)[t_parts[i]], to_c)

    for i in range(4):
        steps[N.tdf(i)] = functools.partial(pass_df, i)
    for i in range(2):
        steps[N.tn(i)] = functools.partial(pass_n2, i)

    def down_last(i):
        got = travels[DOWN[i]].last()
        post(N.rd4(i), got, k.rd4, targets[i], gives[i])
        put(got, k.g_down, home[i])

    def down_take():
        for i in range(2):
            when(away_at[i], lambda: arrived(N.rd4(i), k.rd4))
        put(k.rd4, k.g_down, away)

    def wide_last(tag):
        mine, out = (k.rg4, k.g_gate) if tag == N.g else (k.ru4, k.g_up)
        for core in range(2):
            got = travels[(GATE if tag == N.g else UP)[core]].last()
            post((tag, core), got, mine, to_c, holds[1 - core])
            put(got, out, holds[core])

    lends = [jnp.logical_and(lender, c == i) for i in range(2)]

    def wide_take(tag):
        mine, out = (k.rg4, k.g_gate) if tag == N.g else (k.ru4, k.g_up)
        for core in range(2):
            when(lends[core], lambda: arrived((tag, core), mine))
        put(mine, out, lender)

    for i in range(2):
        steps[N.dl(i)] = functools.partial(down_last, i)
    steps[N.dt] = down_take
    for tag in (N.g, N.u):
        steps[N.w3(tag)] = functools.partial(wide_last, tag)
        steps[N.w4(tag)] = functools.partial(wide_take, tag)

    def small_rows():
        total = k.sg[:, small_cols[0]]
        for i in range(1, 8):
            arrived(N.sa(i), At(k.sa)[i - 1])
            total = total + k.sa[i - 1]
        k.ss[...] = total
        for i in range(1, 4):
            post(N.sb(i), k.ss, At(k.sb)[i - 1], (r, seq_peers[i]))

    def small_seq():
        total = k.ss[...]
        for i in range(1, 4):
            arrived(N.sb(i), At(k.sb)[i - 1])
            left(N.sb(i))
            total = total + k.sb[i - 1]
        k.ss[...] = total
        put(k.ss, k.small)

    steps[N.sg(0)], steps[N.sg(1)] = small_rows, small_seq

    def layer_output():
        arrived(N.fz, k.fz)

        @functools.partial(loop, passes, unroll=False)
        def _(i):
            rows = block(i, step)
            valid = mask(MASK_VALID, rows)
            k.cot[rows, :] = (k.loa[rows, :] + valid * k.fz[rows, :].astype(F32)).astype(BF)

        put(k.cot, k.layer_out.at[0])

    steps[N.lo] = layer_output
    feed_end = 1 + max(i for i, name in enumerate(ORDER) if name[0] in FEED)

    def feed_forward(wg, wu, wd, hid, dg, du):
        q = 2 * c + z0
        got_wg = fetch(k.w_gate.at[:, block(q, quarter)], wg)
        got_wu = fetch(k.w_up.at[:, block(q, quarter)], wu)
        got_wd = fetch(k.w_down.at[block(q, quarter), :], wd)

        def tiles(body, unroll):
            loop(quarter // 256, lambda j: body(block(j, 256)), unroll)
            if quarter % 256:
                body(pl.ds(quarter - quarter % 256, quarter % 256))

        def expand(rows, unroll):
            def tile(cols):
                n = k.n2[rows, :]
                g = dot(n, wg[:, cols])
                u = dot(n, wu[:, cols])
                sig = jax.nn.sigmoid(g)
                silu = g * sig
                hid[rows, cols] = (silu * u).astype(BF)
                dg[rows, cols] = (u * sig * (1.0 + g * (1.0 - sig))).astype(BF)
                du[rows, cols] = silu.astype(BF)

            tiles(tile, unroll)

        def retreat(slot, unroll):
            rows = pl.ds(slot * span, span)

            def tile(cols):
                d = dot_nt(k.df[rows, :], wd[cols, :])
                dg[rows, cols] = (d * dg[rows, cols].astype(F32)).astype(BF)
                du[rows, cols] = (d * du[rows, cols].astype(F32)).astype(BF)

            tiles(tile, unroll)

        def back(slot, ref, plus, unroll):
            rows = pl.ds(slot * span, span)

            @functools.partial(loop, width // 256, unroll=unroll)
            def _(j):
                cols = block(j, 256)
                value = dot_nt(dg[rows, :], wg[cols, :]) + dot_nt(du[rows, :], wu[cols, :])
                if plus is not None:
                    value = value + plus[:, cols].astype(F32)
                ref[:, cols] = value.astype(ref.dtype)

        def forth(slot, store):
            rows = pl.ds(slot * span, span)

            @functools.partial(loop, width // 256, unroll=False)
            def _(j):
                cols = block(j, 256)
                store(cols, dot(hid[rows, :], wd[:, cols]))

        own = steps

        waiting = [got_wd]

        def take_wd():
            while waiting:
                waiting.pop().wait()

        def ex0():
            got_wg.wait()
            got_wu.wait()
            expand(pl.ds(0, span), False)

        def ex1():
            arrived(N.n2_c, At(k.n2)[pl.ds(span, span)])
            expand(pl.ds(span, span), False)

        def re0():
            take_wd()
            retreat(0, False)

        def re1():
            take_wd()
            arrived(N.df_c, At(k.df)[pl.ds(span, span)])
            retreat(1, False)

        def bk1():
            back(1, k.ps.at[0], None, False)
            post(N.pr0, At(k.ps)[0], At(k.pr)[0], to_c)

        def bk0():
            arrived(N.pr0, At(k.pr)[0])
            back(0, k.own, k.pr.at[0], False)

        def ex2(i):
            expand(z_parts[i], True)

        def ex3(i):
            arrived(N.n2_t(i), At(k.n2)[t_parts[i]])
            expand(t_parts[i], True)

        def bk3():
            back(3, k.ps.at[1], None, True)
            post(N.pr1, At(k.ps)[1], At(k.pr)[1], to_c)

        def bk2():
            arrived(N.pr1, At(k.pr)[1])
            back(2, k.pr.at[1], k.pr.at[1], True)
            post(N.pz, At(k.pr)[1], k.pz, to_z)

        def wide_grad(tag, core, u, grad):
            travel = travels[tag]
            rel = unit_bits(tag, u)
            rho = 4 * chosen(rel[N.y], y) + 2 * chosen(rel[N.x], x) + core
            travel.own[u] = dot_tn(k.n2[:, block(rho, slim)], grad[...]).astype(BF)

        def to_ref(ref, plus=None):
            def store(cols, value):
                if plus is not None:
                    value = value + plus[:, cols].astype(F32)
                ref[:, cols] = value.astype(ref.dtype)

            return store

        def fo1():
            left(N.pr0)
            forth(1, to_ref(k.ps.at[0]))
            post(N.fr0, At(k.ps)[0], At(k.fr)[0], to_c)

        def fo3():
            left(N.pr1)
            forth(3, to_ref(k.ps.at[1]))
            post(N.fr1, At(k.ps)[1], At(k.fr)[1], to_c)

        def fo2():
            arrived(N.fr1, At(k.fr)[1])
            forth(2, to_ref(k.fr.at[1], k.fr.at[1]))
            post(N.fz, At(k.fr)[1], k.fz, to_z)

        def fo0():
            arrived(N.fr0, At(k.fr)[0])

            def store(cols, value):
                value = value + k.fr[0, :, cols].astype(F32)
                k.loa[:, cols] = k.res[:, cols] + mask(MASK_VALID) * value

            forth(0, store)

        own.update({N.ex(0): ex0, N.ex(1): ex1, N.re(0): re0, N.re(1): re1})
        own.update({N.bk(0): bk0, N.bk(1): bk1, N.bk(2): bk2, N.bk(3): bk3})
        own.update({N.fo(0): fo0, N.fo(1): fo1, N.fo(2): fo2, N.fo(3): fo3})
        own[N.re(2)] = functools.partial(retreat, 2, True)

        taken_df = set()

        def take_df(i):
            if i not in taken_df:
                taken_df.add(i)
                arrived(N.df_t(i), At(k.df)[t_rows, df_cols[i]])

        def re3():
            for i in range(4):
                take_df(i)
            retreat(3, True)

        def dn(i):
            take_df(i)
            rel = {N.x: i % 2, N.z1: i // 2}
            value = dot_tn(hid[...], k.df[:, df_cols[i]])
            for j, tag in enumerate(DOWN):
                travels[tag].own[unit_index(tag, rel)] = value[j * tall : (j + 1) * tall].astype(BF)

        own[N.re(3)] = re3
        for i in range(4):
            own[N.dn(i)] = functools.partial(dn, i)
        for i in range(2):
            own[N.ex(2, i)] = functools.partial(ex2, i)
            own[N.ex(3, i)] = functools.partial(ex3, i)
            for u in range(4):
                own[N.gg(i, u)] = functools.partial(wide_grad, GATE[i], i, u, dg)
                own[N.uu(i, u)] = functools.partial(wide_grad, UP[i], i, u, du)
        for name in ORDER[:feed_end]:
            own[name]()

    pl.run_scoped(
        feed_forward,
        pltpu.VMEM((width, quarter), BF),
        pltpu.VMEM((width, quarter), BF),
        pltpu.VMEM((quarter, width), BF),
        pltpu.VMEM((4 * span, quarter), BF),
        pltpu.VMEM((4 * span, quarter), BF),
        pltpu.VMEM((4 * span, quarter), BF),
    )

    shares, start = {}, 0
    for tag in MIXED:
        size = unit_shape(tag, slim * 8, 0, 8, 4)[0]
        shares[tag] = slice(start, start + size)
        start += size

    def mixer_backward(win, *own_mixed):
        got_win = fetch(k.w_in, win)
        for tag, own in zip(MIXED, own_mixed):
            travels[tag].own = own

        def mb1():
            arrived(N.pz, k.pz)
            k.sg[...] = jnp.zeros((8, width), F32)

            @functools.partial(loop, passes, unroll=False)
            def _(i):
                rows = block(i, step)
                d = k.own[rows, :] + k.pz[rows, :].astype(F32)
                v = k.res[rows, :]
                scale = k.sc2[rows, :]
                scaled = gain(k.gain2) * d
                k.sg[1:2, :] = k.sg[1:2, :] + jnp.sum(d * v * scale, axis=0, keepdims=True)
                d = (
                    k.cot[rows, :].astype(F32)
                    + scale * scaled
                    - v * (scale * scale * scale) * jnp.mean(scaled * v, axis=-1, keepdims=True)
                )
                k.own[rows, :] = d
                k.dmx[rows, :] = d.astype(BF)

            post(N.dmx_c, At(k.dmx)[pl.ds(0, span)], At(k.dmx)[pl.ds(span, span)], to_c)

        def mb2():
            @functools.partial(loop, width // 256)
            def _(j):
                cols = block(j, 256)
                d = dot_nt(k.dmx[:span, :], k.wout[cols, :])
                valid = mask(MASK_VALID)
                k.dc[:span, cols] = (valid * k.gc[:, cols] * d).astype(BF).astype(F32)
                c_cols = pl.ds(pl.multiple_of(width + j * 256, 256), 256)
                k.dpj[:span, c_cols] = (valid * conv_of(cols) * d).astype(BF)

            post(N.halo2, At(k.dc)[pl.ds(0, 8)], k.hr2, before, not_first)

        def mb3():
            @pl.when(s == 3)
            def _():
                k.dc[span:, :] = jnp.zeros((8, width), F32)

            @pl.when(not_last)
            def _():
                arrived(N.halo2, k.hr2)
                k.dc[span:, :] = k.hr2[...]

            @functools.partial(loop, width // 256, unroll=False)
            def _(j):
                cols = block(j, 256)
                d0 = k.dc[:span, cols]
                d = (
                    tap(0, cols) * mask(MASK_S0) * d0
                    + tap(1, cols) * mask(MASK_N1) * k.dc[1 : 1 + span, cols]
                    + tap(2, cols) * mask(MASK_N2) * k.dc[2 : 2 + span, cols]
                )
                valid = mask(MASK_VALID)
                k.dpj[:span, cols] = (valid * k.va[:, cols].astype(F32) * d).astype(BF)
                x_cols = pl.ds(pl.multiple_of(2 * width + j * 256, 256), 256)
                k.dpj[:span, x_cols] = (valid * k.gb[:, cols].astype(F32) * d).astype(BF)
                for i, m in ((0, MASK_S0), (1, MASK_S1), (2, MASK_S2)):
                    k.sg[2 + i : 3 + i, cols] = jnp.sum(
                        d0 * mask(m) * k.mix[8 - i : 8 - i + span, cols], axis=0, keepdims=True
                    )

            post(N.dpj_c, At(k.dpj)[pl.ds(0, span)], At(k.dpj)[pl.ds(span, span)], to_c)

        def mb4():
            got_win.wait()

            @functools.partial(loop, width // 256)
            def _(j):
                cols = block(j, 256)
                k.gc[:, cols] = dot_nt(k.dpj[:span, :], win[cols, :])

            @functools.partial(loop, passes, unroll=False)
            def _(i):
                rows = block(i, step)
                d = k.gc[rows, :]
                t = k.tok[rows, :].astype(F32)
                scale = k.sc1[rows, :]
                scaled = gain(k.gain1) * d
                k.sg[0:1, :] = k.sg[0:1, :] + jnp.sum(d * t * scale, axis=0, keepdims=True)
                d = (
                    k.own[rows, :]
                    + scale * scaled
                    - t * (scale * scale * scale) * jnp.mean(scaled * t, axis=-1, keepdims=True)
                )
                k.tok[rows, :] = d.astype(BF)

            put(k.tok, k.grad_tokens.at[0])
            for i in range(1, 8):
                post(N.sa(i), At(k.sg)[:, small_cols[i]], At(k.sa)[i - 1], (row_peers[i], s))
            for name, ref in (
                (N.nrm_c, k.nrm),
                (N.gat_c, k.gat),
                (N.dmx_c, k.dmx),
                (N.dpj_c, k.dpj),
            ):
                arrived(name, At(ref)[pl.ds(span, span)])

        def mg(rel_x, rel_y):
            rho = 4 * chosen(rel_y, y) + 2 * chosen(rel_x, x) + c
            rows = block(rho, slim)
            for a in range(2):
                for b in range(2):
                    sigma = 2 * chosen(b, z1) + chosen(a, z0)
                    first = dot_tn(k.nrm[:, rows], k.dpj[:, block(sigma, wide)])
                    second = dot_tn(k.gat[:, rows], k.dmx[:, block(sigma, side)])
                    for tag in MIXED:
                        u = unit_index(tag, {N.x: rel_x, N.y: rel_y, N.z0: a, N.z1: b})
                        own = travels[tag].own
                        own[u, :, :wide] = first[shares[tag]].astype(BF)
                        own[u, :, wide:] = second[shares[tag]].astype(BF)

        def finish_mixed():
            for tag in MIXED:
                got, at = travels[tag].got, travels[tag].starts[-1]
                rows = pl.ds(shares[tag].start, shares[tag].stop - shares[tag].start)
                put(At(got)[at, :, pl.ds(0, wide)], At(k.g_in)[rows, :])
                put(At(got)[at, :, pl.ds(wide, width - wide)], At(k.g_out)[rows, :])

        steps.update({N.mb(1): mb1, N.mb(2): mb2, N.mb(3): mb3, N.mb(4): mb4})
        for a in range(2):
            for b in range(2):
                steps[N.mg(a, b)] = functools.partial(mg, a, b)
        for name in ORDER[feed_end:]:
            steps[name]()
        finish_mixed()
        for name in list(pending):
            left(name)
        for cond, copy in stored:
            when(cond, lambda: copy().wait())

    pl.run_scoped(
        mixer_backward,
        pltpu.VMEM((width, 3 * width), BF),
        *[pltpu.VMEM((16, shares[tag].stop - shares[tag].start, width), BF) for tag in MIXED],
    )


def finish_kernel(n, *refs):
    sources, small = refs[:n], refs[n]
    targets, smalls = refs[n + 1 : 2 * n + 1], refs[2 * n + 1 : 2 * n + 4]
    rest = refs[2 * n + 4 :]
    held, wide, gets, puts = rest[:n], rest[n : 2 * n], rest[2 * n], rest[2 * n + 1]
    copies = [pltpu.make_async_copy(sources[i], held[i], gets.at[i]) for i in range(n)]
    for copy in copies:
        copy.start()
    s = lax.axis_index("seq")
    piece = smalls[0].shape[-1]
    value = jnp.zeros((8, piece), F32)
    for i in range(small.shape[1] // piece):
        value = jnp.where(s == i, small[:, i * piece : (i + 1) * piece], value)
    smalls[0][...] = value[0:1]
    smalls[1][...] = value[2:5]
    smalls[2][...] = value[1:2]
    out = []
    for i in range(n):
        copies[i].wait()
        ref = held[i]
        if sources[i].dtype != targets[i].dtype:
            rows = 64

            @functools.partial(loop, ref.shape[0] // rows, unroll=False)
            def _(j):
                here = block(j, rows)
                wide[i][here, :] = ref[here, :].astype(F32)

            ref = wide[i]
        copy = pltpu.make_async_copy(ref, targets[i], puts.at[i])
        copy.start()
        out.append(copy)
    for copy in out:
        copy.wait()


def fused(
    tokens,
    doc_lengths,
    valid_counts,
    norm_in,
    w_in,
    w_conv,
    w_out,
    norm_ffn,
    w_gate,
    w_up,
    w_down,
    cotangent,
):
    _, span, width = tokens.shape
    ff = w_gate.shape[1]
    rows, seq = lax.axis_size("rows"), lax.axis_size("seq")
    scratch = scratch_list(span, width, ff, rows, seq)
    anywhere = pl.BlockSpec(memory_space=pl.ANY)
    scalars = pl.BlockSpec(memory_space=pltpu.SMEM)
    vectors = pl.BlockSpec(memory_space=pltpu.VMEM)
    grads = [
        (width // rows, 3 * width // seq),
        (width // rows, width // seq),
        (width // rows, ff // seq),
        (width // rows, ff // seq),
        (ff // rows, width // seq),
    ]
    *outs, small = pl.pallas_call(
        functools.partial(layer_kernel, OPERANDS + list(scratch)),
        out_shape=[jax.ShapeDtypeStruct((1, span, width), BF)] * 2
        + [jax.ShapeDtypeStruct(shape, BF) for shape in grads]
        + [jax.ShapeDtypeStruct((8, width // rows), F32)],
        in_specs=[scalars] * 2 + [anywhere] * 2 + [vectors] * 3 + [anywhere] * 5,
        out_specs=[anywhere] * 8,
        scratch_shapes=list(scratch.values()),
        compiler_params=pltpu.CompilerParams(
            collective_id=0, has_side_effects=True, vmem_limit_bytes=67043328
        ),
        name="layer",
    )(
        doc_lengths,
        valid_counts,
        tokens,
        cotangent,
        norm_in,
        w_conv,
        norm_ffn,
        w_in,
        w_out,
        w_gate,
        w_up,
        w_down,
    )
    piece = width // (rows * seq)
    n = len(outs)
    held = [(1, span, width)] * 2 + grads
    *final, first, taps, second = pl.pallas_call(
        functools.partial(finish_kernel, n),
        out_shape=[jax.ShapeDtypeStruct((1, span, width), BF)] * 2
        + [jax.ShapeDtypeStruct(shape, F32) for shape in grads]
        + [jax.ShapeDtypeStruct((i, piece), F32) for i in (1, 3, 1)],
        in_specs=[anywhere] * n + [vectors],
        out_specs=[anywhere] * n + [vectors] * 3,
        scratch_shapes=[pltpu.VMEM(shape, BF) for shape in held]
        + [pltpu.VMEM(shape if i > 1 else (8, 128), F32) for i, shape in enumerate(held)]
        + [pltpu.SemaphoreType.DMA((n,))] * 2,
        name="finish",
    )(*outs, small)
    layer_out, grad_tokens, g_in, g_out, g_gate, g_up, g_down = final
    return (
        layer_out,
        grad_tokens,
        first[0],
        g_in,
        taps,
        g_out,
        second[0],
        g_gate,
        g_up,
        g_down,
    )


def solution(mesh):
    placed = (
        P("rows", "seq", None),
        P("rows", None),
        P("rows"),
        P(),
        P(),
        P(),
        P(),
        P(),
        P(),
        P(),
        P(),
        P("rows", "seq", None),
    )
    paired = mesh.shape["rows"] == 8 and mesh.shape["seq"] == 4
    return jax.shard_map(
        fused if paired else plain,
        mesh=mesh,
        in_specs=placed,
        out_specs=(
            P("rows", "seq", None),
            P("rows", "seq", None),
            P(("rows", "seq")),
            P("rows", "seq"),
            P(None, ("rows", "seq")),
            P("rows", "seq"),
            P(("rows", "seq")),
            P("rows", "seq"),
            P("rows", "seq"),
            P("rows", "seq"),
        ),
        check_vma=False,
    )
```

```python
import functools

import jax
import jax.numpy as jnp
import numpy as np
from jax import lax
from jax.experimental import pallas as pl
from jax.experimental.pallas import tpu as pltpu
from jax.sharding import PartitionSpec as P

EPSILON = 1e-05
BF = jnp.bfloat16
F32 = jnp.float32
MESH = pl.DeviceIdType.MESH


def passed_along(value, axis, steps):
    count = lax.axis_size(axis)
    first, last = (max(0, -steps), min(count, count - steps))
    return lax.ppermute(value, axis, [(source, source + steps) for source in range(first, last)])


def rms_scale(values):
    return lax.rsqrt(jnp.mean(values * values, axis=-1, keepdims=True) + EPSILON)


def doc_masks(lengths, positions):
    starts = jnp.cumsum(lengths) - lengths
    within = starts[None, :] <= positions[:, None]
    first = jnp.max(jnp.where(within, starts[None, :], 0), axis=1)
    return [(positions - offset >= first).astype(jnp.float32)[:, None] for offset in range(3)]


def weight_grad(left, right):
    return jnp.einsum("ta,tb->ab", left, right, preferred_element_type=jnp.float32)


def back_product(grad, weight):
    return jnp.einsum("tb,ab->ta", grad, weight, preferred_element_type=jnp.float32)


def scattered(value, row_dim, seq_dim):
    part = lax.psum_scatter(value.astype(BF), "rows", scatter_dimension=row_dim, tiled=True)
    part = lax.psum_scatter(part, "seq", scatter_dimension=seq_dim, tiled=True)
    return part.astype(F32)


def plain(
    tokens,
    doc_lengths,
    valid_counts,
    norm_in,
    w_in,
    w_conv,
    w_out,
    norm_ffn,
    w_gate,
    w_up,
    w_down,
    cotangent,
):
    inputs = tokens[0].astype(jnp.float32)
    span = inputs.shape[0]
    width = inputs.shape[1]
    start_pos = lax.axis_index("seq") * span
    positions = start_pos + jnp.arange(span + 2, dtype=jnp.int32)
    valid = (positions[:span] < valid_counts[0]).astype(jnp.float32)[:, None]
    same = doc_masks(doc_lengths[0], positions)
    taps = w_conv.astype(jnp.float32)
    gain_in = norm_in.astype(jnp.float32)
    gain_ffn = norm_ffn.astype(jnp.float32)
    scale1 = rms_scale(inputs)
    normed = (inputs * scale1 * gain_in).astype(jnp.bfloat16)
    proj = jnp.dot(normed, w_in, preferred_element_type=jnp.float32)
    gate_b = proj[:, :width]
    gate_c = proj[:, width : 2 * width]
    values = proj[:, 2 * width :]
    mixed_in = (valid * gate_b * values).astype(jnp.bfloat16)
    tail_rows = passed_along(mixed_in[span - 2 :], "seq", 1)
    padded = jnp.concatenate([tail_rows, mixed_in], axis=0).astype(jnp.float32)
    conv = jnp.zeros((span, width), jnp.float32)
    for offset in range(3):
        conv = conv + taps[offset] * same[offset][:span] * padded[2 - offset : 2 - offset + span]
    gated = (valid * gate_c * conv).astype(jnp.bfloat16)
    mixer_out = jnp.dot(gated, w_out, preferred_element_type=jnp.float32)
    resid = inputs + mixer_out
    scale2 = rms_scale(resid)
    normed2 = (resid * scale2 * gain_ffn).astype(jnp.bfloat16)
    gate_act = jnp.dot(normed2, w_gate, preferred_element_type=jnp.float32)
    up_act = jnp.dot(normed2, w_up, preferred_element_type=jnp.float32)
    sigmoid_gate = jax.nn.sigmoid(gate_act)
    silu_gate = gate_act * sigmoid_gate
    hidden = (silu_gate * up_act).astype(jnp.bfloat16)
    ffn_out = jnp.dot(hidden, w_down, preferred_element_type=jnp.float32)
    layer_out = (resid + valid * ffn_out).astype(jnp.bfloat16)
    grad_out = cotangent[0].astype(jnp.float32)
    d_ffn = (valid * grad_out).astype(jnp.bfloat16)
    grad_w_down = weight_grad(hidden, d_ffn)
    d_hidden = back_product(d_ffn, w_down)
    d_gate = (d_hidden * up_act * sigmoid_gate * (1.0 + gate_act * (1.0 - sigmoid_gate))).astype(
        jnp.bfloat16
    )
    d_up = (d_hidden * silu_gate).astype(jnp.bfloat16)
    grad_w_gate = weight_grad(normed2, d_gate)
    grad_w_up = weight_grad(normed2, d_up)
    d_normed2 = back_product(d_gate, w_gate) + back_product(d_up, w_up)
    grad_norm_ffn = jnp.sum(d_normed2 * resid * scale2, axis=0)
    scaled_ffn = gain_ffn * d_normed2
    d_resid = (
        grad_out
        + scale2 * scaled_ffn
        - resid * scale2**3 * jnp.mean(scaled_ffn * resid, axis=-1, keepdims=True)
    )
    d_mixer = d_resid.astype(jnp.bfloat16)
    grad_w_out = weight_grad(gated, d_mixer)
    d_gated = back_product(d_mixer, w_out)
    d_conv = (valid * gate_c * d_gated).astype(jnp.bfloat16)
    d_gate_c = valid * conv * d_gated
    head_rows = passed_along(d_conv[:2], "seq", -1)
    extended = jnp.concatenate([d_conv, head_rows], axis=0).astype(jnp.float32)
    d_mixed = jnp.zeros((span, width), jnp.float32)
    conv_rows = []
    for offset in range(3):
        d_mixed = (
            d_mixed
            + taps[offset] * same[offset][offset : offset + span] * extended[offset : offset + span]
        )
        conv_rows.append(
            jnp.sum(
                extended[:span] * same[offset][:span] * padded[2 - offset : 2 - offset + span],
                axis=0,
            )
        )
    grad_w_conv = jnp.stack(conv_rows, axis=0)
    d_proj = jnp.concatenate(
        [valid * values * d_mixed, d_gate_c, valid * gate_b * d_mixed], axis=1
    ).astype(jnp.bfloat16)
    grad_w_in = weight_grad(normed, d_proj)
    d_normed = back_product(d_proj, w_in)
    grad_norm_in = jnp.sum(d_normed * inputs * scale1, axis=0)
    scaled_in = gain_in * d_normed
    grad_tokens = (
        d_resid
        + scale1 * scaled_in
        - inputs * scale1**3 * jnp.mean(scaled_in * inputs, axis=-1, keepdims=True)
    )
    grad_tokens = grad_tokens.astype(jnp.bfloat16)
    return (
        layer_out[None],
        grad_tokens[None],
        scattered(grad_norm_in, 0, 0),
        scattered(grad_w_in, 0, 1),
        scattered(grad_w_conv, 1, 1),
        scattered(grad_w_out, 0, 1),
        scattered(grad_norm_ffn, 0, 0),
        scattered(grad_w_gate, 0, 1),
        scattered(grad_w_up, 0, 1),
        scattered(grad_w_down, 0, 1),
    )


def dot(a, b):
    return jnp.dot(a, b, preferred_element_type=F32)


def dot_nt(a, b):
    return lax.dot_general(a, b, (((1,), (1,)), ((), ())), preferred_element_type=F32)


def dot_tn(a, b):
    return lax.dot_general(a, b, (((0,), (0,)), ((), ())), preferred_element_type=F32)


def bit_of(value, weight):
    return lax.rem(lax.div(value, np.int32(weight)), np.int32(2))


def flipped(value, weights):
    for weight in (1, 2, 4):
        if weights & weight:
            value = value + weight - 2 * weight * bit_of(value, weight)
    return value


def loop(count, body, unroll=True):
    lax.fori_loop(0, count, lambda i, carry: (body(i), carry)[1], 0, unroll=unroll)


def block(index, size):
    return pl.ds(pl.multiple_of(index * size, size), size)


class Name(str):
    def __call__(self, *index):
        return (self,) + index


class Names:
    def __getattr__(self, name):
        return Name(name)


N = Names()

STAGES = {
    N.A: (N.x, N.y, N.z1),
    N.B: (N.y, N.z1, N.x),
    N.g0: (N.y, N.x, N.z1),
    N.g1: (N.y, N.x, N.z1),
    N.u0: (N.x, N.z1, N.y),
    N.u1: (N.x, N.y, N.z1),
    N.m0: (N.y, N.x, N.z0, N.z1),
    N.m1: (N.x, N.z0, N.y, N.z1),
    N.m2: (N.z0, N.x, N.z1, N.y),
}
ORDER = [
    N.ex(0), N.ex(1), N.re(1), N.tn(0), N.bk(1), N.ex(2, 0), N.re(0), N.bk(0),
    N.tn(1), N.tdf(0), N.ex(2, 1), N.ex(3, 0), N.ex(3, 1), N.dn(0), N.go(N.A, 0, 0), N.go(N.B, 0, 0),
    N.tdf(1), N.dn(1), N.go(N.B, 0, 1), N.tdf(2), N.tdf(3), N.re(2), N.dn(2), N.go(N.A, 0, 1),
    N.go(N.B, 0, 2), N.B(0, 0), N.go(N.B, 1, 0), N.re(3), N.bk(3), N.gg(0, 3), N.gg(0, 0), N.go(N.g0, 0, 0),
    N.gg(1, 0), N.go(N.g1, 0, 0), N.uu(0, 0), N.go(N.u0, 0, 0), N.B(0, 1), N.go(N.B, 1, 1), N.A(0, 0), N.go(N.A, 1, 0),
    N.bk(2), N.uu(1, 0), N.go(N.u1, 0, 0), N.dn(3), N.go(N.B, 0, 3), N.gg(0, 1), N.go(N.g0, 0, 1), N.uu(0, 3),
    N.gg(1, 1), N.go(N.g1, 0, 1), N.uu(0, 2), N.gg(1, 2), N.uu(1, 3), N.fo(1), N.uu(0, 1), N.go(N.u0, 0, 1),
    N.uu(1, 1), N.go(N.u1, 0, 1), N.uu(1, 2), N.B(0, 2), N.gg(1, 3), N.fo(3), N.u0(0, 0), N.go(N.u0, 1, 0),
    N.fo(2), N.u1(0, 0), N.go(N.u1, 1, 0), N.A(0, 1), N.go(N.A, 1, 1), N.B(1, 0), N.go(N.B, 2, 0), N.fo(0),
    N.gg(0, 2), N.g0(0, 0), N.go(N.g0, 1, 0), N.mb(1), N.mb(2), N.u0(0, 1), N.go(N.u0, 1, 1), N.u1(0, 1),
    N.B(0, 3), N.g1(0, 0), N.go(N.g1, 1, 0), N.g0(0, 1), N.u0(1, 0), N.go(N.u0, 2, 0), N.B(1, 1), N.mb(3),
    N.A(1, 0), N.go(N.A, 2, 0), N.mb(4), N.lo, N.mg(0, 0), N.go(N.m0, 0, 0), N.go(N.m1, 0, 0), N.go(N.m2, 0, 0),
    N.go(N.m0, 0, 1), N.go(N.m1, 0, 1), N.go(N.m0, 0, 2), N.go(N.m2, 0, 2), N.go(N.m0, 0, 3), N.go(N.m1, 0, 4), N.go(N.m1, 0, 5), N.g1(0, 1),
    N.mg(0, 1), N.go(N.m2, 0, 1), N.go(N.m1, 0, 2), N.go(N.m1, 0, 3), N.go(N.m2, 0, 3), N.go(N.m1, 0, 6), N.go(N.m1, 0, 7), N.mg(1, 0),
    N.go(N.m0, 0, 4), N.go(N.m2, 0, 4), N.go(N.m0, 0, 5), N.go(N.m0, 0, 6), N.go(N.m2, 0, 6), N.go(N.m0, 0, 7), N.B(2, 0), N.mg(1, 1),
    N.go(N.m2, 0, 5), N.go(N.m2, 0, 7), N.g0(1, 0), N.go(N.g0, 2, 0), N.sg(0), N.dl(1), N.u1(1, 0), N.go(N.u1, 2, 0),
    N.m2(0, 6), N.A(1, 1), N.A(2, 0), N.dl(0), N.u0(1, 1), N.g1(1, 0), N.go(N.g1, 2, 0), N.m2(0, 0),
    N.go(N.m2, 1, 0), N.m1(0, 0), N.go(N.m1, 1, 0), N.m2(0, 3), N.go(N.m2, 1, 3), N.m2(0, 1), N.go(N.m2, 1, 1), N.m1(0, 1),
    N.go(N.m1, 1, 1), N.m2(0, 4), N.m2(0, 2), N.go(N.m2, 1, 2), N.m2(0, 5), N.m1(0, 4), N.m1(0, 7), N.m1(0, 5),
    N.m0(0, 0), N.go(N.m0, 1, 0), N.u0(2, 0), N.m1(0, 2), N.go(N.m1, 1, 2), N.m0(0, 1), N.go(N.m0, 1, 1), N.sg(1),
    N.u1(2, 0), N.m1(0, 3), N.go(N.m1, 1, 3), N.m0(0, 2), N.go(N.m0, 1, 2), N.m1(1, 0), N.go(N.m1, 2, 0), N.m1(1, 1),
    N.go(N.m1, 2, 1), N.m2(0, 7), N.w3(N.u), N.m2(1, 0), N.go(N.m2, 2, 0), N.w4(N.u), N.m0(0, 3), N.go(N.m0, 1, 3),
    N.m1(0, 6), N.m2(1, 1), N.go(N.m2, 2, 1), N.m1(1, 2), N.m2(1, 3), N.m0(0, 4), N.dt, N.g1(2, 0),
    N.m0(1, 0), N.go(N.m0, 2, 0), N.m1(1, 3), N.m2(1, 2), N.g0(2, 0), N.m2(2, 0), N.go(N.m2, 3, 0), N.m0(0, 5),
    N.m2(2, 1), N.m0(0, 6), N.m0(1, 1), N.go(N.m0, 2, 1), N.m0(1, 2), N.m0(2, 0), N.go(N.m0, 3, 0), N.m1(2, 0),
    N.go(N.m1, 3, 0), N.m0(0, 7), N.w3(N.g), N.m2(3, 0), N.m0(1, 3), N.m1(2, 1), N.w4(N.g), N.m0(2, 1),
    N.m0(3, 0), N.m1(3, 0),
]
FEED = (N.ex, N.re, N.bk, N.dn, N.gg, N.uu, N.fo)
EIGHTHS = {N.m0: 6, N.m1: 1, N.m2: 1}
MIXED = list(EIGHTHS)
DOWN = [N.A, N.B]
GATE = [N.g0, N.g1]
UP = [N.u0, N.u1]
N_SEM = 192
MASK_VALID, MASK_S0, MASK_S1, MASK_S2, MASK_N1, MASK_N2 = range(6)


def scatter_of(tag):
    return (N.x, N.y, N.z0, N.z1) if tag in MIXED else (N.x, N.z1) if tag in DOWN else (N.x, N.y)


def counts_of(tag):
    counts = [2 ** len(scatter_of(tag))]
    for dim in STAGES[tag]:
        counts.append(counts[-1] // 2 if dim in scatter_of(tag) else counts[-1])
    return counts


def unit_index(tag, rel):
    index = 0
    for dim in STAGES[tag]:
        if dim in scatter_of(tag):
            index = 2 * index + rel[dim]
    return index


def unit_bits(tag, index):
    dims = [dim for dim in STAGES[tag] if dim in scatter_of(tag)]
    return {dim: (index >> (len(dims) - 1 - i)) & 1 for i, dim in enumerate(dims)}


def unit_shape(tag, width, ff, rows, seq):
    if tag in DOWN:
        return ff // rows, width // seq
    if tag in MIXED:
        return width // rows * EIGHTHS[tag] // 8, width
    return width // rows, ff // 4


def scratch_list(span, width, ff, rows, seq):
    group = 4 * span
    shapes = dict(
        tok=pltpu.VMEM((span, width), BF),
        cot=pltpu.VMEM((span, width), BF),
        wout=pltpu.VMEM((width, width), BF),
        nrm=pltpu.VMEM((2 * span, width), BF),
        gat=pltpu.VMEM((2 * span, width), BF),
        dmx=pltpu.VMEM((2 * span, width), BF),
        dpj=pltpu.VMEM((2 * span, 3 * width), BF),
        gb=pltpu.VMEM((span, width), BF),
        va=pltpu.VMEM((span, width), BF),
        gc=pltpu.VMEM((span, width), F32),
        mix=pltpu.VMEM((span + 8, width), F32),
        dc=pltpu.VMEM((span + 8, width), F32),
        res=pltpu.VMEM((span, width), F32),
        own=pltpu.VMEM((span, width), F32),
        loa=pltpu.VMEM((span, width), F32),
        mask=pltpu.VMEM((span, 128), F32),
        sc1=pltpu.VMEM((span, 1), F32),
        sc2=pltpu.VMEM((span, 1), F32),
        n2=pltpu.VMEM((group, width), BF),
        df=pltpu.VMEM((group, width), BF),
        hr=pltpu.VMEM((8, width), F32),
        hr2=pltpu.VMEM((8, width), F32),
        ps=pltpu.VMEM((2, span, width), BF),
        pr=pltpu.VMEM((2, span, width), BF),
        pz=pltpu.VMEM((span, width), BF),
        fr=pltpu.VMEM((2, span, width), BF),
        fz=pltpu.VMEM((span, width), BF),
        sg=pltpu.VMEM((8, width), F32),
        sa=pltpu.VMEM((rows - 1, 8, width // rows), F32),
        ss=pltpu.VMEM((8, width // rows), F32),
        sb=pltpu.VMEM((seq - 1, 8, width // rows), F32),
        rd4=pltpu.VMEM(unit_shape(N.A, width, ff, rows, seq), BF),
        rg4=pltpu.VMEM(unit_shape(N.g0, width, ff, rows, seq), BF),
        ru4=pltpu.VMEM(unit_shape(N.u0, width, ff, rows, seq), BF),
        send=pltpu.SemaphoreType.DMA((N_SEM,)),
        recv=pltpu.SemaphoreType.DMA((N_SEM,)),
        local=pltpu.SemaphoreType.DMA((32,)),
    )
    for tag in STAGES:
        unit = unit_shape(tag, width, ff, rows, seq)
        counts = counts_of(tag)
        if tag not in MIXED:
            shapes[N.own, tag] = pltpu.VMEM((counts[0],) + unit, BF)
        shapes[N.got, tag] = pltpu.VMEM((sum(counts[1:]),) + unit, BF)
    return shapes


OPERANDS = [
    N.lengths,
    N.counts,
    N.tokens,
    N.cotangent,
    N.gain1,
    N.taps,
    N.gain2,
    N.w_in,
    N.w_out,
    N.w_gate,
    N.w_up,
    N.w_down,
    N.layer_out,
    N.grad_tokens,
    N.g_in,
    N.g_out,
    N.g_gate,
    N.g_up,
    N.g_down,
    N.small,
]


class Refs:
    pass


class View:
    def __init__(self, ref, index):
        self.ref, self.index = ref, index

    def take(self):
        return self.ref.at[self.index]


class At:
    def __init__(self, ref):
        self.ref = ref

    def __getitem__(self, index):
        return View(self.ref, index)


def taken(ref):
    return ref.take() if isinstance(ref, View) else ref


def layer_kernel(names, *refs):
    k = Refs()
    travelling = {}
    for name, ref in zip(names, refs):
        if isinstance(name, tuple):
            travelling[name] = ref
        else:
            setattr(k, name, ref)
    span, width = k.tok.shape
    slim, quarter = k.rg4.shape
    tall, side = k.rd4.shape
    wide = 3 * width // 4

    r = lax.axis_index("rows")
    s = lax.axis_index("seq")
    c, x, y = bit_of(r, 1), bit_of(r, 2), bit_of(r, 4)
    z0, z1 = bit_of(s, 1), bit_of(s, 2)
    row_peers = [flipped(r, i) for i in range(8)]
    seq_peers = [flipped(s, i) for i in range(4)]
    to_c = (row_peers[1], s)
    to_z = (r, seq_peers[1])
    to_dim = {
        N.x: (row_peers[2], s),
        N.y: (row_peers[4], s),
        N.z0: to_z,
        N.z1: (r, seq_peers[2]),
    }
    partners = [(row, s) for row in row_peers[1:]] + [(r, seq) for seq in seq_peers[1:]]
    partners += [(row_peers[2], seq_peers[1]), (row_peers[3], seq_peers[1])]
    after = (r, lax.rem(s + 1, np.int32(4)))
    before = (r, lax.rem(s + 3, np.int32(4)))
    df_cols = [block(2 * (z1 if w else 1 - z1) + (x if v else 1 - x), side) for w in (0, 1) for v in (0, 1)]
    active, idle = c == y, c != y
    holder, lender = c == z1, c != z1
    not_last, not_first = s < 3, s > 0
    home = [jnp.logical_and(active, jnp.logical_and(x == z0, y == i)) for i in range(2)]
    gives = [jnp.logical_and(active, jnp.logical_not(home[i])) for i in range(2)]
    targets = [(4 * y + 2 * z0 + i, 2 * z1 + x) for i in range(2)]
    away = jnp.logical_not(jnp.logical_and(active, x == z0))
    away_at = [jnp.logical_and(away, c == i) for i in range(2)]
    core_is = [c == 0, c == 1]
    holds = [jnp.logical_and(holder, c == i) for i in range(2)]
    small_cols = [block(row, slim) for row in row_peers]

    sems = {}
    pending = {}

    def remote(name, src, dst, device):
        at = sems.setdefault(name, len(sems))
        assert at < N_SEM
        return pltpu.make_async_remote_copy(
            src_ref=taken(src),
            dst_ref=taken(dst),
            send_sem=k.send.at[at],
            recv_sem=k.recv.at[at],
            device_id=device,
            device_id_type=MESH,
        )

    def when(cond, go):
        if cond is None:
            go()
        else:
            pl.when(cond)(go)

    def post(name, src, dst, device, cond=None):
        when(cond, lambda: remote(name, src, dst, device).start())
        pending[name] = cond, (name, src, dst, device)

    def left(name):
        cond, args = pending.pop(name)
        when(cond, lambda: remote(*args).wait_send())

    def arrived(name, dst):
        remote(name, dst, dst, to_c).wait_recv()

    local_count = [0]

    def local_copy(src, dst):
        at = local_count[0]
        local_count[0] += 1
        return pltpu.make_async_copy(taken(src), taken(dst), k.local.at[at])

    def fetch(src, dst):
        copy = local_copy(src, dst)
        copy.start()
        return copy

    stored = []

    def put(src, dst, cond=None):
        at = local_count[0]
        local_count[0] += 1

        def copy():
            return pltpu.make_async_copy(taken(src), taken(dst), k.local.at[at])

        when(cond, lambda: copy().start())
        stored.append((cond, copy))

    def add(dst, src):
        dst[...] = (dst[...].astype(F32) + src[...].astype(F32)).astype(BF)

    def chosen(rel, bit):
        return bit if rel else 1 - bit

    class Travel:
        def __init__(self, tag, own):
            self.tag, self.own, self.order = tag, own, STAGES[tag]
            self.counts = counts_of(tag)
            self.got = travelling[N.got, tag]
            self.starts = [sum(self.counts[1 : p + 1]) for p in range(len(self.order))]
            self.alive = active if tag in DOWN else holder
            self.role_at = len(self.order)
            for p, dim in enumerate(self.order):
                if dim not in scatter_of(tag):
                    self.role_at = p

        def held(self, p, i):
            return (self.own, i) if p == 0 else (self.got, self.starts[p - 1] + i)

        def leave(self, p, i):
            if p == len(self.order):
                return
            dim = self.order[p]
            ref, at = self.held(p, i)
            cond = None
            if dim in scatter_of(self.tag):
                if i >= self.counts[p] // 2:
                    return
                if p > self.role_at:
                    cond = self.alive
            else:
                cond = idle if self.tag in DOWN else lender
            post((self.tag, p, i), At(ref)[at], At(self.got)[self.starts[p] + i], to_dim[dim], cond)

        def step(self, p, i):
            at = self.starts[p] + i
            halved = self.order[p] in scatter_of(self.tag)
            ref, mine = self.held(p, i + (self.counts[p + 1] if halved else 0))

            def go():
                arrived((self.tag, p, i), At(self.got)[at])
                add(self.got.at[at], ref.at[mine])

            when(self.alive if p >= self.role_at else None, go)

        def last(self):
            return At(self.got)[self.starts[-1]]

    travels = {tag: Travel(tag, travelling.get((N.own, tag))) for tag in STAGES}
    steps = {}
    for tag, travel in travels.items():
        for p in range(len(travel.order)):
            for i in range(travel.counts[p + 1]):
                steps[tag, p, i] = functools.partial(travel.step, p, i)
        for p in range(len(travel.order)):
            for i in range(travel.counts[p]):
                steps[N.go, tag, p, i] = functools.partial(travel.leave, p, i)

    got_tok = fetch(k.tokens.at[0], k.tok)
    got_cot = fetch(k.cotangent.at[0], k.cot)
    barrier = pltpu.get_barrier_semaphore()
    for device in partners:
        pl.semaphore_signal(barrier, inc=1, device_id=device, device_id_type=MESH)

    position = s * span + lax.broadcasted_iota(jnp.int32, (span, 1), 0)
    starts = [np.int32(0)]
    for i in range(k.lengths.shape[1] - 1):
        starts.append(starts[-1] + k.lengths[0, i])

    def first_of(at):
        first = jnp.zeros_like(at)
        for start in starts:
            first = jnp.maximum(first, jnp.where(start <= at, start, 0))
        return first

    def flag(test):
        return jnp.where(test, 1.0, 0.0).astype(F32)

    def write_masks():
        first0, first1, first2 = (first_of(position + i) for i in range(3))
        columns = [
            flag(position < k.counts[0]),
            flag(position >= first0),
            flag(position - 1 >= first0),
            flag(position - 2 >= first0),
            flag(position >= first1),
            flag(position >= first2),
        ]
        lane = lax.broadcasted_iota(jnp.int32, (span, 128), 1)
        table = jnp.zeros((span, 128), F32)
        for i, column in enumerate(columns):
            table = jnp.where(lane == i, column, table)
        k.mask[...] = table

    def mask(i, rows=slice(None)):
        return k.mask[rows, i : i + 1]

    def gain(ref):
        return ref[...].astype(F32).reshape(1, width)

    step = 64
    passes = span // step
    part = span // 2

    def send_df(i):
        cols = df_cols[i]
        src, dst = At(k.df)[pl.ds(0, span), cols], At(k.df)[pl.ds(2 * span, span), cols]
        post(N.df_z(i), src, dst, to_z)

    def mixer_forward(win):
        got_win = [fetch(k.w_in.at[:, block(i, width)], win.at[:, block(i, width)]) for i in (0, 2, 1)]
        got_wout = fetch(k.w_out, k.wout)
        write_masks()
        got_tok.wait()

        @functools.partial(loop, passes, unroll=False)
        def _(i):
            rows = block(i, step)
            t = k.tok[rows, :].astype(F32)
            scale = lax.rsqrt(jnp.mean(t * t, axis=-1, keepdims=True) + EPSILON)
            k.sc1[rows, :] = scale
            k.nrm[rows, :] = (t * scale * gain(k.gain1)).astype(BF)

        got_cot.wait()

        @functools.partial(loop, passes, unroll=False)
        def _(i):
            rows = block(i, step)
            k.df[rows, :] = (mask(MASK_VALID, rows) * k.cot[rows, :].astype(F32)).astype(BF)

        pl.semaphore_wait(barrier, len(partners))
        send_df(0)
        post(N.df_c, At(k.df)[pl.ds(0, span)], At(k.df)[pl.ds(span, span)], to_c)
        got_win[0].wait()
        got_win[1].wait()

        @functools.partial(loop, width // 256)
        def _(j):
            n = k.nrm[:span, :]
            cols = block(j, 256)
            gb = dot(n, win[:, cols])
            va = dot(n, win[:, pl.ds(pl.multiple_of(2 * width + j * 256, 256), 256)])
            k.gb[:, cols] = gb.astype(BF)
            k.va[:, cols] = va.astype(BF)
            k.mix[8:, cols] = (mask(MASK_VALID) * gb * va).astype(BF).astype(F32)

        post(N.halo, At(k.mix)[pl.ds(span, 8)], k.hr, after, not_last)
        got_win[2].wait()

        @functools.partial(loop, width // 256)
        def _(j):
            cols = block(j, 256)
            c_cols = pl.ds(pl.multiple_of(width + j * 256, 256), 256)
            k.gc[:, cols] = dot(k.nrm[:span, :], win[:, c_cols])

        got_wout.wait()

    pl.run_scoped(mixer_forward, pltpu.VMEM((width, 3 * width), BF))

    @pl.when(s == 0)
    def _():
        k.mix[:8, :] = jnp.zeros((8, width), F32)

    @pl.when(not_first)
    def _():
        arrived(N.halo, k.hr)
        k.mix[:8, :] = k.hr[...]

    def tap(i, cols):
        return k.taps[i : i + 1, cols].astype(F32)

    def conv_of(cols):
        return (
            tap(0, cols) * mask(MASK_S0) * k.mix[8 : 8 + span, cols]
            + tap(1, cols) * mask(MASK_S1) * k.mix[7 : 7 + span, cols]
            + tap(2, cols) * mask(MASK_S2) * k.mix[6 : 6 + span, cols]
        )

    @functools.partial(loop, width // 256, unroll=False)
    def _(j):
        cols = block(j, 256)
        k.gat[:span, cols] = (mask(MASK_VALID) * k.gc[:, cols] * conv_of(cols)).astype(BF)

    @functools.partial(loop, width // 256)
    def _(j):
        cols = block(j, 256)
        k.res[:, cols] = k.tok[:, cols].astype(F32) + dot(k.gat[:span, :], k.wout[:, cols])

    for i in range(2):

        @functools.partial(loop, passes // 2, unroll=False)
        def _(j):
            rows = block(i * (passes // 2) + j, step)
            v = k.res[rows, :]
            scale = lax.rsqrt(jnp.mean(v * v, axis=-1, keepdims=True) + EPSILON)
            k.sc2[rows, :] = scale
            k.n2[rows, :] = (v * scale * gain(k.gain2)).astype(BF)

        here = pl.ds(i * part, part)
        post(N.n2_z(i), At(k.n2)[here], At(k.n2)[pl.ds(2 * span + i * part, part)], to_z)
    post(N.n2_c, At(k.n2)[pl.ds(0, span)], At(k.n2)[pl.ds(span, span)], to_c)
    for i in (1, 2, 3):
        send_df(i)
    post(N.nrm_c, At(k.nrm)[pl.ds(0, span)], At(k.nrm)[pl.ds(span, span)], to_c)
    post(N.gat_c, At(k.gat)[pl.ds(0, span)], At(k.gat)[pl.ds(span, span)], to_c)

    z_rows, t_rows = pl.ds(2 * span, span), pl.ds(3 * span, span)
    z_parts = [pl.ds(2 * span + i * part, part) for i in range(2)]
    t_parts = [pl.ds(3 * span + i * part, part) for i in range(2)]

    def pass_df(i):
        arrived(N.df_z(i), At(k.df)[z_rows, df_cols[i]])
        post(N.df_t(i), At(k.df)[z_rows, df_cols[i]], At(k.df)[t_rows, df_cols[i]], to_c)

    def pass_n2(i):
        arrived(N.n2_z(i), At(k.n2)[z_parts[i]])
        post(N.n2_t(i), At(k.n2)[z_parts[i]], At(k.n2)[t_parts[i]], to_c)

    for i in range(4):
        steps[N.tdf(i)] = functools.partial(pass_df, i)
    for i in range(2):
        steps[N.tn(i)] = functools.partial(pass_n2, i)

    def down_last(i):
        got = travels[DOWN[i]].last()
        post(N.rd4(i), got, k.rd4, targets[i], gives[i])
        put(got, k.g_down, home[i])

    def down_take():
        for i in range(2):
            when(away_at[i], lambda: arrived(N.rd4(i), k.rd4))
        put(k.rd4, k.g_down, away)

    def wide_last(tag):
        mine, out = (k.rg4, k.g_gate) if tag == N.g else (k.ru4, k.g_up)
        for core in range(2):
            got = travels[(GATE if tag == N.g else UP)[core]].last()
            post((tag, core), got, mine, to_c, holds[1 - core])
            put(got, out, holds[core])

    lends = [jnp.logical_and(lender, c == i) for i in range(2)]

    def wide_take(tag):
        mine, out = (k.rg4, k.g_gate) if tag == N.g else (k.ru4, k.g_up)
        for core in range(2):
            when(lends[core], lambda: arrived((tag, core), mine))
        put(mine, out, lender)

    for i in range(2):
        steps[N.dl(i)] = functools.partial(down_last, i)
    steps[N.dt] = down_take
    for tag in (N.g, N.u):
        steps[N.w3(tag)] = functools.partial(wide_last, tag)
        steps[N.w4(tag)] = functools.partial(wide_take, tag)

    def small_rows():
        total = k.sg[:, small_cols[0]]
        for i in range(1, 8):
            arrived(N.sa(i), At(k.sa)[i - 1])
            total = total + k.sa[i - 1]
        k.ss[...] = total
        for i in range(1, 4):
            post(N.sb(i), k.ss, At(k.sb)[i - 1], (r, seq_peers[i]))

    def small_seq():
        total = k.ss[...]
        for i in range(1, 4):
            arrived(N.sb(i), At(k.sb)[i - 1])
            left(N.sb(i))
            total = total + k.sb[i - 1]
        k.ss[...] = total
        put(k.ss, k.small)

    steps[N.sg(0)], steps[N.sg(1)] = small_rows, small_seq

    def layer_output():
        arrived(N.fz, k.fz)

        @functools.partial(loop, passes, unroll=False)
        def _(i):
            rows = block(i, step)
            valid = mask(MASK_VALID, rows)
            k.cot[rows, :] = (k.loa[rows, :] + valid * k.fz[rows, :].astype(F32)).astype(BF)

        put(k.cot, k.layer_out.at[0])

    steps[N.lo] = layer_output
    feed_end = 1 + max(i for i, name in enumerate(ORDER) if name[0] in FEED)

    def feed_forward(wg, wu, wd, hid, dg, du):
        q = 2 * c + z0
        got_wg = fetch(k.w_gate.at[:, block(q, quarter)], wg)
        got_wu = fetch(k.w_up.at[:, block(q, quarter)], wu)
        got_wd = fetch(k.w_down.at[block(q, quarter), :], wd)

        def tiles(body, unroll):
            loop(quarter // 256, lambda j: body(block(j, 256)), unroll)
            if quarter % 256:
                body(pl.ds(quarter - quarter % 256, quarter % 256))

        def expand(rows, unroll):
            def tile(cols):
                n = k.n2[rows, :]
                g = dot(n, wg[:, cols])
                u = dot(n, wu[:, cols])
                sig = jax.nn.sigmoid(g)
                silu = g * sig
                hid[rows, cols] = (silu * u).astype(BF)
                dg[rows, cols] = (u * sig * (1.0 + g * (1.0 - sig))).astype(BF)
                du[rows, cols] = silu.astype(BF)

            tiles(tile, unroll)

        def retreat(slot, unroll):
            rows = pl.ds(slot * span, span)

            def tile(cols):
                d = dot_nt(k.df[rows, :], wd[cols, :])
                dg[rows, cols] = (d * dg[rows, cols].astype(F32)).astype(BF)
                du[rows, cols] = (d * du[rows, cols].astype(F32)).astype(BF)

            tiles(tile, unroll)

        def back(slot, ref, plus, unroll):
            rows = pl.ds(slot * span, span)

            @functools.partial(loop, width // 256, unroll=unroll)
            def _(j):
                cols = block(j, 256)
                value = dot_nt(dg[rows, :], wg[cols, :]) + dot_nt(du[rows, :], wu[cols, :])
                if plus is not None:
                    value = value + plus[:, cols].astype(F32)
                ref[:, cols] = value.astype(ref.dtype)

        def forth(slot, store):
            rows = pl.ds(slot * span, span)

            @functools.partial(loop, width // 256, unroll=False)
            def _(j):
                cols = block(j, 256)
                store(cols, dot(hid[rows, :], wd[:, cols]))

        own = steps

        waiting = [got_wd]

        def take_wd():
            while waiting:
                waiting.pop().wait()

        def ex0():
            got_wg.wait()
            got_wu.wait()
            expand(pl.ds(0, span), False)

        def ex1():
            arrived(N.n2_c, At(k.n2)[pl.ds(span, span)])
            expand(pl.ds(span, span), False)

        def re0():
            take_wd()
            retreat(0, False)

        def re1():
            take_wd()
            arrived(N.df_c, At(k.df)[pl.ds(span, span)])
            retreat(1, False)

        def bk1():
            back(1, k.ps.at[0], None, False)
            post(N.pr0, At(k.ps)[0], At(k.pr)[0], to_c)

        def bk0():
            arrived(N.pr0, At(k.pr)[0])
            back(0, k.own, k.pr.at[0], False)

        def ex2(i):
            expand(z_parts[i], True)

        def ex3(i):
            arrived(N.n2_t(i), At(k.n2)[t_parts[i]])
            expand(t_parts[i], True)

        def bk3():
            back(3, k.ps.at[1], None, True)
            post(N.pr1, At(k.ps)[1], At(k.pr)[1], to_c)

        def bk2():
            arrived(N.pr1, At(k.pr)[1])
            back(2, k.pr.at[1], k.pr.at[1], True)
            post(N.pz, At(k.pr)[1], k.pz, to_z)

        def wide_grad(tag, core, u, grad):
            travel = travels[tag]
            rel = unit_bits(tag, u)
            rho = 4 * chosen(rel[N.y], y) + 2 * chosen(rel[N.x], x) + core
            travel.own[u] = dot_tn(k.n2[:, block(rho, slim)], grad[...]).astype(BF)

        def to_ref(ref, plus=None):
            def store(cols, value):
                if plus is not None:
                    value = value + plus[:, cols].astype(F32)
                ref[:, cols] = value.astype(ref.dtype)

            return store

        def fo1():
            left(N.pr0)
            forth(1, to_ref(k.ps.at[0]))
            post(N.fr0, At(k.ps)[0], At(k.fr)[0], to_c)

        def fo3():
            left(N.pr1)
            forth(3, to_ref(k.ps.at[1]))
            post(N.fr1, At(k.ps)[1], At(k.fr)[1], to_c)

        def fo2():
            arrived(N.fr1, At(k.fr)[1])
            forth(2, to_ref(k.fr.at[1], k.fr.at[1]))
            post(N.fz, At(k.fr)[1], k.fz, to_z)

        def fo0():
            arrived(N.fr0, At(k.fr)[0])

            def store(cols, value):
                value = value + k.fr[0, :, cols].astype(F32)
                k.loa[:, cols] = k.res[:, cols] + mask(MASK_VALID) * value

            forth(0, store)

        own.update({N.ex(0): ex0, N.ex(1): ex1, N.re(0): re0, N.re(1): re1})
        own.update({N.bk(0): bk0, N.bk(1): bk1, N.bk(2): bk2, N.bk(3): bk3})
        own.update({N.fo(0): fo0, N.fo(1): fo1, N.fo(2): fo2, N.fo(3): fo3})
        own[N.re(2)] = functools.partial(retreat, 2, True)

        taken_df = set()

        def take_df(i):
            if i not in taken_df:
                taken_df.add(i)
                arrived(N.df_t(i), At(k.df)[t_rows, df_cols[i]])

        def re3():
            for i in range(4):
                take_df(i)
            retreat(3, True)

        def dn(i):
            take_df(i)
            rel = {N.x: i % 2, N.z1: i // 2}
            value = dot_tn(hid[...], k.df[:, df_cols[i]])
            for j, tag in enumerate(DOWN):
                travels[tag].own[unit_index(tag, rel)] = value[j * tall : (j + 1) * tall].astype(BF)

        own[N.re(3)] = re3
        for i in range(4):
            own[N.dn(i)] = functools.partial(dn, i)
        for i in range(2):
            own[N.ex(2, i)] = functools.partial(ex2, i)
            own[N.ex(3, i)] = functools.partial(ex3, i)
            for u in range(4):
                own[N.gg(i, u)] = functools.partial(wide_grad, GATE[i], i, u, dg)
                own[N.uu(i, u)] = functools.partial(wide_grad, UP[i], i, u, du)
        for name in ORDER[:feed_end]:
            own[name]()

    pl.run_scoped(
        feed_forward,
        pltpu.VMEM((width, quarter), BF),
        pltpu.VMEM((width, quarter), BF),
        pltpu.VMEM((quarter, width), BF),
        pltpu.VMEM((4 * span, quarter), BF),
        pltpu.VMEM((4 * span, quarter), BF),
        pltpu.VMEM((4 * span, quarter), BF),
    )

    shares, start = {}, 0
    for tag in MIXED:
        size = unit_shape(tag, slim * 8, 0, 8, 4)[0]
        shares[tag] = slice(start, start + size)
        start += size

    def mixer_backward(win, *own_mixed):
        got_win = fetch(k.w_in, win)
        for tag, own in zip(MIXED, own_mixed):
            travels[tag].own = own

        def mb1():
            arrived(N.pz, k.pz)
            k.sg[...] = jnp.zeros((8, width), F32)

            @functools.partial(loop, passes, unroll=False)
            def _(i):
                rows = block(i, step)
                d = k.own[rows, :] + k.pz[rows, :].astype(F32)
                v = k.res[rows, :]
                scale = k.sc2[rows, :]
                scaled = gain(k.gain2) * d
                k.sg[1:2, :] = k.sg[1:2, :] + jnp.sum(d * v * scale, axis=0, keepdims=True)
                d = (
                    k.cot[rows, :].astype(F32)
                    + scale * scaled
                    - v * (scale * scale * scale) * jnp.mean(scaled * v, axis=-1, keepdims=True)
                )
                k.own[rows, :] = d
                k.dmx[rows, :] = d.astype(BF)

            post(N.dmx_c, At(k.dmx)[pl.ds(0, span)], At(k.dmx)[pl.ds(span, span)], to_c)

        def mb2():
            @functools.partial(loop, width // 256)
            def _(j):
                cols = block(j, 256)
                d = dot_nt(k.dmx[:span, :], k.wout[cols, :])
                valid = mask(MASK_VALID)
                k.dc[:span, cols] = (valid * k.gc[:, cols] * d).astype(BF).astype(F32)
                c_cols = pl.ds(pl.multiple_of(width + j * 256, 256), 256)
                k.dpj[:span, c_cols] = (valid * conv_of(cols) * d).astype(BF)

            post(N.halo2, At(k.dc)[pl.ds(0, 8)], k.hr2, before, not_first)

        def mb3():
            @pl.when(s == 3)
            def _():
                k.dc[span:, :] = jnp.zeros((8, width), F32)

            @pl.when(not_last)
            def _():
                arrived(N.halo2, k.hr2)
                k.dc[span:, :] = k.hr2[...]

            @functools.partial(loop, width // 256, unroll=False)
            def _(j):
                cols = block(j, 256)
                d0 = k.dc[:span, cols]
                d = (
                    tap(0, cols) * mask(MASK_S0) * d0
                    + tap(1, cols) * mask(MASK_N1) * k.dc[1 : 1 + span, cols]
                    + tap(2, cols) * mask(MASK_N2) * k.dc[2 : 2 + span, cols]
                )
                valid = mask(MASK_VALID)
                k.dpj[:span, cols] = (valid * k.va[:, cols].astype(F32) * d).astype(BF)
                x_cols = pl.ds(pl.multiple_of(2 * width + j * 256, 256), 256)
                k.dpj[:span, x_cols] = (valid * k.gb[:, cols].astype(F32) * d).astype(BF)
                for i, m in ((0, MASK_S0), (1, MASK_S1), (2, MASK_S2)):
                    k.sg[2 + i : 3 + i, cols] = jnp.sum(
                        d0 * mask(m) * k.mix[8 - i : 8 - i + span, cols], axis=0, keepdims=True
                    )

            post(N.dpj_c, At(k.dpj)[pl.ds(0, span)], At(k.dpj)[pl.ds(span, span)], to_c)

        def mb4():
            got_win.wait()

            @functools.partial(loop, width // 256)
            def _(j):
                cols = block(j, 256)
                k.gc[:, cols] = dot_nt(k.dpj[:span, :], win[cols, :])

            @functools.partial(loop, passes, unroll=False)
            def _(i):
                rows = block(i, step)
                d = k.gc[rows, :]
                t = k.tok[rows, :].astype(F32)
                scale = k.sc1[rows, :]
                scaled = gain(k.gain1) * d
                k.sg[0:1, :] = k.sg[0:1, :] + jnp.sum(d * t * scale, axis=0, keepdims=True)
                d = (
                    k.own[rows, :]
                    + scale * scaled
                    - t * (scale * scale * scale) * jnp.mean(scaled * t, axis=-1, keepdims=True)
                )
                k.tok[rows, :] = d.astype(BF)

            put(k.tok, k.grad_tokens.at[0])
            for i in range(1, 8):
                post(N.sa(i), At(k.sg)[:, small_cols[i]], At(k.sa)[i - 1], (row_peers[i], s))
            for name, ref in (
                (N.nrm_c, k.nrm),
                (N.gat_c, k.gat),
                (N.dmx_c, k.dmx),
                (N.dpj_c, k.dpj),
            ):
                arrived(name, At(ref)[pl.ds(span, span)])

        def mg(rel_x, rel_y):
            rho = 4 * chosen(rel_y, y) + 2 * chosen(rel_x, x) + c
            rows = block(rho, slim)
            for a in range(2):
                for b in range(2):
                    sigma = 2 * chosen(b, z1) + chosen(a, z0)
                    first = dot_tn(k.nrm[:, rows], k.dpj[:, block(sigma, wide)])
                    second = dot_tn(k.gat[:, rows], k.dmx[:, block(sigma, side)])
                    for tag in MIXED:
                        u = unit_index(tag, {N.x: rel_x, N.y: rel_y, N.z0: a, N.z1: b})
                        own = travels[tag].own
                        own[u, :, :wide] = first[shares[tag]].astype(BF)
                        own[u, :, wide:] = second[shares[tag]].astype(BF)

        def finish_mixed():
            for tag in MIXED:
                got, at = travels[tag].got, travels[tag].starts[-1]
                rows = pl.ds(shares[tag].start, shares[tag].stop - shares[tag].start)
                put(At(got)[at, :, pl.ds(0, wide)], At(k.g_in)[rows, :])
                put(At(got)[at, :, pl.ds(wide, width - wide)], At(k.g_out)[rows, :])

        steps.update({N.mb(1): mb1, N.mb(2): mb2, N.mb(3): mb3, N.mb(4): mb4})
        for a in range(2):
            for b in range(2):
                steps[N.mg(a, b)] = functools.partial(mg, a, b)
        for name in ORDER[feed_end:]:
            steps[name]()
        finish_mixed()
        for name in list(pending):
            left(name)
        for cond, copy in stored:
            when(cond, lambda: copy().wait())

    pl.run_scoped(
        mixer_backward,
        pltpu.VMEM((width, 3 * width), BF),
        *[pltpu.VMEM((16, shares[tag].stop - shares[tag].start, width), BF) for tag in MIXED],
    )


def finish_kernel(n, *refs):
    sources, small = refs[:n], refs[n]
    targets, smalls = refs[n + 1 : 2 * n + 1], refs[2 * n + 1 : 2 * n + 4]
    rest = refs[2 * n + 4 :]
    held, wide, gets, puts = rest[:n], rest[n : 2 * n], rest[2 * n], rest[2 * n + 1]
    copies = [pltpu.make_async_copy(sources[i], held[i], gets.at[i]) for i in range(n)]
    for copy in copies:
        copy.start()
    s = lax.axis_index("seq")
    piece = smalls[0].shape[-1]
    value = jnp.zeros((8, piece), F32)
    for i in range(small.shape[1] // piece):
        value = jnp.where(s == i, small[:, i * piece : (i + 1) * piece], value)
    smalls[0][...] = value[0:1]
    smalls[1][...] = value[2:5]
    smalls[2][...] = value[1:2]
    out = []
    for i in range(n):
        copies[i].wait()
        ref = held[i]
        if sources[i].dtype != targets[i].dtype:
            rows = 64

            @functools.partial(loop, ref.shape[0] // rows, unroll=False)
            def _(j):
                here = block(j, rows)
                wide[i][here, :] = ref[here, :].astype(F32)

            ref = wide[i]
        copy = pltpu.make_async_copy(ref, targets[i], puts.at[i])
        copy.start()
        out.append(copy)
    for copy in out:
        copy.wait()


def fused(
    tokens,
    doc_lengths,
    valid_counts,
    norm_in,
    w_in,
    w_conv,
    w_out,
    norm_ffn,
    w_gate,
    w_up,
    w_down,
    cotangent,
):
    _, span, width = tokens.shape
    ff = w_gate.shape[1]
    rows, seq = lax.axis_size("rows"), lax.axis_size("seq")
    scratch = scratch_list(span, width, ff, rows, seq)
    anywhere = pl.BlockSpec(memory_space=pl.ANY)
    scalars = pl.BlockSpec(memory_space=pltpu.SMEM)
    vectors = pl.BlockSpec(memory_space=pltpu.VMEM)
    grads = [
        (width // rows, 3 * width // seq),
        (width // rows, width // seq),
        (width // rows, ff // seq),
        (width // rows, ff // seq),
        (ff // rows, width // seq),
    ]
    *outs, small = pl.pallas_call(
        functools.partial(layer_kernel, OPERANDS + list(scratch)),
        out_shape=[jax.ShapeDtypeStruct((1, span, width), BF)] * 2
        + [jax.ShapeDtypeStruct(shape, BF) for shape in grads]
        + [jax.ShapeDtypeStruct((8, width // rows), F32)],
        in_specs=[scalars] * 2 + [anywhere] * 2 + [vectors] * 3 + [anywhere] * 5,
        out_specs=[anywhere] * 8,
        scratch_shapes=list(scratch.values()),
        compiler_params=pltpu.CompilerParams(
            collective_id=0, has_side_effects=True, vmem_limit_bytes=67043328
        ),
        name="layer",
    )(
        doc_lengths,
        valid_counts,
        tokens,
        cotangent,
        norm_in,
        w_conv,
        norm_ffn,
        w_in,
        w_out,
        w_gate,
        w_up,
        w_down,
    )
    piece = width // (rows * seq)
    n = len(outs)
    held = [(1, span, width)] * 2 + grads
    *final, first, taps, second = pl.pallas_call(
        functools.partial(finish_kernel, n),
        out_shape=[jax.ShapeDtypeStruct((1, span, width), BF)] * 2
        + [jax.ShapeDtypeStruct(shape, F32) for shape in grads]
        + [jax.ShapeDtypeStruct((i, piece), F32) for i in (1, 3, 1)],
        in_specs=[anywhere] * n + [vectors],
        out_specs=[anywhere] * n + [vectors] * 3,
        scratch_shapes=[pltpu.VMEM(shape, BF) for shape in held]
        + [pltpu.VMEM(shape if i > 1 else (8, 128), F32) for i, shape in enumerate(held)]
        + [pltpu.SemaphoreType.DMA((n,))] * 2,
        name="finish",
    )(*outs, small)
    layer_out, grad_tokens, g_in, g_out, g_gate, g_up, g_down = final
    return (
        layer_out,
        grad_tokens,
        first[0],
        g_in,
        taps,
        g_out,
        second[0],
        g_gate,
        g_up,
        g_down,
    )


def solution(mesh):
    placed = (
        P("rows", "seq", None),
        P("rows", None),
        P("rows"),
        P(),
        P(),
        P(),
        P(),
        P(),
        P(),
        P(),
        P(),
        P("rows", "seq", None),
    )
    paired = mesh.shape["rows"] == 8 and mesh.shape["seq"] == 4
    return jax.shard_map(
        fused if paired else plain,
        mesh=mesh,
        in_specs=placed,
        out_specs=(
            P("rows", "seq", None),
            P("rows", "seq", None),
            P(("rows", "seq")),
            P("rows", "seq"),
            P(None, ("rows", "seq")),
            P("rows", "seq"),
            P(("rows", "seq")),
            P("rows", "seq"),
            P("rows", "seq"),
            P("rows", "seq"),
        ),
        check_vma=False,
    )
```
